32 devices in a mesh: dp: 4 (over z), head: 2 (over y), hid: 4 (over x, core).
Axes of the slice: x: 2, y: 2, z: 4, core: 2. Of those that a mesh axis runs over, the one named last changes fastest.
Arguments:
- inputs: bfloat16 [8, 1024, 1472], P('dp', ('head', 'hid')), may hold values from -6 to 6
- lengths: int32 [8], P('dp'), may hold values from 512 to 1024, as said below
- delete_mask: float32 [8, 1024], P('dp'), may hold values from -3 to 0
- buckets: int32 [2047], replicated, may hold values from 0 to 31
- gain_attn: float32 [1472], replicated, may hold values from 0.1 to 1.9
- w_query: bfloat16 [1472, 384], P(None, 'head'), may hold values from -0.078125 to 0.078125
- w_key: bfloat16 [1472, 384], P(None, 'head'), may hold values from -0.078125 to 0.078125
- w_value: bfloat16 [1472, 384], P(None, 'head'), may hold values from -0.15625 to 0.15625
- w_out: bfloat16 [384, 1472], P('head'), may hold values from -1.25 to 1.25
- rel_bias: float32 [32, 6], replicated, may hold values from -4 to 4
- gain_ffn: float32 [1472], replicated, may hold values from 0.1 to 1.9
- gate_weight: bfloat16 [1472, 3584], P(None, ('head', 'hid')), may hold values from -0.15625 to 0.15625
- up_weight: bfloat16 [1472, 3584], P(None, ('head', 'hid')), may hold values from -0.15625 to 0.15625
- down_weight: bfloat16 [3584, 1472], P(('head', 'hid')), may hold values from -0.125 to 0.125
- cotangent: bfloat16 [8, 1024, 1472], P('dp', ('head', 'hid')), may hold values from -6 to 6
Outputs:
- output: bfloat16 [8, 1024, 1472], P('dp', ('head', 'hid'))
- grad_inputs: float32 [8, 1024, 1472], P('dp', ('head', 'hid'))
- grad_mask: float32 [8, 1024], P('dp', ('head', 'hid'))
- grad_gain_attn: float32 [1472], replicated
- grad_w_query: float32 [1472, 384], P(None, 'head')
- grad_w_key: float32 [1472, 384], P(None, 'head')
- grad_w_value: float32 [1472, 384], P(None, 'head')
- grad_w_out: float32 [384, 1472], P('head')
- grad_rel_bias: float32 [32, 6], replicated
- grad_gain_ffn: float32 [1472], replicated
- gate_weight_gradient: float32 [1472, 3584], P(None, ('head', 'hid'))
- up_weight_gradient: float32 [1472, 3584], P(None, ('head', 'hid'))
- grad_w_down: float32 [3584, 1472], P(('head', 'hid'))
The draws below stay inside these ranges and needn't reach their ends.
Inputs may be any that keep to these rules, and one draw needn't show every extreme that they name: `lengths`: keys at or after a sequence's length are padding; the first sequence has length 1024.
All inputs are finite; a program needn't handle non-finite values.
Results may differ from the reference program's by a relative error of at most 0.017.
The reference program's roundings to bfloat16 on the way count: a program that leaves them out, or rounds other values in their place, can miss the bound.
Values may be sent and summed in bfloat16 or wider, within the bound.
No kernel may reach another device: no remote copies, remote signals or barrier semaphores. Data moves between devices by JAX's collectives and lax.ppermute only.
A program may use at most 192 MiB of HBM per device.

```python
import jax
import jax.numpy as jnp
from jax import lax

D = 1472
H = 6
DH = 64
FF = 3584
NB = 32
LEN = 1024
SEQS = 8
INNER = 384


def draw_lengths(key, part):
    drawn = jax.random.randint(key, (SEQS,), LEN // 2, LEN + 1, dtype=jnp.int32)
    return drawn.at[0].set(LEN)


def set_ends(entries, rng, smallest, top_value):
    longest = entries.shape.index(max(entries.shape))
    spots = []
    for shift in (0, 1):
        where = [jax.random.randint(jax.random.fold_in(rng, axis), (), 0, length) for axis, length in enumerate(entries.shape)]
        where[longest] = (where[longest] + shift) % entries.shape[longest]
        spots.append(tuple(where))
    return entries.at[spots[0]].set(smallest).at[spots[1]].set(top_value)


def block_scale(rng, dims, shards, low, top_value):
    gain = 1.0
    for dim, blocks in shards:
        steps = jax.random.uniform(jax.random.fold_in(jax.random.fold_in(rng, 6), dim), (blocks,), jnp.float32, low / len(shards), top_value / len(shards))
        gain = gain * jnp.repeat(jnp.exp(steps), dims[dim] // blocks).reshape((-1,) + (1,) * (len(dims) - 1 - dim))
    return gain


def gaussian(own_key, shape, deviation, bound, pieces=(), kind=jnp.bfloat16):
    array = deviation * jax.random.normal(own_key, shape, jnp.float32)
    if pieces:
        array = array * block_scale(own_key, shape, pieces, -0.22, 0.18)
    return jnp.clip(array, -bound, bound).astype(kind)


def setup_inputs(seed: int = 0) -> dict:
    streams_of = jax.random.split(jax.random.key(seed), 16)
    return {
        "inputs": gaussian(streams_of[0], (SEQS, LEN, D), 1.0, 6.0, ((0, 4), (1, 8))),
        "lengths": draw_lengths(jax.random.fold_in(streams_of[15], 71), 0),
        "delete_mask": jnp.clip(-3.0 + 3.0 * jax.random.uniform(streams_of[2], (SEQS, LEN), jnp.float32) ** block_scale(streams_of[2], (SEQS, LEN), ((0, 4),), -0.2, 0.2), -3.0, 0.0),
        "buckets": set_ends(jax.random.randint(streams_of[3], (2 * LEN - 1,), 0, NB), jax.random.fold_in(streams_of[3], 1), 0, NB - 1).astype(jnp.int32),
        "gain_attn": jnp.clip(1.0 + 0.18 * jax.random.normal(streams_of[4], (D,), jnp.float32), 0.1, 1.9),
        "w_query": gaussian(streams_of[5], (D, INNER), (4 * D) ** -0.5, 0.078125, ((1, 2),)),
        "w_key": gaussian(streams_of[6], (D, INNER), (4 * D) ** -0.5, 0.078125, ((1, 2),)),
        "w_value": gaussian(streams_of[7], (D, INNER), D ** -0.5, 0.15625, ((1, 2),)),
        "w_out": gaussian(streams_of[8], (INNER, D), (INNER // 16) ** -0.5, 1.25, ((0, 2),)),
        "rel_bias": gaussian(streams_of[9], (NB, H), 1.0, 4.0, (), jnp.float32),
        "gain_ffn": jnp.clip(1.0 + 0.18 * jax.random.normal(streams_of[10], (D,), jnp.float32), 0.1, 1.9),
        "gate_weight": gaussian(streams_of[11], (D, FF), D ** -0.5, 0.15625, ((1, 8),)),
        "up_weight": gaussian(streams_of[12], (D, FF), D ** -0.5, 0.15625, ((1, 8),)),
        "down_weight": gaussian(streams_of[13], (FF, D), (FF // 2) ** -0.5, 0.125, ((0, 8),)),
        "cotangent": gaussian(streams_of[14], (SEQS, LEN, D), 1.0, 6.0, ((0, 4), (1, 8))),
    }


epsilon = 1e-06
neg_fill = -1e+30

@jax.custom_vjp
def low(v):
    return lax.optimization_barrier(v.astype(jnp.bfloat16)).astype(jnp.float32)

@jax.custom_vjp
def low_back(v):
    return v

def low_keep(v):
    return (low(v), None)

def low_pass(kept, grad):
    return (grad,)

def back_keep(v):
    return (v, None)

def back_low(kept, grad):
    return (low(grad),)
low.defvjp(low_keep, low_pass)
low_back.defvjp(back_keep, back_low)

def rms_scale(rows_in, gain_vec):
    inverse = lax.rsqrt(lax.optimization_barrier(jnp.mean(rows_in * rows_in, axis=-1, keepdims=True)) + epsilon)
    return rows_in * inverse * gain_vec

def gated_unit(gate_in, up_in):
    return jax.nn.gelu(gate_in, approximate=True) * up_in

def forward(seq_in, mask_row, gain_attn, w_query, w_key, w_value, w_out, rel_bias, gain_ffn, gate_weight, up_weight, down_weight, seq_len, buckets):
    highest = lax.Precision.HIGHEST
    normed_one = low(rms_scale(seq_in, gain_attn))
    query_all = low_back(low(jnp.dot(normed_one, w_query, precision=highest))).reshape(LEN, H, DH)
    key_all = low_back(low(jnp.dot(normed_one, w_key, precision=highest))).reshape(LEN, H, DH)
    value_all = low_back(low(jnp.dot(normed_one, w_value, precision=highest))).reshape(LEN, H, DH)
    product = low_back(jnp.einsum('qhd,khd->hqk', query_all, key_all, precision=highest))
    position = jnp.arange(LEN, dtype=jnp.int32)
    bucket_of = buckets[position[None, :] - position[:, None] + LEN - 1]
    bias_all = jnp.transpose(rel_bias[bucket_of], (2, 0, 1))
    scores = product + bias_all + mask_row[None, None, :]
    scores = jnp.where((position < seq_len)[None, None, :], scores, neg_fill)
    weights_soft = low(jax.nn.softmax(scores, axis=-1))
    mixed_heads = low_back(low(jnp.einsum('hqk,khd->qhd', weights_soft, value_all, precision=highest))).reshape(LEN, H * DH)
    attended = low_back(jnp.dot(mixed_heads, w_out, precision=highest))
    residual = seq_in + attended
    normed_two = low(rms_scale(residual, gain_ffn))
    gate_proj = low_back(jnp.dot(normed_two, gate_weight, precision=highest))
    up_proj = low_back(jnp.dot(normed_two, up_weight, precision=highest))
    hidden_activation = low(gated_unit(gate_proj, up_proj))
    return residual + jnp.dot(hidden_activation, down_weight, precision=highest)

def reference(inputs, lengths, delete_mask, buckets, gain_attn, w_query, w_key, w_value, w_out, rel_bias, gain_ffn, gate_weight, up_weight, down_weight, cotangent):
    params = (gain_attn, w_query.astype(jnp.float32), w_key.astype(jnp.float32), w_value.astype(jnp.float32), w_out.astype(jnp.float32), rel_bias, gain_ffn, gate_weight.astype(jnp.float32), up_weight.astype(jnp.float32), down_weight.astype(jnp.float32))
    start = tuple((jnp.zeros(param.shape, jnp.float32) for param in params))

    def step_seq(totals, sequence_item):
        seq_in, mask_row, seq_len, cot_row = sequence_item

        def run_forward(seq_x, mask_x, *param_list):
            return forward(seq_x, mask_x, *param_list, seq_len, buckets)
        out_row, pullback = jax.vjp(run_forward, seq_in.astype(jnp.float32), mask_row, *params)
        gradients = pullback(cot_row.astype(jnp.float32))
        totals = tuple((total_one + grad_one for total_one, grad_one in zip(totals, gradients[2:])))
        return (totals, (out_row.astype(jnp.bfloat16), gradients[0], gradients[1]))
    totals, (outputs, grad_x, grad_mask) = lax.scan(step_seq, start, (inputs, delete_mask, lengths, cotangent))
    return (outputs, grad_x, grad_mask, totals[0], totals[1], totals[2], totals[3], totals[4], totals[5], totals[6], totals[7], totals[8], totals[9])
```

```python
import functools

import jax
import jax.numpy as jnp
from jax import lax
from jax.experimental import pallas as pl
from jax.experimental.pallas import tpu as pltpu
from jax.sharding import PartitionSpec as P

DH = 64
EPS = 1e-06
NEG = -1e30
BF = jnp.bfloat16
F32 = jnp.float32
GELU_C = 0.7978845608028654
GELU_K = 0.044715

NT = (((1,), (1,)), ((), ()))
TN = (((0,), (0,)), ((), ()))


def dot(a, b):
    return jnp.dot(a, b, preferred_element_type=F32)


def dot_nt(a, b):
    return lax.dot_general(a, b, NT, preferred_element_type=F32)


def dot_tn(a, b):
    return lax.dot_general(a, b, TN, preferred_element_type=F32)


def bias_kernel(start_ref, table_ref, mask_ref, out_ref, *, heads, block, q_blocks):
    kb = pl.program_id(0)
    qb = pl.program_id(1)
    start = pl.multiple_of(start_ref[kb * q_blocks + qb], block)
    k_at = pl.multiple_of(kb * block, block)
    mask = mask_ref[:, pl.ds(k_at, block)]
    mask = jnp.broadcast_to(mask, (block, block)).T
    for h in range(heads):
        window = table_ref[h : h + 1, pl.ds(start, 2 * block)]
        window = jnp.broadcast_to(window, (block, 2 * block))
        rolled = pltpu.roll(window, block, 1, stride=1, stride_axis=0)
        out_ref[h] = rolled[:, :block] + mask


def make_bias(starts, table, mask_row, heads, block, k_blocks, q_blocks):
    length = k_blocks * block
    return pl.pallas_call(
        functools.partial(bias_kernel, heads=heads, block=block, q_blocks=q_blocks),
        out_shape=jax.ShapeDtypeStruct((heads, length, q_blocks * block), F32),
        grid_spec=pltpu.PrefetchScalarGridSpec(
            num_scalar_prefetch=1,
            grid=(k_blocks, q_blocks),
            in_specs=[
                pl.BlockSpec(table.shape, lambda k, q, s: (0, 0)),
                pl.BlockSpec((1, length), lambda k, q, s: (0, 0)),
            ],
            out_specs=pl.BlockSpec((heads, block, block), lambda k, q, s: (0, k, q)),
        ),
        name="bias",
    )(starts, table, mask_row)


def head_mask(h, rows, width):
    lane = lax.broadcasted_iota(jnp.int32, (rows, width), 1)
    return (lane >= h * DH) & (lane < (h + 1) * DH)


def attn_fwd_kernel(q_ref, kv0_ref, kv1_ref, bias_ref, p_ref, o_ref, *, heads):
    inner = heads * DH
    q = q_ref[...]
    rows = q.shape[0]
    outs = []
    for h in range(heads):
        qm = jnp.where(head_mask(h, rows, inner), q, jnp.zeros_like(q))
        s0 = dot_nt(kv0_ref[:, :inner], qm)
        s1 = dot_nt(kv1_ref[:, :inner], qm)
        s = jnp.concatenate([s0, s1], axis=0) + bias_ref[h]
        top = jnp.max(s, axis=0, keepdims=True)
        e = jnp.exp(s - top)
        total = jnp.sum(e, axis=0, keepdims=True)
        p = e * (1.0 / total)
        p_ref[h] = p
        pb = p.astype(BF)
        half = s0.shape[0]
        o_t = dot_tn(kv0_ref[:, inner:], pb[:half]) + dot_tn(kv1_ref[:, inner:], pb[half:])
        outs.append(o_t[h * DH : (h + 1) * DH])
    o_ref[...] = jnp.concatenate(outs, axis=0).T.astype(BF)


def attn_fwd(q, kv0, kv1, bias, heads, block):
    rows, inner = q.shape
    length = bias.shape[1]
    full = lambda i: (0, 0)
    return pl.pallas_call(
        functools.partial(attn_fwd_kernel, heads=heads),
        out_shape=(
            jax.ShapeDtypeStruct((heads, length, rows), F32),
            jax.ShapeDtypeStruct((rows, inner), BF),
        ),
        grid=(rows // block,),
        in_specs=[
            pl.BlockSpec((block, inner), lambda i: (i, 0)),
            pl.BlockSpec(kv0.shape, full),
            pl.BlockSpec(kv1.shape, full),
            pl.BlockSpec((heads, length, block), lambda i: (0, 0, i)),
        ],
        out_specs=(
            pl.BlockSpec((heads, length, block), lambda i: (0, 0, i)),
            pl.BlockSpec((block, inner), lambda i: (i, 0)),
        ),
        compiler_params=pltpu.CompilerParams(vmem_limit_bytes=48 << 20),
        name="attn_fwd",
    )(q, kv0, kv1, bias)


def diagonals(piece, block):
    lanes = 128
    total = None
    for shift in range(0, lanes, 8):
        wide = None
        for part in range(block // lanes):
            rows = piece[part * lanes + shift : part * lanes + shift + 8]
            pieces = [jnp.zeros((8, block - part * lanes), F32), rows]
            if part:
                pieces.append(jnp.zeros((8, part * lanes), F32))
            rows = jnp.concatenate(pieces, axis=1)
            wide = rows if wide is None else wide + rows
        if shift:
            wide = pltpu.roll(wide, 2 * block - shift, 1)
        total = wide if total is None else total + wide
    return total


def attn_bwd_kernel(
    start_ref,
    p_ref,
    q_ref,
    do_ref,
    kv0_ref,
    kv1_ref,
    dq_ref,
    dkv0_ref,
    dkv1_ref,
    col_ref,
    table_ref,
    acc0,
    acc1,
    *,
    heads,
    block,
    q_blocks,
):
    qb = pl.program_id(0)
    inner = heads * DH
    rows = q_ref.shape[0]
    half = kv0_ref.shape[0]

    @pl.when(qb == 0)
    def _():
        acc0[...] = jnp.zeros_like(acc0)
        acc1[...] = jnp.zeros_like(acc1)
        col_ref[...] = jnp.zeros_like(col_ref)
        table_ref[...] = jnp.zeros_like(table_ref)

    q = q_ref[...]
    do = do_ref[...]
    zero = jnp.zeros_like(q)
    outs = []
    col = None
    for h in range(heads):
        pick = head_mask(h, rows, inner)
        qm = jnp.where(pick, q, zero)
        dom = jnp.where(pick, do, zero)
        dp = jnp.concatenate(
            [dot_nt(kv0_ref[:, inner:], dom), dot_nt(kv1_ref[:, inner:], dom)], axis=0
        )
        p = p_ref[h]
        inside = jnp.sum(p * dp, axis=0, keepdims=True)
        ds = p * (dp - inside)
        col = ds if col is None else col + ds
        for kb in range(2 * half // block):
            start = pl.multiple_of(start_ref[kb * q_blocks + qb], block)
            piece = ds[kb * block : (kb + 1) * block]
            table_ref[h, :, pl.ds(start, 2 * block)] += diagonals(piece, block)
        dsb = ds.astype(BF)
        pb = p.astype(BF)
        acc0[:, :inner] += dot(dsb[:half], qm)
        acc1[:, :inner] += dot(dsb[half:], qm)
        acc0[:, inner:] += dot(pb[:half], dom)
        acc1[:, inner:] += dot(pb[half:], dom)
        dq_t = dot_tn(kv0_ref[:, :inner], dsb[:half]) + dot_tn(kv1_ref[:, :inner], dsb[half:])
        outs.append(dq_t[h * DH : (h + 1) * DH])
    dq_ref[...] = jnp.concatenate(outs, axis=0).T.astype(BF)
    col_ref[...] += jnp.sum(col.T, axis=0, keepdims=True)

    @pl.when(qb == q_blocks - 1)
    def _():
        dkv0_ref[...] = acc0[...]
        dkv1_ref[...] = acc1[...].astype(BF)


def attn_bwd(starts, p, q, do, kv0, kv1, heads, block):
    rows, inner = q.shape
    length = p.shape[1]
    q_blocks = rows // block
    full = lambda i, s: (0, 0)
    row = lambda i, s: (i, 0)
    return pl.pallas_call(
        functools.partial(attn_bwd_kernel, heads=heads, block=block, q_blocks=q_blocks),
        out_shape=(
            jax.ShapeDtypeStruct((rows, inner), BF),
            jax.ShapeDtypeStruct(kv0.shape, F32),
            jax.ShapeDtypeStruct(kv1.shape, BF),
            jax.ShapeDtypeStruct((1, length), F32),
            jax.ShapeDtypeStruct((heads, 8, 2 * length), F32),
        ),
        grid_spec=pltpu.PrefetchScalarGridSpec(
            num_scalar_prefetch=1,
            grid=(q_blocks,),
            in_specs=[
                pl.BlockSpec((heads, length, block), lambda i, s: (0, 0, i)),
                pl.BlockSpec((block, inner), row),
                pl.BlockSpec((block, inner), row),
                pl.BlockSpec(kv0.shape, full),
                pl.BlockSpec(kv1.shape, full),
            ],
            out_specs=(
                pl.BlockSpec((block, inner), row),
                pl.BlockSpec(kv0.shape, full),
                pl.BlockSpec(kv1.shape, full),
                pl.BlockSpec((1, length), full),
                pl.BlockSpec((heads, 8, 2 * length), lambda i, s: (0, 0, 0)),
            ),
            scratch_shapes=[pltpu.VMEM(kv0.shape, F32), pltpu.VMEM(kv1.shape, F32)],
        ),
        compiler_params=pltpu.CompilerParams(vmem_limit_bytes=48 << 20),
        name="attn_bwd",
    )(starts, p, q, do, kv0, kv1)


def ffn_kernel(n_ref, dy_ref, g0, g1, u0, u1, d0, d1, a_ref, dg_ref, du_ref, dn_ref):
    n = n_ref[...]
    dy = dy_ref[...]
    total = None
    for part, (g_w, u_w, d_w) in enumerate(((g0, u0, d0), (g1, u1, d1))):
        gate = dot(n, g_w[...])
        up = dot(n, u_w[...])
        d_act = dot_nt(dy, d_w[...])
        square = gate * gate
        t = jnp.tanh(GELU_C * gate * (1.0 + GELU_K * square))
        half = 0.5 * (1.0 + t)
        gelu = gate * half
        slope = half + 0.5 * gate * (1.0 - t * t) * (GELU_C * (1.0 + 3.0 * GELU_K * square))
        a_ref[part] = (gelu * up).astype(BF)
        d_gate = (d_act * up * slope).astype(BF)
        d_up = (d_act * gelu).astype(BF)
        dg_ref[part] = d_gate
        du_ref[part] = d_up
        more = dot_nt(d_gate, g_w[...]) + dot_nt(d_up, u_w[...])
        total = more if total is None else total + more
    dn_ref[...] = total.astype(dn_ref.dtype)


def ffn_chunk(n, dy, weights, tile, out_dtype):
    rows, width = n.shape
    hidden = weights[0].shape[1]
    row = lambda i: (i, 0)
    full = lambda i: (0, 0)
    mid = pl.BlockSpec((2, tile, hidden), lambda i: (0, i, 0))
    mid_shape = jax.ShapeDtypeStruct((2, rows, hidden), BF)
    return pl.pallas_call(
        ffn_kernel,
        out_shape=(mid_shape, mid_shape, mid_shape, jax.ShapeDtypeStruct((rows, width), out_dtype)),
        grid=(rows // tile,),
        in_specs=[pl.BlockSpec((tile, width), row)] * 2
        + [pl.BlockSpec(w.shape, full, pipeline_mode=pl.Buffered(1)) for w in weights],
        out_specs=(mid, mid, mid, pl.BlockSpec((tile, width), row)),
        compiler_params=pltpu.CompilerParams(vmem_limit_bytes=56 << 20),
        name="ffn",
    )(n, dy, *weights)


def rms_parts(rows):
    return lax.rsqrt(jnp.mean(rows * rows, axis=-1, keepdims=True) + EPS)


def rms_back(rows, inverse, gain, grad):
    scaled = grad * gain
    inside = jnp.mean(rows * scaled, axis=-1, keepdims=True)
    return inverse * scaled - rows * (inverse * inverse * inverse * inside)


def per_device(
    inputs,
    lengths,
    delete_mask,
    buckets,
    gain_attn,
    w_query,
    w_key,
    w_value,
    w_out,
    rel_bias,
    gain_ffn,
    gate_weight,
    up_weight,
    down_weight,
    cotangent,
):
    seqs, row_count, width = inputs.shape
    heads_axis = lax.axis_size("head")
    hid_axis = lax.axis_size("hid")
    assert seqs == 2 and heads_axis == 2 and hid_axis == 4
    h_at = lax.axis_index("head")
    hid_at = lax.axis_index("hid")
    c_at = hid_at % 2
    x_at = hid_at // 2
    length = row_count * heads_axis * hid_axis
    block = 2 * row_count
    inner = w_query.shape[1]
    heads = inner // DH
    bucket_count, total_heads = rel_bias.shape

    def core_swap(v):
        return lax.ppermute(v, "hid", [(i, i ^ 1) for i in range(hid_axis)])

    def x_swap(v):
        return lax.ppermute(v, "hid", [(i, i ^ 2) for i in range(hid_axis)])

    def y_swap(v):
        return lax.ppermute(v, "head", [(0, 1), (1, 0)])

    def grid_swap(v, first):
        pairs = []
        for h in range(heads_axis):
            for i in range(hid_axis):
                along_x = (i % 2 == 0) == first
                to = (h * hid_axis + (i ^ 2)) if along_x else ((1 - h) * hid_axis + i)
                pairs.append((h * hid_axis + i, to))
        return lax.ppermute(v, ("head", "hid"), pairs)

    def pair_rows(own, other):
        return jnp.where(
            c_at == 0,
            jnp.concatenate([own, other], axis=0),
            jnp.concatenate([other, own], axis=0),
        )

    def mine(v):
        return lax.dynamic_index_in_dim(v, c_at, 0, keepdims=False)

    def others(v):
        return lax.dynamic_index_in_dim(v, 1 - c_at, 0, keepdims=False)

    x_rows = pair_rows(mine(inputs), core_swap(others(inputs))).astype(F32)
    inv_one = rms_parts(x_rows)
    normed_one = (x_rows * inv_one * gain_attn).astype(BF)
    normed_far = y_swap(normed_one)

    dy_own = pair_rows(mine(cotangent), core_swap(others(cotangent)))
    dy_a = grid_swap(dy_own, True)
    dy_b = grid_swap(jnp.concatenate([dy_own, dy_a], axis=0), False)

    gate_other = core_swap(gate_weight)
    up_other = core_swap(up_weight)
    down_other = core_swap(down_weight)
    ffn_weights = (gate_weight, gate_other, up_weight, up_other, down_weight, down_other)
    w_out_far = y_swap(w_out)

    base = jnp.stack(
        [
            (h * 2 + x) * block
            for x in (x_at, 1 - x_at)
            for h in (h_at, 1 - h_at)
        ]
    ).astype(jnp.int32)
    starts = (length - block - (base[:, None] - base[None, :2])).reshape(-1).astype(jnp.int32)
    bucket_rev = jnp.concatenate([jnp.full((1,), -1, jnp.int32), buckets[::-1]])
    hot = bucket_rev[None, :] == jnp.arange(bucket_count, dtype=jnp.int32)[:, None]
    local_bias = lax.dynamic_slice_in_dim(rel_bias, h_at * heads, heads, 1)
    table = jnp.sum(jnp.where(hot[None], local_bias.T[:, :, None], 0.0), axis=1)
    table = jnp.concatenate([table, jnp.zeros((8 - heads, 2 * length), F32)], axis=0)
    seq_mask = lax.dynamic_index_in_dim(delete_mask, c_at, 0, keepdims=False)
    seq_len = lax.dynamic_index_in_dim(lengths, c_at, 0, keepdims=False)
    seq_mask = jnp.where(jnp.arange(length, dtype=jnp.int32) < seq_len, seq_mask, NEG)

    def own_order(v):
        v = v.reshape(2, 2, block)
        v = jnp.where(h_at == 0, v, v[::-1])
        v = jnp.where(x_at == 0, v, v[:, ::-1])
        return jnp.swapaxes(v, 0, 1).reshape(1, length)

    bias = make_bias(starts, table, own_order(seq_mask), heads, block, 4, 2)

    w_qkv = jnp.concatenate([w_query, w_key, w_value], axis=1)
    qkv_own = dot(normed_one, w_qkv).astype(BF)
    qkv_far = dot(normed_far, w_qkv).astype(BF)
    qkv = jnp.concatenate([qkv_own, qkv_far], axis=0)
    queries = qkv[:, :inner]
    kv0 = qkv[:, inner:]
    kv1 = x_swap(kv0)

    probs, mixed = attn_fwd(queries, kv0, kv1, bias, heads, block)
    mixed_far = y_swap(mixed[block:])
    mixed_own = mixed[:block]
    attended = dot(mixed_own, w_out) + dot(mixed_far, w_out_far)
    residual = x_rows + attended
    inv_two = rms_parts(residual)
    normed_two = (residual * inv_two * gain_ffn).astype(BF)

    n_a = grid_swap(normed_two, True)
    n_b = grid_swap(jnp.concatenate([normed_two, n_a], axis=0), False)

    act_o, dg_o, du_o, dn_o = ffn_chunk(normed_two, dy_own, ffn_weights, block, F32)
    act_a, dg_a, du_a, dn_a = ffn_chunk(n_a, dy_a, ffn_weights, block, BF)
    act_b, dg_b, du_b, dn_b = ffn_chunk(n_b, dy_b, ffn_weights, block, BF)

    def scatter(own, part_a, part_b):
        got_a = grid_swap(part_a, True)
        got_d = grid_swap(part_b[block:], True)
        relay = (part_b[:block].astype(F32) + got_d.astype(F32)).astype(BF)
        got_b = grid_swap(relay, False)
        return own + got_a.astype(F32) + got_b.astype(F32)

    d_normed_two = scatter(dn_o, dn_a, dn_b)

    n_all = jnp.concatenate([normed_two, n_a, n_b], axis=0)
    dy_all = jnp.concatenate([dy_own, dy_a, dy_b], axis=0)
    act_all = jnp.concatenate([act_o, act_a, act_b], axis=1)
    dg_all = jnp.concatenate([dg_o, dg_a, dg_b], axis=1)
    du_all = jnp.concatenate([du_o, du_a, du_b], axis=1)

    def pair_sum(own, other):
        return (own + core_swap(other.astype(BF)).astype(F32)).astype(BF)

    grad_down = pair_sum(dot_tn(act_all[0], dy_all), dot_tn(act_all[1], dy_all))
    grad_gate = pair_sum(dot_tn(n_all, dg_all[0]), dot_tn(n_all, dg_all[1]))
    grad_up = pair_sum(dot_tn(n_all, du_all[0]), dot_tn(n_all, du_all[1]))
    grad_gate, grad_up, grad_down = [
        v.astype(F32) for v in lax.psum((grad_gate, grad_up, grad_down), "dp")
    ]

    def down(act):
        return dot(act[0], down_weight) + dot(act[1], down_other)

    ffn_out = scatter(down(act_o), down(act_a).astype(BF), down(act_b).astype(BF))
    out_rows = (residual + ffn_out).astype(BF)

    grad_gain_ffn = jnp.sum(d_normed_two * (residual * inv_two), axis=0)
    d_residual = dy_own.astype(F32) + rms_back(residual, inv_two, gain_ffn, d_normed_two)
    d_branch = d_residual.astype(BF)
    d_mixed_own = dot_nt(d_branch, w_out).astype(BF)
    d_mixed_far = y_swap(dot_nt(d_branch, w_out_far).astype(BF))
    d_mixed = jnp.concatenate([d_mixed_own, d_mixed_far], axis=0)
    grad_out_own = dot_tn(d_branch, mixed_own)
    grad_out_far = y_swap(dot_tn(d_branch, mixed_far).astype(BF))
    grad_out = grad_out_own + grad_out_far.astype(F32)

    dq, dkv0, dkv1, col, table_grad = attn_bwd(
        starts, probs, queries, d_mixed, kv0, kv1, heads, block
    )
    d_kv = (dkv0 + x_swap(dkv1).astype(F32)).astype(BF)
    d_qkv = jnp.concatenate([dq, d_kv], axis=1)

    col = col.reshape(2, 2, block)
    col = col[0] + x_swap(col[1])
    col = col[0] + y_swap(col[1])
    col = col.reshape(2, row_count)
    grad_mask_own = mine(col)
    grad_mask_far = core_swap(others(col))

    def by_seq(own, far):
        return jnp.where(c_at == 0, jnp.stack([own, far]), jnp.stack([far, own]))

    grad_mask = by_seq(grad_mask_own, grad_mask_far)

    d_normed_one = dot_nt(d_qkv, w_qkv)
    d_normed_one = d_normed_one[:block] + y_swap(d_normed_one[block:].astype(BF)).astype(F32)
    grad_gain_attn = jnp.sum(d_normed_one * (x_rows * inv_one), axis=0)
    grad_rows = d_residual + rms_back(x_rows, inv_one, gain_attn, d_normed_one)

    def to_owner(rows):
        rows = rows.reshape(2, row_count, width)
        return by_seq(mine(rows), core_swap(others(rows)))

    output = to_owner(out_rows)
    grad_inputs = to_owner(grad_rows)

    normed_both = jnp.concatenate([normed_one, normed_far], axis=0)
    grads = jnp.concatenate([dot_tn(normed_both, d_qkv), grad_out], axis=1)

    def half_sum(v, at, swap):
        v = v.reshape(2, v.shape[0] // 2, v.shape[1])
        keep = lax.dynamic_index_in_dim(v, at, 0, keepdims=False)
        give = lax.dynamic_index_in_dim(v, 1 - at, 0, keepdims=False)
        return keep + swap(give.astype(BF)).astype(F32)

    def half_join(v, at, swap):
        far = swap(v)
        return jnp.where(
            at == 0, jnp.concatenate([v, far], axis=0), jnp.concatenate([far, v], axis=0)
        )

    grads = half_sum(grads, c_at, core_swap)
    grads = half_sum(grads, x_at, x_swap)
    grads = lax.psum(grads.astype(BF), "dp")
    grads = half_join(grads, x_at, x_swap)
    grads = half_join(grads, c_at, core_swap).astype(F32)
    grad_w_query = grads[:, :inner]
    grad_w_key = grads[:, inner : 2 * inner]
    grad_w_value = grads[:, 2 * inner : 3 * inner]
    grad_w_out = grads[:, 3 * inner :].T

    table_grad = sum(jnp.roll(table_grad[:, i], -i, axis=1) for i in range(8))
    grad_rel = jnp.sum(jnp.where(hot[None], table_grad[:, None, :], 0.0), axis=2).T
    grad_rel = lax.dynamic_update_slice_in_dim(
        jnp.zeros((bucket_count, total_heads), F32), grad_rel, h_at * heads, 1
    )
    small = jnp.concatenate([grad_gain_attn, grad_gain_ffn, grad_rel.reshape(-1)])
    small = lax.psum(small, ("dp", "head", "hid"))
    grad_gain_attn = small[:width]
    grad_gain_ffn = small[width : 2 * width]
    grad_rel = small[2 * width :].reshape(bucket_count, total_heads)
    return (
        output,
        grad_inputs,
        grad_mask,
        grad_gain_attn,
        grad_w_query,
        grad_w_key,
        grad_w_value,
        grad_w_out,
        grad_rel,
        grad_gain_ffn,
        grad_gate,
        grad_up,
        grad_down,
    )


def solution(mesh):
    rows = P("dp", ("head", "hid"), None)
    return jax.shard_map(
        per_device,
        mesh=mesh,
        in_specs=(
            rows,
            P("dp"),
            P("dp", None),
            P(),
            P(),
            P(None, "head"),
            P(None, "head"),
            P(None, "head"),
            P("head", None),
            P(),
            P(),
            P(None, ("head", "hid")),
            P(None, ("head", "hid")),
            P(("head", "hid"), None),
            rows,
        ),
        out_specs=(
            rows,
            rows,
            P("dp", ("head", "hid")),
            P(),
            P(None, "head"),
            P(None, "head"),
            P(None, "head"),
            P("head", None),
            P(),
            P(),
            P(None, ("head", "hid")),
            P(None, ("head", "hid")),
            P(("head", "hid"), None),
        ),
        check_vma=False,
    )
```

```python
import functools

import jax
import jax.numpy as jnp
from jax import lax
from jax.experimental import pallas as pl
from jax.experimental.pallas import tpu as pltpu
from jax.sharding import PartitionSpec as P


DH = 64
EPS = 1e-06
NEG = -1e30
BF = jnp.bfloat16
F32 = jnp.float32
GELU_C = 0.7978845608028654
GELU_K = 0.044715
LANES = 128
EXTRA = 16


def cost(us):
    return pl.CostEstimate(flops=0, bytes_accessed=int(us * 3.0e6), transcendentals=0)


NT = (((1,), (1,)), ((), ()))
TN = (((0,), (0,)), ((), ()))


def dot(a, b):
    return jnp.dot(a, b, preferred_element_type=F32)


def dot_nt(a, b):
    return lax.dot_general(a, b, NT, preferred_element_type=F32)


def dot_tn(a, b):
    return lax.dot_general(a, b, TN, preferred_element_type=F32)


def sds(shape, dtype):
    return jax.ShapeDtypeStruct(shape, dtype)


class Order:
    last = None

    @classmethod
    def follow(cls, v):
        return v if cls.last is None else lax.optimization_barrier((v, cls.last))[0]

    @classmethod
    def done(cls, outs):
        cls.last = min(jax.tree.leaves(outs), key=lambda v: v.size)
        return outs


def call(kernel, out_shape, args, name, scalars=(), vmem=12, us=0.01, **kw):
    args = (Order.follow(args[0]), *args[1:])
    in_specs = [pl.BlockSpec(memory_space=pltpu.SMEM)] * len(scalars)
    in_specs += [pl.BlockSpec(memory_space=pltpu.VMEM)] * len(args)
    outs = pl.pallas_call(
        kernel,
        out_shape=out_shape,
        in_specs=in_specs,
        out_specs=jax.tree.map(lambda _: pl.BlockSpec(memory_space=pltpu.VMEM), out_shape),
        compiler_params=pltpu.CompilerParams(vmem_limit_bytes=vmem << 20),
        cost_estimate=cost(us),
        name=name,
        **kw,
    )(*scalars, *args)
    return Order.done(outs)


def in_hbm(v):
    return pltpu.with_memory_space_constraint(v, pltpu.HBM)


def move(v, axes, pairs, name):
    with jax.named_scope(name):
        return lax.ppermute(v, axes, pairs)


def lane_sum(v):
    total = v[:, :LANES]
    for at in range(LANES, v.shape[1], LANES):
        total = total + v[:, at : at + LANES]
    return jnp.sum(total.T, axis=0, keepdims=True)


def column(row, width):
    wide = jnp.broadcast_to(row, (LANES, row.shape[1])).T
    return jnp.concatenate([wide] * (width // LANES), axis=1)


def pair_rows(c, own_ref, far_ref):
    own = own_ref[c]
    far = far_ref[c]
    first = c == 0
    return jnp.concatenate([jnp.where(first, own, far), jnp.where(first, far, own)], axis=1)


def pick_kernel(c_ref, first_ref, second_ref, out_ref):
    out_ref[...] = jnp.where(c_ref[0] == 0, first_ref[...], second_ref[...])


def pair_kernel(c_ref, own_ref, far_ref, out_ref):
    out_ref[...] = pair_rows(c_ref[0], own_ref, far_ref)


def prep_kernel(c_ref, own_ref, far_ref, gain_ref, x_ref, n_ref, inv_ref):
    rows = pair_rows(c_ref[0], own_ref, far_ref)
    x_ref[...] = rows
    x = rows.astype(F32)
    inverse = lax.rsqrt(jnp.mean(x * x, axis=0, keepdims=True) + EPS)
    inv_ref[...] = inverse
    n_ref[...] = (x * inverse * column(gain_ref[...], x.shape[1])).astype(BF)


def qkv_kernel(n_ref, wq_ref, wk_ref, wv_ref, q_ref, kv_ref):
    n = n_ref[...]
    inner = wq_ref.shape[0]
    q_ref[...] = dot(wq_ref[...], n).astype(BF)
    kv_ref[:inner] = dot(wk_ref[...], n).astype(BF)
    kv_ref[inner:] = dot(wv_ref[...], n).astype(BF)


def bias_kernel(start_ref, table_ref, mask_ref, out_ref, *, heads, block, q_blocks):
    kb = pl.program_id(0)
    qb = pl.program_id(1)
    start = pl.multiple_of(start_ref[kb * q_blocks + qb], block)
    k_at = pl.multiple_of(kb * block, block)
    mask = column(mask_ref[:, pl.ds(k_at, block)], block)
    for h in range(heads):
        window = table_ref[h : h + 1, pl.ds(start, 2 * block)]
        window = jnp.broadcast_to(window, (block, 2 * block))
        rolled = pltpu.roll(window, block, 1, stride=1, stride_axis=0)
        out_ref[h] = rolled[:, :block] + mask


def make_bias(starts, table, mask_row, heads, block, k_blocks, q_blocks):
    length = k_blocks * block
    outs = pl.pallas_call(
        functools.partial(bias_kernel, heads=heads, block=block, q_blocks=q_blocks),
        out_shape=pltpu.HBM((heads, length, q_blocks * block), F32),
        grid_spec=pltpu.PrefetchScalarGridSpec(
            num_scalar_prefetch=1,
            grid=(k_blocks, q_blocks),
            in_specs=[
                pl.BlockSpec(table.shape, lambda k, q, s: (0, 0)),
                pl.BlockSpec((1, length), lambda k, q, s: (0, 0)),
            ],
            out_specs=pl.BlockSpec((heads, block, block), lambda k, q, s: (0, k, q)),
        ),
        compiler_params=pltpu.CompilerParams(vmem_limit_bytes=16 << 20),
        cost_estimate=cost(0.01),
        name="bias",
    )(starts, table, Order.follow(mask_row))
    return Order.done(outs)


def attn_fwd_kernel(q_ref, k0, k1, k2, k3, bias_ref, p_ref, o_ref, *, inner):
    h = pl.program_id(1)
    at_k = pl.ds(pl.multiple_of(h * DH, DH), DH)
    at_v = pl.ds(pl.multiple_of(inner + h * DH, DH), DH)
    q = q_ref[...]
    parts = [dot_tn(ref[at_k, :], q) for ref in (k0, k1, k2, k3)]
    s = jnp.concatenate(parts, axis=0) + bias_ref[0]
    top = jnp.max(s, axis=0, keepdims=True)
    e = jnp.exp(s - top)
    total = jnp.sum(e, axis=0, keepdims=True)
    p = e * (1.0 / total)
    p_ref[0] = p
    pb = p.astype(BF)
    values = jnp.concatenate([ref[at_v, :] for ref in (k0, k1, k2, k3)], axis=1)
    o_ref[...] = dot(values, pb).astype(BF)


def attn_fwd(q, kvs, bias, heads, block):
    inner, rows = q.shape
    length = bias.shape[1]
    full = lambda i, h: (0, 0)
    slab = pl.BlockSpec((1, length, block), lambda i, h: (h, 0, i))
    head = pl.BlockSpec((DH, block), lambda i, h: (h, i))
    outs = pl.pallas_call(
        functools.partial(attn_fwd_kernel, inner=inner),
        out_shape=(pltpu.HBM((heads, length, rows), F32), sds((inner, rows), BF)),
        grid=(rows // block, heads),
        in_specs=[head] + [pl.BlockSpec(kv.shape, full) for kv in kvs] + [slab],
        out_specs=(slab, head),
        compiler_params=pltpu.CompilerParams(vmem_limit_bytes=14 << 20),
        cost_estimate=cost(0.01),
        name="attn_fwd",
    )(Order.follow(q), *kvs, in_hbm(bias))
    return Order.done(outs)


def diagonals(piece, block):
    total = None
    for shift in range(0, LANES, 8):
        wide = None
        for part in range(block // LANES):
            rows = piece[part * LANES + shift : part * LANES + shift + 8]
            pieces = [jnp.zeros((8, block - part * LANES), F32), rows]
            if part:
                pieces.append(jnp.zeros((8, part * LANES), F32))
            rows = jnp.concatenate(pieces, axis=1)
            wide = rows if wide is None else wide + rows
        if shift:
            wide = pltpu.roll(wide, 2 * block - shift, 1)
        total = wide if total is None else total + wide
    return total


def attn_bwd_kernel(
    start_ref, p_ref, q_ref, do_ref, k0, k1, k2, k3, dq_ref, own_ref, give_ref, col_ref, table_ref,
    acc, col_acc, *, inner, heads, block, q_blocks,
):
    qb = pl.program_id(0)
    h = pl.program_id(1)
    kvs = (k0, k1, k2, k3)
    at_k = pl.ds(pl.multiple_of(h * DH, DH), DH)
    at_v = pl.ds(pl.multiple_of(inner + h * DH, DH), DH)
    half = len(kvs) * block // 2

    @pl.when((qb == 0) & (h == 0))
    def _():
        acc[...] = jnp.zeros_like(acc)
        col_acc[...] = jnp.zeros_like(col_acc)
        table_ref[...] = jnp.zeros_like(table_ref)

    q = q_ref[...]
    do = do_ref[...]
    dp = jnp.concatenate([dot_tn(ref[at_v, :], do) for ref in kvs], axis=0)
    p = p_ref[0]
    inside = jnp.sum(p * dp, axis=0, keepdims=True)
    ds = p * (dp - inside)
    col_acc[...] += ds
    for kb in range(len(kvs)):
        start = pl.multiple_of(start_ref[kb * q_blocks + qb], block)
        piece = ds[kb * block : (kb + 1) * block]
        table_ref[h, :, pl.ds(start, 2 * block)] += diagonals(piece, block)
    dsb = ds.astype(BF)
    pb = p.astype(BF)
    acc[at_k, :] += dot_nt(q, dsb)
    acc[at_v, :] += dot_nt(do, pb)
    keys = jnp.concatenate([ref[at_k, :] for ref in kvs], axis=1)
    dq_ref[...] = dot(keys, dsb).astype(BF)

    @pl.when((qb == q_blocks - 1) & (h == heads - 1))
    def _():
        own_ref[...] = acc[:, :half]
        col = lane_sum(col_acc[...])
        col_ref[...] = col[:, :half]
        give_ref[: 2 * inner] = acc[:, half:].astype(BF)
        give_ref[2 * inner :] = split_rows(col[:, half:])


def split(v):
    high = v.astype(BF)
    return high, (v - high.astype(F32)).astype(BF)


def merge(high, low):
    return high.astype(F32) + low.astype(F32)


def split_rows(row):
    high = row.astype(BF)
    low = (row - high.astype(F32)).astype(BF)
    at = lax.broadcasted_iota(jnp.int32, (EXTRA, row.shape[1]), 0)
    wide = jnp.where(at == 0, high.astype(F32), jnp.where(at == 1, low.astype(F32), 0.0))
    return wide.astype(BF)


def attn_bwd(starts, p, q, do, kvs, heads, block):
    inner, rows = q.shape
    length = p.shape[1]
    half = length // 2
    q_blocks = rows // block
    full = lambda i, h, s: (0, 0)
    head = pl.BlockSpec((DH, block), lambda i, h, s: (h, i))
    outs = pl.pallas_call(
        functools.partial(
            attn_bwd_kernel, inner=inner, heads=heads, block=block, q_blocks=q_blocks
        ),
        out_shape=(
            sds((inner, rows), BF),
            sds((2 * inner, half), F32),
            sds((2 * inner + EXTRA, half), BF),
            sds((1, half), F32),
            sds((heads, 8, 2 * length), F32),
        ),
        grid_spec=pltpu.PrefetchScalarGridSpec(
            num_scalar_prefetch=1,
            grid=(q_blocks, heads),
            in_specs=[pl.BlockSpec((1, length, block), lambda i, h, s: (h, 0, i)), head, head]
            + [pl.BlockSpec(kv.shape, full) for kv in kvs],
            out_specs=(
                head,
                pl.BlockSpec((2 * inner, half), full),
                pl.BlockSpec((2 * inner + EXTRA, half), full),
                pl.BlockSpec((1, half), full),
                pl.BlockSpec((heads, 8, 2 * length), lambda i, h, s: (0, 0, 0)),
            ),
            scratch_shapes=[
                pltpu.VMEM((2 * inner, length), F32),
                pltpu.VMEM((length, block), F32),
            ],
        ),
        compiler_params=pltpu.CompilerParams(vmem_limit_bytes=28 << 20),
        cost_estimate=cost(500),
        name="attn_bwd",
    )(starts, in_hbm(p), Order.follow(q), do, *kvs)
    return Order.done(outs)


def halves(c_ref, half):
    return [pl.ds(pl.multiple_of(at * half, half), half) for at in (c_ref[0], 1 - c_ref[0])]


def mid_kernel(
    c_ref, x_ref, m0_ref, m1_ref, w0_ref, w1_ref, w2_ref, gain_ref, res_ref, n_ref, inv_ref
):
    attended = dot_tn(w0_ref[...], m0_ref[...])
    for at, w_ref in zip(halves(c_ref, w1_ref.shape[0]), (w1_ref, w2_ref)):
        attended = attended + dot_tn(w_ref[...], m1_ref[at, :])
    res = x_ref[...].astype(F32) + attended
    res_ref[...] = res
    inverse = lax.rsqrt(jnp.mean(res * res, axis=0, keepdims=True) + EPS)
    inv_ref[...] = inverse
    n_ref[...] = (res * inverse * column(gain_ref[...], res.shape[1])).astype(BF)


def rms_back(rows, inverse, gain, grad):
    scaled = grad * gain
    inside = jnp.mean(rows * scaled, axis=0, keepdims=True)
    return inverse * scaled - rows * (inverse * inverse * inverse * inside)


def mid_back_kernel(
    c_ref, own_ref, ga_ref, gb_ref, gd_ref, dy_ref, res_ref, inv_ref, gain_ref, w0_ref, w1_ref, w2_ref,
    dres_ref, branch_ref, gain_grad_ref, dm0_ref, dm1_ref,
):
    grad = own_ref[...] + ga_ref[...].astype(F32) + gb_ref[...].astype(F32)
    grad = grad + gd_ref[...].astype(F32)
    res = res_ref[...]
    inverse = inv_ref[...]
    gain_grad_ref[...] = lane_sum(grad * (res * inverse))
    gain = column(gain_ref[...], res.shape[1])
    d_res = dy_ref[...].astype(F32) + rms_back(res, inverse, gain, grad)
    dres_ref[...] = d_res
    branch = d_res.astype(BF)
    branch_ref[...] = branch
    dm0_ref[...] = dot(w0_ref[...], branch).astype(BF)
    for at, w_ref in zip(halves(c_ref, w1_ref.shape[0]), (w1_ref, w2_ref)):
        dm1_ref[at, :] = dot(w_ref[...], branch).astype(BF)


def out_grad_kernel(m0_ref, m1_ref, branch_ref, own_ref, far_ref):
    branch = branch_ref[...]
    own_ref[...] = dot_nt(m0_ref[...], branch)
    far_ref[...] = dot_nt(m1_ref[...], branch).astype(BF)


def ffn_kernel(n_ref, dy_ref, g0, g1, u0, u1, d0, d1, a_ref, dg_ref, du_ref, dn_ref):
    n = n_ref[...]
    dy = dy_ref[...]
    total = None
    for part, (g_w, u_w, d_w) in enumerate(((g0, u0, d0), (g1, u1, d1))):
        gate = dot(g_w[...], n)
        up = dot(u_w[...], n)
        d_act = dot(d_w[...], dy)
        square = gate * gate
        t = jnp.tanh(gate * (GELU_C + (GELU_C * GELU_K) * square))
        half = 0.5 + 0.5 * t
        gelu = gate * half
        slope = half + gelu * (1.0 - t) * (GELU_C + (3.0 * GELU_C * GELU_K) * square)
        a_ref[part] = (gelu * up).astype(BF)
        d_gate = (d_act * up * slope).astype(BF)
        d_up = (d_act * gelu).astype(BF)
        dg_ref[part] = d_gate
        du_ref[part] = d_up
        more = dot_tn(g_w[...], d_gate) + dot_tn(u_w[...], d_up)
        total = more if total is None else total + more
    dn_ref[...] = total.astype(dn_ref.dtype)


def ffn_chunk(n, dy, weights, out_dtype):
    width, rows = n.shape
    hidden = weights[0].shape[0]
    mid = sds((2, hidden, rows), BF)
    return call(
        ffn_kernel,
        (mid, mid, mid, sds((width, rows), out_dtype)),
        (n, dy, *weights),
        "ffn",
        vmem=16,
    )


def ffn_out_kernel(a_ref, d0, d1, o_ref):
    total = dot_tn(d0[...], a_ref[0]) + dot_tn(d1[...], a_ref[1])
    o_ref[...] = total.astype(o_ref.dtype)


def ffn_out(act, d0, d1, dtype):
    _, hidden, rows = act.shape
    width = d0.shape[1]
    return call(
        ffn_out_kernel, sds((width, rows), dtype), (act, d0, d1), "ffn_out",
    )


def wgrad_sum_kernel(*refs):
    out_ref = refs[-1]
    n, pieces, rows, _ = out_ref.shape
    got = refs[-2]
    for at in range(pieces):
        mids, blocks = refs[8 * at : 8 * at + 4], refs[8 * at + 4 : 8 * at + 8]
        total = None
        for mid, block in zip(mids, blocks):
            more = dot_nt(mid[0], block[...])
            total = more if total is None else total + more
        total = (total + got[at].astype(F32)).astype(BF)
        for q in range(n):
            out_ref[q, at] = total[q * rows : (q + 1) * rows]


def wgrad_stack_kernel(part, *refs):
    out_ref = refs[-1]
    for at in range(out_ref.shape[0]):
        mids, rows = refs[8 * at : 8 * at + 4], refs[8 * at + 4 : 8 * at + 8]
        total = None
        for mid, row in zip(mids, rows):
            more = dot_nt(mid[part], row[...])
            total = more if total is None else total + more
        out_ref[at] = total.astype(BF)


def wgrad_give(pieces):
    mids, rows = pieces[0]
    shape = (len(pieces), mids[0].shape[1], rows[0].shape[0])
    args = [v for mids, rows in pieces for v in (*mids, *rows)]
    return call(
        functools.partial(wgrad_stack_kernel, 1), sds(shape, BF), args, "wgrad_give",
        vmem=20,
    )


def wgrad_sum(pieces, got, shares):
    mids, rows = pieces[0]
    shape = (shares, len(pieces), mids[0].shape[1] // shares, rows[0].shape[0])
    args = [v for mids, rows in pieces for v in (*mids, *rows)]
    return call(
        wgrad_sum_kernel, sds(shape, BF), (*args, got), "wgrad_sum", vmem=20,
    )


def q_back_kernel(dq_ref, n0_ref, n1_ref, w_ref, gw_ref, own_ref, far_ref):
    block = n0_ref.shape[1]
    dq0 = dq_ref[:, :block]
    dq1 = dq_ref[:, block:]
    gw_ref[...] = (dot_nt(dq0, n0_ref[...]) + dot_nt(dq1, n1_ref[...])).astype(gw_ref.dtype)
    own_ref[...] = dot_tn(w_ref[...], dq0)
    far_ref[...] = dot_tn(w_ref[...], dq1)


def kv_sum_kernel(
    own_ref, got_ref, col_ref, back_own_ref, back_far_ref, n0_ref, n1_ref, wk_ref, wv_ref,
    gain_ref, gain_ffn_ref, rel_ref, dkv_ref, total_ref, give_ref, small_ref,
):
    inner = wk_ref.shape[0]
    width, block = back_far_ref.shape
    d_kv = (own_ref[...] + got_ref[: 2 * inner].astype(F32)).astype(BF)
    dkv_ref[...] = d_kv
    col = col_ref[...] + merge(got_ref[2 * inner : 2 * inner + 1], got_ref[2 * inner + 1 : 2 * inner + 2])
    far = back_far_ref[...] + dot_tn(wk_ref[...], d_kv[:inner, block:])
    far = far + dot_tn(wv_ref[...], d_kv[inner:, block:])
    give_ref[:width] = far.astype(BF)
    own = back_own_ref[...] + dot_tn(wk_ref[...], d_kv[:inner, :block])
    own = own + dot_tn(wv_ref[...], d_kv[inner:, :block])
    total_ref[...] = own
    gain = lane_sum(own * n0_ref[...].astype(F32) + far * n1_ref[...].astype(F32)) / gain_ref[...]
    small_ref[...] = jnp.zeros_like(small_ref)
    for first, row in ((2, gain), (8, gain_ffn_ref[...])):
        for at in range(0, width, block):
            size = min(block, width - at)
            line = first + at // block
            small_ref[line : line + 1, :size] = row[:, at : at + size]
    small_ref[1:2, : rel_ref.shape[1]] = rel_ref[...]
    small_ref[0:1] = col[:, block:]
    high, low = split(small_ref[...])
    give_ref[width : width + EXTRA] = high
    give_ref[width + EXTRA :] = low
    small_ref[...] = merge(high, low)
    small_ref[0:1] = col[:, :block]


def kv_back_kernel(dkv_ref, n0_ref, n1_ref, gk_ref, gv_ref):
    inner = gk_ref.shape[0]
    block = n0_ref.shape[1]
    for at, out in ((0, gk_ref), (inner, gv_ref)):
        d0 = dkv_ref[at : at + inner, :block]
        d1 = dkv_ref[at : at + inner, block:]
        out[...] = dot_nt(d0, n0_ref[...]) + dot_nt(d1, n1_ref[...])


def last_kernel(
    c_ref, own_ref, got_ref, small_ref, x_ref, inv_ref, gain_ref, dres_ref,
    keep_ref, give_ref, keep_small_ref, rows_ref,
):
    width = x_ref.shape[0]
    grad = own_ref[...] + got_ref[:width].astype(F32)
    small = small_ref[...] + merge(got_ref[width : width + EXTRA], got_ref[width + EXTRA :])
    x = x_ref[...].astype(F32)
    gain = column(gain_ref[...], x.shape[1])
    rows_ref[:width] = dres_ref[...] + rms_back(x, inv_ref[...], gain, grad)
    rows_ref[width:] = small
    rows = keep_ref.shape[1]
    mine = pl.ds(pl.multiple_of(c_ref[0] * rows, rows), rows)
    theirs = pl.ds(pl.multiple_of((1 - c_ref[0]) * rows, rows), rows)
    keep_ref[...] = rows_ref[:width, mine]
    give_ref[:width] = rows_ref[:width, theirs]
    keep_small_ref[:EXTRA] = small[:, :rows]
    keep_small_ref[EXTRA:] = small[:, rows:]
    give_ref[width:] = keep_small_ref[...]
    give_ref[width : width + 1] = rows_ref[width : width + 1, theirs]
    keep_small_ref[0:1] = rows_ref[width : width + 1, mine]


def out_rows_kernel(c_ref, res_ref, own_ref, ga_ref, gb_ref, gd_ref, keep_ref, give_ref, rows_ref):
    total = res_ref[...] + (
        own_ref[...]
        + ga_ref[...].astype(F32)
        + gb_ref[...].astype(F32)
        + gd_ref[...].astype(F32)
    )
    rows_ref[...] = total.astype(BF)
    rows = keep_ref.shape[1]
    keep_ref[...] = rows_ref[:, pl.ds(pl.multiple_of(c_ref[0] * rows, rows), rows)]
    give_ref[...] = rows_ref[:, pl.ds(pl.multiple_of((1 - c_ref[0]) * rows, rows), rows)]


def fold_core_kernel(c_ref, gq_ref, gk_ref, gv_ref, go_ref, got_ref, keep_ref, give_ref):
    out = go_ref[...] + got_ref[...].astype(F32)
    first = c_ref[0] == 0
    keep_ref[0] = jnp.where(first, gq_ref[...], gv_ref[...])
    keep_ref[1] = jnp.where(first, gk_ref[...], out)
    give_ref[0] = jnp.where(first, gv_ref[...], gq_ref[...]).astype(BF)
    give_ref[1] = jnp.where(first, out, gk_ref[...]).astype(BF)


def fold_x_kernel(x_ref, mine_ref, got_ref, keep_ref, give_ref):
    total = mine_ref[...] + got_ref[...].astype(F32)
    first = x_ref[0] == 0
    keep_ref[...] = jnp.where(first, total[0], total[1])
    give_ref[...] = jnp.where(first, total[1], total[0]).astype(BF)


def share_kernel(z_ref, mine_ref, got_ref, sum_ref, own_ref, *give_refs):
    sum_ref[...] = mine_ref[...] + got_ref[...].astype(F32)
    rows = own_ref.shape[0]
    n = len(give_refs) + 1
    for k, out in enumerate((own_ref, *give_refs)):
        at = lax.rem(z_ref[0] + k, n)
        out[...] = sum_ref[pl.ds(pl.multiple_of(at * rows, rows), rows), :].astype(out.dtype)


def lines(small, first, width):
    half = small.shape[0] // 2
    pieces = []
    for at in range(-(-width // (2 * LANES))):
        line = first + at
        pieces += [small[line : line + 1], small[half + line : half + line + 1]]
    return jnp.concatenate(pieces, axis=1)[:, :width]


def share_sum_kernel(own_ref, small_ref, small_got_ref, *refs):
    out_ref = refs[-1]
    rows, width = own_ref.shape
    total = own_ref[...]
    for ref in refs[:-1]:
        total = total + ref[...].astype(F32)
    out_ref[:rows] = total.astype(BF)
    small = small_ref[...] + small_got_ref[...]
    rel = small[1:2]
    rel = jnp.concatenate([rel, small[EXTRA + 1 : EXTRA + 2]], axis=1)
    rel = jnp.concatenate([rel, jnp.zeros((1, width - rel.shape[1]), F32)], axis=1)
    three = jnp.concatenate(
        [lines(small, 2, width), lines(small, 8, width), rel, jnp.zeros((5, width), F32)], axis=0
    )
    out_ref[rows:] = jnp.concatenate(split(three), axis=0)


def share_join_kernel(z_ref, *refs):
    shares, (out_ref, hold_ref) = refs[:-2], refs[-2:]
    n = len(shares)
    rows = shares[0].shape[0] - EXTRA
    for k, ref in enumerate(shares):
        at = lax.rem(z_ref[0] + n - k, n)
        out_ref[pl.ds(pl.multiple_of(at * rows, rows), rows), :] = ref[:rows]
        hold_ref[at] = merge(ref[rows : rows + 8], ref[rows + 8 :])
    total = hold_ref[0]
    for k in range(1, n):
        total = total + hold_ref[k]
    out_ref[n * rows :] = jnp.concatenate(split(total), axis=0)


def join_x_kernel(x_ref, own_ref, got_ref, out_ref, small_ref):
    inner = out_ref.shape[1]
    first = x_ref[0] == 0
    own = own_ref[:inner]
    got = got_ref[:inner]
    out_ref[0] = jnp.where(first, own, got)
    out_ref[1] = jnp.where(first, got, own)
    small_ref[...] = merge(own_ref[inner : inner + 8], own_ref[inner + 8 :]) + merge(
        got_ref[inner : inner + 8], got_ref[inner + 8 :]
    )


def join_core_kernel(c_ref, own_ref, got_ref, *outs):
    first = c_ref[0] == 0
    own = own_ref[...]
    got = got_ref[...]
    pair = (jnp.where(first, own, got), jnp.where(first, got, own))
    for at, out in enumerate(outs):
        out[...] = pair[at // 2][at % 2].astype(F32)


def place_kernel(c_ref, own_ref, got_ref, out_ref):
    out_ref[c_ref[0]] = own_ref[...]
    out_ref[1 - c_ref[0]] = got_ref[: own_ref.shape[0]]


def widen_kernel(src, *outs):
    for at, out in enumerate(outs):
        out[...] = src[0, at].astype(F32)


def widen(v):
    n, pieces, rows, width = v.shape
    outs = pl.pallas_call(
        widen_kernel,
        out_shape=[sds((n * rows, width), F32)] * pieces,
        grid=(n,),
        in_specs=[pl.BlockSpec((1, pieces, rows, width), lambda i: (i, 0, 0, 0))],
        out_specs=[pl.BlockSpec((rows, width), lambda i: (i, 0))] * pieces,
        compiler_params=pltpu.CompilerParams(vmem_limit_bytes=32 << 20),
        cost_estimate=cost(500),
        name="widen",
    )(Order.follow(v))
    return Order.done(outs)


def per_device(*args):
    Order.last = None
    return run(*args)


def run(
    inputs,
    lengths,
    delete_mask,
    buckets,
    gain_attn,
    w_query,
    w_key,
    w_value,
    w_out,
    rel_bias,
    gain_ffn,
    gate_weight,
    up_weight,
    down_weight,
    cotangent,
):
    seqs, row_count, width = inputs.shape
    dp_axis = lax.axis_size("dp")
    heads_axis = lax.axis_size("head")
    hid_axis = lax.axis_size("hid")
    assert seqs == 2 and heads_axis == 2 and hid_axis == 4
    z_at = lax.axis_index("dp")
    h_at = lax.axis_index("head")
    hid_at = lax.axis_index("hid")
    c_at = hid_at % 2
    x_at = hid_at // 2
    length = row_count * heads_axis * hid_axis
    block = 2 * row_count
    inner = w_query.shape[1]
    heads = inner // DH
    hidden = gate_weight.shape[1]
    bucket_count, total_heads = rel_bias.shape
    c_scalar = c_at.astype(jnp.int32).reshape(1)
    x_scalar = x_at.astype(jnp.int32).reshape(1)
    z_scalar = z_at.astype(jnp.int32).reshape(1)

    def core_swap(v, name):
        return move(v, "hid", [(i, i ^ 1) for i in range(hid_axis)], name)

    def x_swap(v, name):
        return move(v, "hid", [(i, i ^ 2) for i in range(hid_axis)], name)

    def y_swap(v, name):
        return move(v, "head", [(0, 1), (1, 0)], name)

    def grid_swap(v, relayed, name):
        pairs = []
        for h in range(heads_axis):
            for i in range(hid_axis):
                along_x = not relayed or i % 2 == 1
                along_y = not relayed or i % 2 == 0
                to = ((1 - h) if along_y else h) * hid_axis + ((i ^ 2) if along_x else i)
                pairs.append((h * hid_axis + i, to))
        return move(v, ("head", "hid"), pairs, name)

    def relay(from_x, from_y, name):
        picked = call(
            pick_kernel, sds(from_x.shape, BF), (from_x, from_y), "pick", scalars=(c_scalar,),
        )
        return grid_swap(picked, True, name)

    def stack(a, b):
        return jnp.concatenate([a, b], axis=0)

    def place(own, got):
        shape = sds((2, *own.shape), own.dtype)
        return call(place_kernel, shape, (own, got), "place", scalars=(c_scalar,), us=100)

    def after(v, *earlier):
        return lax.optimization_barrier((v, *earlier))[0]

    x_in = jnp.swapaxes(inputs, 1, 2)
    dy_in = jnp.swapaxes(cotangent, 1, 2)
    wq, wk, wv = w_query.T, w_key.T, w_value.T
    gate_w, up_w = gate_weight.T, up_weight.T
    gain_one = gain_attn.reshape(1, width)
    gain_two = gain_ffn.reshape(1, width)

    w_half = w_out.reshape(2, inner // 2, width)
    w_half = lax.dynamic_index_in_dim(w_half, c_at, 0, keepdims=False)
    x_rows, normed_one, inv_one = call(
        prep_kernel,
        (sds((width, block), BF), sds((width, block), BF), sds((1, block), F32)),
        (x_in, core_swap(x_in, "x_core"), gain_one),
        "prep",
        scalars=(c_scalar,),
    )
    normed_far_raw = y_swap(normed_one, "n1_y")

    dy_own = call(
        pair_kernel,
        sds((width, block), BF),
        (dy_in, core_swap(dy_in, "dy_core")),
        "pair",
        scalars=(c_scalar,),
    )

    gate_other = core_swap(gate_w, "gate_core")
    up_other = core_swap(up_w, "up_core")
    down_other = core_swap(down_weight, "down_core")
    ffn_weights = (gate_w, gate_other, up_w, up_other, down_weight, down_other)
    def project(n):
        return call(
            qkv_kernel,
            (sds((inner, block), BF), sds((2 * inner, block), BF)),
            (n, wq, wk, wv),
            "qkv",
        )

    q_own, kv_own = project(normed_one)
    base = jnp.stack(
        [(h * 2 + x) * block for x in (x_at, 1 - x_at) for h in (h_at, 1 - h_at)]
    ).astype(jnp.int32)
    starts = (length - block - (base[:, None] - base[None, :2])).reshape(-1).astype(jnp.int32)
    bucket_rev = jnp.concatenate([jnp.full((1,), -1, jnp.int32), buckets[::-1]])
    hot = bucket_rev[None, :] == jnp.arange(bucket_count, dtype=jnp.int32)[:, None]
    local_bias = lax.dynamic_slice_in_dim(rel_bias, h_at * heads, heads, 1)
    table = jnp.sum(jnp.where(hot[None], local_bias.T[:, :, None], 0.0), axis=1)
    table = jnp.concatenate([table, jnp.zeros((8 - heads, 2 * length), F32)], axis=0)
    seq_mask = lax.dynamic_index_in_dim(delete_mask, c_at, 0, keepdims=False)
    seq_len = lax.dynamic_index_in_dim(lengths, c_at, 0, keepdims=False)
    seq_mask = jnp.where(jnp.arange(length, dtype=jnp.int32) < seq_len, seq_mask, NEG)
    seq_mask = seq_mask.reshape(2, 2, block)
    seq_mask = jnp.where(h_at == 0, seq_mask, seq_mask[::-1])
    seq_mask = jnp.where(x_at == 0, seq_mask, seq_mask[:, ::-1])
    seq_mask = jnp.swapaxes(seq_mask, 0, 1).reshape(1, length)
    seq_mask = after(seq_mask, gate_other, up_other)
    bias = make_bias(starts, table, seq_mask, heads, block, 4, 2)

    kv_own_x = x_swap(kv_own, "kv_own_x")
    normed_far_raw = after(normed_far_raw, bias, kv_own)
    normed_far = after(normed_far_raw, down_other, kv_own_x)
    w_half = y_swap(after(w_half, normed_far_raw), "wout_y")
    dy_y = y_swap(after(dy_own, w_half), "dy_y")
    w_half_got = core_swap(w_half, "wout_core")
    q_far, kv_far = project(normed_far)
    kv_far_x = x_swap(kv_far, "kv_far_x")
    dy_x = x_swap(after(dy_own, kv_far_x), "dy_x")
    queries = jnp.concatenate([q_own, q_far], axis=1)
    kvs = (kv_own, kv_far, kv_own_x, kv_far_x)

    probs, mixed = attn_fwd(queries, kvs, bias, heads, block)
    mixed_far = y_swap(mixed[:, block:], "mixed_y")
    dy_d = relay(dy_x, dy_y, "dy_d")
    mixed_own = mixed[:, :block]
    residual, normed_two, inv_two = call(
        mid_kernel,
        (sds((width, block), F32), sds((width, block), BF), sds((1, block), F32)),
        (x_rows, mixed_own, mixed_far, w_out, w_half, w_half_got, gain_two),
        "mid",
        scalars=(c_scalar,),
    )

    n_x = x_swap(normed_two, "n2_x")
    n_y = y_swap(normed_two, "n2_y")
    act_o, dg_o, du_o, dn_o = ffn_chunk(normed_two, dy_own, ffn_weights, F32)
    n_d = relay(n_x, n_y, "n2_d")
    act_x, dg_x, du_x, dn_x = ffn_chunk(n_x, dy_x, ffn_weights, BF)
    got_x = x_swap(dn_x, "dn_x")
    act_y, dg_y, du_y, dn_y = ffn_chunk(n_y, dy_y, ffn_weights, BF)
    got_y = y_swap(dn_y, "dn_y")
    act_d, dg_d, du_d, dn_d = ffn_chunk(n_d, dy_d, ffn_weights, BF)
    got_d = grid_swap(dn_d, False, "dn_d")

    n_all = (normed_two, n_x, n_y, n_d)
    dy_all = (dy_own, dy_x, dy_y, dy_d)
    pieces = (
        ((act_o, act_x, act_y, act_d), dy_all),
        ((dg_o, dg_x, dg_y, dg_d), n_all),
        ((du_o, du_x, du_y, du_d), n_all),
    )
    out_o = ffn_out(act_o, down_weight, down_other, F32)
    mids, rows = pieces[0]
    pieces = (((after(mids[0], got_x, got_y), *mids[1:]), rows), *pieces[1:])
    given = core_swap(wgrad_give(pieces), "wgrad_core")
    part_x = ffn_out(act_x, down_weight, down_other, BF)
    part_y = ffn_out(act_y, down_weight, down_other, BF)
    part_d = ffn_out(act_d, down_weight, down_other, BF)
    shares = dp_axis if dp_axis <= 8 else 1
    ffn_grads = wgrad_sum(pieces, given, shares)
    if shares > 1:
        ffn_grads = lax.psum_scatter(ffn_grads, "dp", scatter_dimension=0, tiled=True)
    else:
        ffn_grads = lax.psum(ffn_grads, "dp")


    d_residual, d_branch, gain_ffn_part, d_mixed_own, d_mixed_give = call(
        mid_back_kernel,
        (
            sds((width, block), F32),
            sds((width, block), BF),
            sds((1, width), F32),
            sds((inner, block), BF),
            sds((inner, block), BF),
        ),
        (dn_o, got_x, got_y, got_d, dy_own, residual, inv_two, gain_two, w_out, w_half, w_half_got),
        "mid_back",
        scalars=(c_scalar,),
    )
    d_mixed = jnp.concatenate([d_mixed_own, y_swap(d_mixed_give, "dmixed_y")], axis=1)

    grad_out_own, grad_out_give = call(
        out_grad_kernel,
        (sds((inner, width), F32), sds((inner, width), BF)),
        (mixed_own, mixed_far, d_branch),
        "out_grad",
    )
    grad_out_got = y_swap(grad_out_give, "gout_y")

    dq, dkv_own, dkv_give, col, table_grad = attn_bwd(
        starts, probs, queries, d_mixed, kvs, heads, block
    )
    dkv_got = x_swap(dkv_give, "dkv_x")
    out_x = x_swap(after(part_x, got_d), "out_x")
    out_y = y_swap(after(part_y, got_d), "out_y")
    dq = after(dq, out_x, out_y)
    dkv_got = after(dkv_got, grad_out_got)
    grad_q, back_own, back_far = call(
        q_back_kernel,
        (sds((inner, width), F32), sds((width, block), F32), sds((width, block), F32)),
        (dq, normed_one, normed_far, wq),
        "q_back",
    )
    table_grad = sum(jnp.roll(table_grad[:, i], -i, axis=1) for i in range(8))
    grad_rel = jnp.sum(jnp.where(hot[None], table_grad[:, None, :], 0.0), axis=2).T
    grad_rel = lax.dynamic_update_slice_in_dim(
        jnp.zeros((bucket_count, total_heads), F32), grad_rel, h_at * heads, 1
    )
    d_kv, back_own, back_give, small = call(
        kv_sum_kernel,
        (
            sds((2 * inner, 2 * block), BF),
            sds((width, block), F32),
            sds((width + 2 * EXTRA, block), BF),
            sds((EXTRA, block), F32),
        ),
        (
            dkv_own, dkv_got, col, back_own, back_far, normed_one, normed_far, wk, wv,
            gain_one, gain_ffn_part, grad_rel.reshape(1, -1),
        ),
        "kv_sum",
    )
    back_got = y_swap(back_give, "back_y")
    grad_k, grad_v = call(
        kv_back_kernel,
        (sds((inner, width), F32), sds((inner, width), F32)),
        (d_kv, normed_one, normed_far),
        "kv_back",
    )

    pair_f32, pair_bf = sds((2, inner, width), F32), sds((2, inner, width), BF)
    one_f32, one_bf = sds((inner, width), F32), sds((inner, width), BF)
    keep, give = call(
        fold_core_kernel,
        (pair_f32, pair_bf),
        (grad_q, grad_k, grad_v, grad_out_own, grad_out_got),
        "fold_core",
        scalars=(c_scalar,),
    )
    keep, give = call(
        fold_x_kernel,
        (one_f32, one_bf),
        (keep, core_swap(give, "fold_core")),
        "fold_x",
        scalars=(x_scalar,),
    )
    got = x_swap(give, "fold_x")
    rows_keep, rows_give, small, _ = call(
        last_kernel,
        (
            sds((width, row_count), F32),
            sds((width + 2 * EXTRA, row_count), F32),
            sds((2 * EXTRA, row_count), F32),
            sds((width + EXTRA, block), F32),
        ),
        (back_own, after(back_got, got), small, x_rows, inv_one, gain_one, d_residual),
        "last",
        scalars=(c_scalar,),
    )
    rows_got = core_swap(rows_give, "grad_core")
    if shares > 1:
        ffn_grads = lax.all_gather(after(ffn_grads, grad_k), "dp", axis=0, tiled=True)
    small_got = rows_got[width:]

    folded, shared = z_sum(keep, got, small, small_got, dp_axis, z_scalar)
    part_d = after(part_d, shared)
    out_d = grid_swap(part_d, False, "out_d")
    out_keep, out_give, _ = call(
        out_rows_kernel,
        (
            sds((width, row_count), BF),
            sds((width, row_count), BF),
            sds((width, block), BF),
        ),
        (residual, out_o, out_x, out_y, out_d),
        "out_rows",
        scalars=(c_scalar,),
    )

    folded, sums = call(
        join_x_kernel,
        (pair_bf, sds((8, width), F32)),
        (folded, x_swap(folded, "join_x")),
        "join_x",
        scalars=(x_scalar,),
    )
    grad_w_query, grad_w_key, grad_w_value, grad_w_out = call(
        join_core_kernel,
        (one_f32,) * 4,
        (folded, core_swap(folded, "join_core")),
        "join_core",
        scalars=(c_scalar,),
    )

    output = place(out_keep, core_swap(out_give, "out_core"))

    grad_inputs = place(rows_keep, rows_got)
    mask_keep, mask_got = small[:1], small_got[:1]
    grad_mask = jnp.where(c_at == 0, stack(mask_keep, mask_got), stack(mask_got, mask_keep))
    grad_down, grad_gate, grad_up = widen(ffn_grads)
    return (
        jnp.swapaxes(output, 1, 2),
        jnp.swapaxes(grad_inputs, 1, 2),
        grad_mask,
        sums[0],
        grad_w_query.T,
        grad_w_key.T,
        grad_w_value.T,
        grad_w_out,
        sums[2, : bucket_count * total_heads].reshape(bucket_count, total_heads),
        sums[1],
        grad_gate.T,
        grad_up.T,
        grad_down,
    )


def z_sum(mine, got, small, small_got, n, z_scalar):
    rows, width = mine.shape
    if n > 8:
        total = lax.psum((mine + got.astype(F32)).astype(BF), "dp")
        small = lax.psum(small + small_got, "dp")
        half = small.shape[0] // 2

        def row(first):
            both = jnp.concatenate([small[first:half], small[half + first :]], axis=1)
            return both.reshape(1, -1)[:, :width]

        three = jnp.concatenate([row(2), row(8), row(1), jnp.zeros((5, width), F32)], axis=0)
        return jnp.concatenate([total, *split(three)], axis=0), mine
    share = rows // n

    def shift(v, k, name):
        return move(v, "dp", [(i, (i + k) % n) for i in range(n)], name)

    _, own, *give = call(
        share_kernel,
        (sds(mine.shape, F32), sds((share, width), F32), *[sds((share, width), BF)] * (n - 1)),
        (mine, got),
        "share",
        scalars=(z_scalar,),
    )
    gots = [shift(v, k + 1, "share_z") for k, v in enumerate(give)]
    total = call(
        share_sum_kernel,
        sds((share + EXTRA, width), BF),
        (own, small, small_got, *gots),
        "share_sum",
    )
    gots = [shift(total, k, "join_z") for k in range(1, n)]
    joined, _ = call(
        share_join_kernel,
        (sds((rows + EXTRA, width), BF), sds((n, 8, width), F32)),
        (total, *gots),
        "share_join",
        scalars=(z_scalar,),
    )
    return joined, own


def solution(mesh):
    rows = P("dp", ("head", "hid"), None)
    return jax.shard_map(
        per_device,
        mesh=mesh,
        in_specs=(
            rows,
            P("dp"),
            P("dp", None),
            P(),
            P(),
            P(None, "head"),
            P(None, "head"),
            P(None, "head"),
            P("head", None),
            P(),
            P(),
            P(None, ("head", "hid")),
            P(None, ("head", "hid")),
            P(("head", "hid"), None),
            rows,
        ),
        out_specs=(
            rows,
            rows,
            P("dp", ("head", "hid")),
            P(),
            P(None, "head"),
            P(None, "head"),
            P(None, "head"),
            P("head", None),
            P(),
            P(),
            P(None, ("head", "hid")),
            P(None, ("head", "hid")),
            P(("head", "hid"), None),
        ),
        check_vma=False,
    )
```

```python
import functools

import jax
import jax.numpy as jnp
from jax import lax
from jax.experimental import pallas as pl
from jax.experimental.pallas import tpu as pltpu
from jax.sharding import PartitionSpec as P


DH = 64
EPS = 1e-06
NEG = -1e30
BF = jnp.bfloat16
F32 = jnp.float32
GELU_C = 0.7978845608028654
GELU_K = 0.044715
LANES = 128
EXTRA = 16


def cost(us):
    return pl.CostEstimate(flops=0, bytes_accessed=int(us * 3.0e6), transcendentals=0)


NT = (((1,), (1,)), ((), ()))
TN = (((0,), (0,)), ((), ()))


def dot(a, b):
    return jnp.dot(a, b, preferred_element_type=F32)


def dot_nt(a, b):
    return lax.dot_general(a, b, NT, preferred_element_type=F32)


def dot_tn(a, b):
    return lax.dot_general(a, b, TN, preferred_element_type=F32)


def sds(shape, dtype):
    return jax.ShapeDtypeStruct(shape, dtype)


class Order:
    last = None

    @classmethod
    def follow(cls, v):
        return v if cls.last is None else lax.optimization_barrier((v, cls.last))[0]

    @classmethod
    def done(cls, outs):
        cls.last = min(jax.tree.leaves(outs), key=lambda v: v.size)
        return outs


def call(kernel, out_shape, args, name, scalars=(), vmem=12, us=0.01, **kw):
    args = (Order.follow(args[0]), *args[1:])
    in_specs = [pl.BlockSpec(memory_space=pltpu.SMEM)] * len(scalars)
    in_specs += [pl.BlockSpec(memory_space=pltpu.VMEM)] * len(args)
    outs = pl.pallas_call(
        kernel,
        out_shape=out_shape,
        in_specs=in_specs,
        out_specs=jax.tree.map(lambda _: pl.BlockSpec(memory_space=pltpu.VMEM), out_shape),
        compiler_params=pltpu.CompilerParams(vmem_limit_bytes=vmem << 20),
        cost_estimate=cost(us),
        name=name,
        **kw,
    )(*scalars, *args)
    return Order.done(outs)


def hbm(shape, dtype):
    return pltpu.HBM(shape, dtype)


def in_hbm(v):
    return pltpu.with_memory_space_constraint(v, pltpu.HBM)


def move(v, axes, pairs, name):
    with jax.named_scope(name):
        return lax.ppermute(v, axes, pairs)


def lane_sum(v):
    total = v[:, :LANES]
    for at in range(LANES, v.shape[1], LANES):
        total = total + v[:, at : at + LANES]
    return jnp.sum(total.T, axis=0, keepdims=True)


def column(row, width):
    wide = jnp.broadcast_to(row, (LANES, row.shape[1])).T
    return jnp.concatenate([wide] * (width // LANES), axis=1)


def pair_rows(c, own_ref, far_ref):
    own = own_ref[c]
    far = far_ref[c]
    first = c == 0
    return jnp.concatenate([jnp.where(first, own, far), jnp.where(first, far, own)], axis=1)


def pick_kernel(c_ref, first_ref, second_ref, out_ref):
    out_ref[...] = jnp.where(c_ref[0] == 0, first_ref[...], second_ref[...])


def pair_kernel(c_ref, own_ref, far_ref, out_ref):
    out_ref[...] = pair_rows(c_ref[0], own_ref, far_ref)


def prep_kernel(c_ref, own_ref, far_ref, gain_ref, x_ref, n_ref, inv_ref):
    rows = pair_rows(c_ref[0], own_ref, far_ref)
    x_ref[...] = rows
    x = rows.astype(F32)
    inverse = lax.rsqrt(jnp.mean(x * x, axis=0, keepdims=True) + EPS)
    inv_ref[...] = inverse
    n_ref[...] = (x * inverse * column(gain_ref[...], x.shape[1])).astype(BF)


def qkv_kernel(n_ref, wq_ref, wk_ref, wv_ref, q_ref, kv_ref):
    n = n_ref[...]
    inner = wq_ref.shape[0]
    q_ref[...] = dot(wq_ref[...], n).astype(BF)
    kv_ref[:inner] = dot(wk_ref[...], n).astype(BF)
    kv_ref[inner:] = dot(wv_ref[...], n).astype(BF)


def bias_kernel(start_ref, table_ref, mask_ref, out_ref, *, heads, block, q_blocks):
    kb = pl.program_id(0)
    qb = pl.program_id(1)
    start = pl.multiple_of(start_ref[kb * q_blocks + qb], block)
    k_at = pl.multiple_of(kb * block, block)
    mask = column(mask_ref[:, pl.ds(k_at, block)], block)
    for h in range(heads):
        window = table_ref[h : h + 1, pl.ds(start, 2 * block)]
        window = jnp.broadcast_to(window, (block, 2 * block))
        rolled = pltpu.roll(window, block, 1, stride=1, stride_axis=0)
        out_ref[h] = rolled[:, :block] + mask


def make_bias(starts, table, mask_row, heads, block, k_blocks, q_blocks):
    length = k_blocks * block
    outs = pl.pallas_call(
        functools.partial(bias_kernel, heads=heads, block=block, q_blocks=q_blocks),
        out_shape=pltpu.HBM((heads, length, q_blocks * block), F32),
        grid_spec=pltpu.PrefetchScalarGridSpec(
            num_scalar_prefetch=1,
            grid=(k_blocks, q_blocks),
            in_specs=[
                pl.BlockSpec(table.shape, lambda k, q, s: (0, 0)),
                pl.BlockSpec((1, length), lambda k, q, s: (0, 0)),
            ],
            out_specs=pl.BlockSpec((heads, block, block), lambda k, q, s: (0, k, q)),
        ),
        compiler_params=pltpu.CompilerParams(vmem_limit_bytes=16 << 20),
        cost_estimate=cost(0.01),
        name="bias",
    )(starts, table, Order.follow(mask_row))
    return Order.done(outs)


def attn_fwd_kernel(q_ref, k0, k1, k2, k3, bias_ref, p_ref, o_ref, *, inner):
    h = pl.program_id(1)
    at_k = pl.ds(pl.multiple_of(h * DH, DH), DH)
    at_v = pl.ds(pl.multiple_of(inner + h * DH, DH), DH)
    q = q_ref[...]
    parts = [dot_tn(ref[at_k, :], q) for ref in (k0, k1, k2, k3)]
    s = jnp.concatenate(parts, axis=0) + bias_ref[0]
    top = jnp.max(s, axis=0, keepdims=True)
    e = jnp.exp(s - top)
    total = jnp.sum(e, axis=0, keepdims=True)
    p = e * (1.0 / total)
    p_ref[0] = p
    pb = p.astype(BF)
    values = jnp.concatenate([ref[at_v, :] for ref in (k0, k1, k2, k3)], axis=1)
    o_ref[...] = dot(values, pb).astype(BF)


def attn_fwd(q, kvs, bias, heads, block):
    inner, rows = q.shape
    length = bias.shape[1]
    full = lambda i, h: (0, 0)
    slab = pl.BlockSpec((1, length, block), lambda i, h: (h, 0, i))
    head = pl.BlockSpec((DH, block), lambda i, h: (h, i))
    outs = pl.pallas_call(
        functools.partial(attn_fwd_kernel, inner=inner),
        out_shape=(pltpu.HBM((heads, length, rows), F32), sds((inner, rows), BF)),
        grid=(rows // block, heads),
        in_specs=[head] + [pl.BlockSpec(kv.shape, full) for kv in kvs] + [slab],
        out_specs=(slab, head),
        compiler_params=pltpu.CompilerParams(vmem_limit_bytes=14 << 20),
        cost_estimate=cost(0.01),
        name="attn_fwd",
    )(Order.follow(q), *kvs, in_hbm(bias))
    return Order.done(outs)


def diagonals(piece, block):
    total = None
    for shift in range(0, LANES, 8):
        wide = None
        for part in range(block // LANES):
            rows = piece[part * LANES + shift : part * LANES + shift + 8]
            pieces = [jnp.zeros((8, block - part * LANES), F32), rows]
            if part:
                pieces.append(jnp.zeros((8, part * LANES), F32))
            rows = jnp.concatenate(pieces, axis=1)
            wide = rows if wide is None else wide + rows
        if shift:
            wide = pltpu.roll(wide, 2 * block - shift, 1)
        total = wide if total is None else total + wide
    return total


def attn_bwd_kernel(
    start_ref, p_ref, q_ref, do_ref, k0, k1, k2, k3, dq_ref, own_ref, give_ref, col_ref, table_ref,
    acc, col_acc, *, inner, heads, block, q_blocks,
):
    qb = pl.program_id(0)
    h = pl.program_id(1)
    kvs = (k0, k1, k2, k3)
    at_k = pl.ds(pl.multiple_of(h * DH, DH), DH)
    at_v = pl.ds(pl.multiple_of(inner + h * DH, DH), DH)
    half = len(kvs) * block // 2

    @pl.when((qb == 0) & (h == 0))
    def _():
        acc[...] = jnp.zeros_like(acc)
        col_acc[...] = jnp.zeros_like(col_acc)
        table_ref[...] = jnp.zeros_like(table_ref)

    q = q_ref[...]
    do = do_ref[...]
    dp = jnp.concatenate([dot_tn(ref[at_v, :], do) for ref in kvs], axis=0)
    p = p_ref[0]
    inside = jnp.sum(p * dp, axis=0, keepdims=True)
    ds = p * (dp - inside)
    col_acc[...] += ds
    for kb in range(len(kvs)):
        start = pl.multiple_of(start_ref[kb * q_blocks + qb], block)
        piece = ds[kb * block : (kb + 1) * block]
        table_ref[h, :, pl.ds(start, 2 * block)] += diagonals(piece, block)
    dsb = ds.astype(BF)
    pb = p.astype(BF)
    acc[at_k, :] += dot_nt(q, dsb)
    acc[at_v, :] += dot_nt(do, pb)
    keys = jnp.concatenate([ref[at_k, :] for ref in kvs], axis=1)
    dq_ref[...] = dot(keys, dsb).astype(BF)

    @pl.when((qb == q_blocks - 1) & (h == heads - 1))
    def _():
        own_ref[...] = acc[:, :half]
        col = lane_sum(col_acc[...])
        col_ref[...] = col[:, :half]
        give_ref[: 2 * inner] = acc[:, half:].astype(BF)
        give_ref[2 * inner :] = split_rows(col[:, half:])


def split(v):
    high = v.astype(BF)
    return high, (v - high.astype(F32)).astype(BF)


def merge(high, low):
    return high.astype(F32) + low.astype(F32)


def split_rows(row):
    high = row.astype(BF)
    low = (row - high.astype(F32)).astype(BF)
    at = lax.broadcasted_iota(jnp.int32, (EXTRA, row.shape[1]), 0)
    wide = jnp.where(at == 0, high.astype(F32), jnp.where(at == 1, low.astype(F32), 0.0))
    return wide.astype(BF)


def attn_bwd(starts, p, q, do, kvs, heads, block):
    inner, rows = q.shape
    length = p.shape[1]
    half = length // 2
    q_blocks = rows // block
    full = lambda i, h, s: (0, 0)
    head = pl.BlockSpec((DH, block), lambda i, h, s: (h, i))
    outs = pl.pallas_call(
        functools.partial(
            attn_bwd_kernel, inner=inner, heads=heads, block=block, q_blocks=q_blocks
        ),
        out_shape=(
            sds((inner, rows), BF),
            hbm((2 * inner, half), F32),
            hbm((2 * inner + EXTRA, half), BF),
            sds((1, half), F32),
            sds((heads, 8, 2 * length), F32),
        ),
        grid_spec=pltpu.PrefetchScalarGridSpec(
            num_scalar_prefetch=1,
            grid=(q_blocks, heads),
            in_specs=[pl.BlockSpec((1, length, block), lambda i, h, s: (h, 0, i)), head, head]
            + [pl.BlockSpec(kv.shape, full) for kv in kvs],
            out_specs=(
                head,
                pl.BlockSpec((2 * inner, half), full),
                pl.BlockSpec((2 * inner + EXTRA, half), full),
                pl.BlockSpec((1, half), full),
                pl.BlockSpec((heads, 8, 2 * length), lambda i, h, s: (0, 0, 0)),
            ),
            scratch_shapes=[
                pltpu.VMEM((2 * inner, length), F32),
                pltpu.VMEM((length, block), F32),
            ],
        ),
        compiler_params=pltpu.CompilerParams(vmem_limit_bytes=28 << 20),
        cost_estimate=cost(500),
        name="attn_bwd",
    )(starts, in_hbm(p), Order.follow(q), do, *kvs)
    return Order.done(outs)


def halves(c_ref, half):
    return [pl.ds(pl.multiple_of(at * half, half), half) for at in (c_ref[0], 1 - c_ref[0])]


def mid_kernel(
    c_ref, x_ref, m0_ref, m1_ref, w0_ref, w1_ref, w2_ref, gain_ref, res_ref, n_ref, inv_ref
):
    attended = dot_tn(w0_ref[...], m0_ref[...])
    for at, w_ref in zip(halves(c_ref, w1_ref.shape[0]), (w1_ref, w2_ref)):
        attended = attended + dot_tn(w_ref[...], m1_ref[at, :])
    res = x_ref[...].astype(F32) + attended
    res_ref[...] = res
    inverse = lax.rsqrt(jnp.mean(res * res, axis=0, keepdims=True) + EPS)
    inv_ref[...] = inverse
    n_ref[...] = (res * inverse * column(gain_ref[...], res.shape[1])).astype(BF)


def rms_back(rows, inverse, gain, grad):
    scaled = grad * gain
    inside = jnp.mean(rows * scaled, axis=0, keepdims=True)
    return inverse * scaled - rows * (inverse * inverse * inverse * inside)


def mid_back_kernel(
    c_ref, own_ref, ga_ref, gb_ref, gd_ref, dy_ref, res_ref, inv_ref, gain_ref, w0_ref, w1_ref, w2_ref,
    dres_ref, branch_ref, gain_grad_ref, dm0_ref, dm1_ref,
):
    grad = own_ref[...].astype(F32) + ga_ref[...].astype(F32) + gb_ref[...].astype(F32)
    grad = grad + gd_ref[...].astype(F32)
    res = res_ref[...]
    inverse = inv_ref[...]
    gain_grad_ref[...] = lane_sum(grad * (res * inverse))
    gain = column(gain_ref[...], res.shape[1])
    d_res = dy_ref[...].astype(F32) + rms_back(res, inverse, gain, grad)
    dres_ref[...] = d_res
    branch = d_res.astype(BF)
    branch_ref[...] = branch
    dm0_ref[...] = dot(w0_ref[...], branch).astype(BF)
    for at, w_ref in zip(halves(c_ref, w1_ref.shape[0]), (w1_ref, w2_ref)):
        dm1_ref[at, :] = dot(w_ref[...], branch).astype(BF)


def out_grad_kernel(m0_ref, m1_ref, branch_ref, own_ref, far_ref):
    branch = branch_ref[...]
    own_ref[...] = dot_nt(m0_ref[...], branch)
    far_ref[...] = dot_nt(m1_ref[...], branch).astype(BF)


def d_act_kernel(dy_ref, d0, d1, out_ref):
    dy = dy_ref[...]
    for part, w_ref in enumerate((d0, d1)):
        out_ref[part] = dot(w_ref[...], dy)


def ffn_kernel(n_ref, da_ref, g0, g1, u0, u1, a_ref, dg_ref, du_ref, dn_ref):
    n = n_ref[...]
    total = None
    for part, (g_w, u_w) in enumerate(((g0, u0), (g1, u1))):
        gate = dot(g_w[...], n)
        up = dot(u_w[...], n)
        d_act = da_ref[part]
        square = gate * gate
        t = jnp.tanh(gate * (GELU_C + (GELU_C * GELU_K) * square))
        half = 0.5 + 0.5 * t
        gelu = gate * half
        slope = half + gelu * (1.0 - t) * (GELU_C + (3.0 * GELU_C * GELU_K) * square)
        a_ref[part] = (gelu * up).astype(BF)
        d_gate = (d_act * up * slope).astype(BF)
        d_up = (d_act * gelu).astype(BF)
        dg_ref[part] = d_gate
        du_ref[part] = d_up
        more = dot_tn(g_w[...], d_gate) + dot_tn(u_w[...], d_up)
        total = more if total is None else total + more
    dn_ref[...] = total.astype(dn_ref.dtype)


def ffn_chunk(n, d_act, weights, out_dtype):
    width, rows = n.shape
    hidden = weights[0].shape[0]
    mid = sds((2, hidden, rows), BF)
    return call(
        ffn_kernel,
        (mid, mid, mid, sds((width, rows), out_dtype)),
        (n, d_act, *weights[:4]),
        "ffn",
        vmem=20,
    )


def ffn_out_kernel(a_ref, d0, d1, o_ref):
    total = dot_tn(d0[...], a_ref[0]) + dot_tn(d1[...], a_ref[1])
    o_ref[...] = total.astype(o_ref.dtype)


def ffn_out(act, d0, d1, dtype):
    _, hidden, rows = act.shape
    width = d0.shape[1]
    return call(
        ffn_out_kernel, hbm((width, rows), dtype), (act, d0, d1), "ffn_out", vmem=16,
    )


def wgrad_sum_kernel(*refs):
    out_ref = refs[-1]
    n, pieces, rows, _ = out_ref.shape
    got = refs[-2]
    for at in range(pieces):
        mids, blocks = refs[8 * at : 8 * at + 4], refs[8 * at + 4 : 8 * at + 8]
        total = None
        for mid, block in zip(mids, blocks):
            more = dot_nt(mid[0], block[...])
            total = more if total is None else total + more
        total = (total + got[at].astype(F32)).astype(BF)
        for q in range(n):
            out_ref[q, at] = total[q * rows : (q + 1) * rows]


def wgrad_stack_kernel(part, *refs):
    out_ref = refs[-1]
    for at in range(out_ref.shape[0]):
        mids, rows = refs[8 * at : 8 * at + 4], refs[8 * at + 4 : 8 * at + 8]
        total = None
        for mid, row in zip(mids, rows):
            more = dot_nt(mid[part], row[...])
            total = more if total is None else total + more
        out_ref[at] = total.astype(BF)


def wgrad_give(pieces):
    mids, rows = pieces[0]
    shape = (len(pieces), mids[0].shape[1], rows[0].shape[0])
    args = [v for mids, rows in pieces for v in (*mids, *rows)]
    return call(
        functools.partial(wgrad_stack_kernel, 1), sds(shape, BF), args, "wgrad_give",
        vmem=20,
    )


def wgrad_sum(pieces, got, shares):
    mids, rows = pieces[0]
    shape = (shares, len(pieces), mids[0].shape[1] // shares, rows[0].shape[0])
    args = [v for mids, rows in pieces for v in (*mids, *rows)]
    return call(
        wgrad_sum_kernel, hbm(shape, BF), (*args, got), "wgrad_sum", vmem=28,
    )


def kv_sum_kernel(
    own_ref, got_ref, col_ref, dq_ref, n0_ref, n1_ref, wq_ref, wk_ref, wv_ref,
    gain_ref, gain_ffn_ref, rel_ref, dkv_ref, total_ref, give_ref, small_ref,
):
    inner = wk_ref.shape[0]
    width, block = n0_ref.shape
    dq = dq_ref[...]
    d_kv = (own_ref[...] + got_ref[: 2 * inner].astype(F32)).astype(BF)
    dkv_ref[...] = d_kv
    col = col_ref[...] + merge(got_ref[2 * inner : 2 * inner + 1], got_ref[2 * inner + 1 : 2 * inner + 2])
    far = dot_tn(wq_ref[...], dq[:, block:]) + dot_tn(wk_ref[...], d_kv[:inner, block:])
    far = far + dot_tn(wv_ref[...], d_kv[inner:, block:])
    give_ref[:width] = far.astype(BF)
    own = dot_tn(wq_ref[...], dq[:, :block]) + dot_tn(wk_ref[...], d_kv[:inner, :block])
    own = own + dot_tn(wv_ref[...], d_kv[inner:, :block])
    total_ref[...] = own
    gain = lane_sum(own * n0_ref[...].astype(F32) + far * n1_ref[...].astype(F32)) / gain_ref[...]
    small_ref[...] = jnp.zeros_like(small_ref)
    for first, row in ((2, gain), (8, gain_ffn_ref[...])):
        for at in range(0, width, block):
            size = min(block, width - at)
            line = first + at // block
            small_ref[line : line + 1, :size] = row[:, at : at + size]
    small_ref[1:2, : rel_ref.shape[1]] = rel_ref[...]
    small_ref[0:1] = col[:, block:]
    high, low = split(small_ref[...])
    give_ref[width : width + EXTRA] = high
    give_ref[width + EXTRA :] = low
    small_ref[...] = merge(high, low)
    small_ref[0:1] = col[:, :block]


def last_kernel(
    c_ref, own_ref, got_ref, small_ref, x_ref, inv_ref, gain_ref, dres_ref,
    keep_ref, give_ref, keep_small_ref, rows_ref,
):
    width = x_ref.shape[0]
    grad = own_ref[...] + got_ref[:width].astype(F32)
    small = small_ref[...] + merge(got_ref[width : width + EXTRA], got_ref[width + EXTRA :])
    x = x_ref[...].astype(F32)
    gain = column(gain_ref[...], x.shape[1])
    rows_ref[:width] = dres_ref[...] + rms_back(x, inv_ref[...], gain, grad)
    rows_ref[width:] = small
    rows = keep_ref.shape[1]
    mine = pl.ds(pl.multiple_of(c_ref[0] * rows, rows), rows)
    theirs = pl.ds(pl.multiple_of((1 - c_ref[0]) * rows, rows), rows)
    keep_ref[...] = rows_ref[:width, mine]
    give_ref[:width] = rows_ref[:width, theirs]
    keep_small_ref[:EXTRA] = small[:, :rows]
    keep_small_ref[EXTRA:] = small[:, rows:]
    give_ref[width:] = keep_small_ref[...]
    give_ref[width : width + 1] = rows_ref[width : width + 1, theirs]
    keep_small_ref[0:1] = rows_ref[width : width + 1, mine]


def out_rows_kernel(c_ref, res_ref, own_ref, ga_ref, gb_ref, gd_ref, keep_ref, give_ref, rows_ref):
    total = res_ref[...] + (
        own_ref[...].astype(F32)
        + ga_ref[...].astype(F32)
        + gb_ref[...].astype(F32)
        + gd_ref[...].astype(F32)
    )
    rows_ref[...] = total.astype(BF)
    rows = keep_ref.shape[1]
    keep_ref[...] = rows_ref[:, pl.ds(pl.multiple_of(c_ref[0] * rows, rows), rows)]
    give_ref[...] = rows_ref[:, pl.ds(pl.multiple_of((1 - c_ref[0]) * rows, rows), rows)]


def fold_core_kernel(
    c_ref, dq_ref, dkv_ref, n0_ref, n1_ref, go_ref, got_ref, keep_ref, give_ref
):
    inner = dq_ref.shape[0]
    block = n0_ref.shape[1]
    n0 = n0_ref[...]
    n1 = n1_ref[...]

    def gradient(rows):
        return dot_nt(rows[:, :block], n0) + dot_nt(rows[:, block:], n1)

    first = c_ref[0] == 0
    gq = gradient(dq_ref[...])
    gv = gradient(dkv_ref[inner:])
    keep_ref[0] = jnp.where(first, gq, gv)
    give_ref[0] = jnp.where(first, gv, gq).astype(BF)
    gk = gradient(dkv_ref[:inner])
    go = go_ref[...] + got_ref[...].astype(F32)
    keep_ref[1] = jnp.where(first, gk, go)
    give_ref[1] = jnp.where(first, go, gk).astype(BF)


def fold_x_kernel(x_ref, mine_ref, got_ref, keep_ref, give_ref):
    total = mine_ref[...] + got_ref[...].astype(F32)
    first = x_ref[0] == 0
    keep_ref[...] = jnp.where(first, total[0], total[1])
    give_ref[...] = jnp.where(first, total[1], total[0]).astype(BF)


def share_kernel(bit_ref, mine_ref, got_ref, own_ref, give_ref, sum_ref):
    sum_ref[...] = mine_ref[...] + got_ref[...].astype(F32)
    keep, give = halves(bit_ref, own_ref.shape[0])
    own_ref[...] = sum_ref[keep, :]
    give_ref[...] = sum_ref[give, :].astype(BF)


def lines(small, first, width):
    half = small.shape[0] // 2
    pieces = []
    for at in range(-(-width // (2 * LANES))):
        line = first + at
        pieces += [small[line : line + 1], small[half + line : half + line + 1]]
    return jnp.concatenate(pieces, axis=1)[:, :width]


def share_sum_kernel(mine_ref, got_ref, small_ref, small_got_ref, out_ref):
    rows, width = mine_ref.shape
    out_ref[:rows] = (mine_ref[...] + got_ref[...].astype(F32)).astype(BF)
    small = small_ref[...] + small_got_ref[...]
    rel = small[1:2]
    rel = jnp.concatenate([rel, small[EXTRA + 1 : EXTRA + 2]], axis=1)
    rel = jnp.concatenate([rel, jnp.zeros((1, width - rel.shape[1]), F32)], axis=1)
    three = jnp.concatenate(
        [lines(small, 2, width), lines(small, 8, width), rel, jnp.zeros((5, width), F32)], axis=0
    )
    out_ref[rows:] = jnp.concatenate(split(three), axis=0)


def share_join_kernel(z_ref, *refs):
    shares, (out_ref, hold_ref) = refs[:-2], refs[-2:]
    n = len(shares)
    rows = shares[0].shape[0] - EXTRA
    for k, ref in enumerate(shares):
        at = lax.rem(z_ref[0] + n - k, n)
        line, rest, size = 0, at, n
        while size > 1:
            size //= 2
            line = line + lax.rem(rest, 2) * size
            rest = rest // 2
        out_ref[pl.ds(pl.multiple_of(line * rows, rows), rows), :] = ref[:rows]
        hold_ref[at] = merge(ref[rows : rows + 8], ref[rows + 8 :])
    total = hold_ref[0]
    for k in range(1, n):
        total = total + hold_ref[k]
    out_ref[n * rows :] = jnp.concatenate(split(total), axis=0)


def join_x_kernel(x_ref, own_ref, got_ref, out_ref, small_ref):
    inner = out_ref.shape[1]
    first = x_ref[0] == 0
    own = own_ref[:inner]
    got = got_ref[:inner]
    out_ref[0] = jnp.where(first, own, got)
    out_ref[1] = jnp.where(first, got, own)
    small_ref[...] = merge(own_ref[inner : inner + 8], own_ref[inner + 8 :]) + merge(
        got_ref[inner : inner + 8], got_ref[inner + 8 :]
    )


def join_core_kernel(c_ref, own_ref, got_ref, *outs):
    first = c_ref[0] == 0
    own = own_ref[...]
    got = got_ref[...]
    pair = (jnp.where(first, own, got), jnp.where(first, got, own))
    for at, out in enumerate(outs):
        out[...] = pair[at // 2][at % 2].astype(F32)


def place_kernel(c_ref, own_ref, got_ref, out_ref):
    out_ref[c_ref[0]] = own_ref[...]
    out_ref[1 - c_ref[0]] = got_ref[: own_ref.shape[0]]


def widen_kernel(src, *outs):
    for at, out in enumerate(outs):
        out[...] = src[0, at].astype(F32)


def widen(v):
    n, pieces, rows, width = v.shape
    outs = pl.pallas_call(
        widen_kernel,
        out_shape=[sds((n * rows, width), F32)] * pieces,
        grid=(n,),
        in_specs=[pl.BlockSpec((1, pieces, rows, width), lambda i: (i, 0, 0, 0))],
        out_specs=[pl.BlockSpec((rows, width), lambda i: (i, 0))] * pieces,
        compiler_params=pltpu.CompilerParams(vmem_limit_bytes=32 << 20),
        cost_estimate=cost(500),
        name="widen",
    )(in_hbm(Order.follow(v)))
    return Order.done(outs)


def per_device(*args):
    Order.last = None
    return run(*args)


def run(
    inputs,
    lengths,
    delete_mask,
    buckets,
    gain_attn,
    w_query,
    w_key,
    w_value,
    w_out,
    rel_bias,
    gain_ffn,
    gate_weight,
    up_weight,
    down_weight,
    cotangent,
):
    seqs, row_count, width = inputs.shape
    dp_axis = lax.axis_size("dp")
    heads_axis = lax.axis_size("head")
    hid_axis = lax.axis_size("hid")
    assert seqs == 2 and heads_axis == 2 and hid_axis == 4
    z_at = lax.axis_index("dp")
    h_at = lax.axis_index("head")
    hid_at = lax.axis_index("hid")
    c_at = hid_at % 2
    x_at = hid_at // 2
    length = row_count * heads_axis * hid_axis
    block = 2 * row_count
    inner = w_query.shape[1]
    heads = inner // DH
    hidden = gate_weight.shape[1]
    bucket_count, total_heads = rel_bias.shape
    c_scalar = c_at.astype(jnp.int32).reshape(1)
    x_scalar = x_at.astype(jnp.int32).reshape(1)
    z_scalar = z_at.astype(jnp.int32).reshape(1)

    def core_swap(v, name):
        return move(v, "hid", [(i, i ^ 1) for i in range(hid_axis)], name)

    def x_swap(v, name):
        return move(v, "hid", [(i, i ^ 2) for i in range(hid_axis)], name)

    def y_swap(v, name):
        return move(v, "head", [(0, 1), (1, 0)], name)

    def grid_swap(v, relayed, name):
        pairs = []
        for h in range(heads_axis):
            for i in range(hid_axis):
                along_x = not relayed or i % 2 == 1
                along_y = not relayed or i % 2 == 0
                to = ((1 - h) if along_y else h) * hid_axis + ((i ^ 2) if along_x else i)
                pairs.append((h * hid_axis + i, to))
        return move(v, ("head", "hid"), pairs, name)

    def relay(from_x, from_y, name):
        picked = call(
            pick_kernel, sds(from_x.shape, BF), (from_x, from_y), "pick", scalars=(c_scalar,),
        )
        return grid_swap(picked, True, name)

    def stack(a, b):
        return jnp.concatenate([a, b], axis=0)

    def place(own, got):
        shape = sds((2, *own.shape), own.dtype)
        return call(place_kernel, shape, (own, got), "place", scalars=(c_scalar,), us=100)

    def after(v, *earlier):
        return lax.optimization_barrier((v, *earlier))[0]

    x_in = jnp.swapaxes(inputs, 1, 2)
    dy_in = jnp.swapaxes(cotangent, 1, 2)
    wq, wk, wv = w_query.T, w_key.T, w_value.T
    gate_w, up_w = gate_weight.T, up_weight.T
    gain_one = gain_attn.reshape(1, width)
    gain_two = gain_ffn.reshape(1, width)

    w_half = w_out.reshape(2, inner // 2, width)
    w_half = lax.dynamic_index_in_dim(w_half, c_at, 0, keepdims=False)
    x_rows, normed_one, inv_one = call(
        prep_kernel,
        (sds((width, block), BF), sds((width, block), BF), sds((1, block), F32)),
        (in_hbm(x_in), core_swap(x_in, "x_core"), gain_one),
        "prep",
        vmem=20,
        scalars=(c_scalar,),
    )
    normed_far_raw = y_swap(normed_one, "n1_y")

    dy_own = call(
        pair_kernel,
        sds((width, block), BF),
        (in_hbm(dy_in), in_hbm(core_swap(dy_in, "dy_core"))),
        "pair",
        vmem=16,
        scalars=(c_scalar,),
    )

    gate_other = core_swap(gate_w, "gate_core")
    up_other = core_swap(up_w, "up_core")
    down_other = core_swap(down_weight, "down_core")
    ffn_weights = (gate_w, gate_other, up_w, up_other, down_weight, down_other)
    def project(n):
        return call(
            qkv_kernel,
            (sds((inner, block), BF), sds((2 * inner, block), BF)),
            (n, wq, wk, wv),
            "qkv",
        )

    q_own, kv_own = project(normed_one)
    base = jnp.stack(
        [(h * 2 + x) * block for x in (x_at, 1 - x_at) for h in (h_at, 1 - h_at)]
    ).astype(jnp.int32)
    starts = (length - block - (base[:, None] - base[None, :2])).reshape(-1).astype(jnp.int32)
    bucket_rev = jnp.concatenate([jnp.full((1,), -1, jnp.int32), buckets[::-1]])
    hot = bucket_rev[None, :] == jnp.arange(bucket_count, dtype=jnp.int32)[:, None]
    local_bias = lax.dynamic_slice_in_dim(rel_bias, h_at * heads, heads, 1)
    table = jnp.sum(jnp.where(hot[None], local_bias.T[:, :, None], 0.0), axis=1)
    table = jnp.concatenate([table, jnp.zeros((8 - heads, 2 * length), F32)], axis=0)
    seq_mask = lax.dynamic_index_in_dim(delete_mask, c_at, 0, keepdims=False)
    seq_len = lax.dynamic_index_in_dim(lengths, c_at, 0, keepdims=False)
    seq_mask = jnp.where(jnp.arange(length, dtype=jnp.int32) < seq_len, seq_mask, NEG)
    seq_mask = seq_mask.reshape(2, 2, block)
    seq_mask = jnp.where(h_at == 0, seq_mask, seq_mask[::-1])
    seq_mask = jnp.where(x_at == 0, seq_mask, seq_mask[:, ::-1])
    seq_mask = jnp.swapaxes(seq_mask, 0, 1).reshape(1, length)
    seq_mask = after(seq_mask, gate_other, up_other)
    bias = make_bias(starts, table, seq_mask, heads, block, 4, 2)

    kv_own_x = x_swap(kv_own, "kv_own_x")
    normed_far_raw = after(normed_far_raw, bias, kv_own)
    normed_far = after(normed_far_raw, down_other, kv_own_x)
    w_half = y_swap(after(w_half, normed_far_raw), "wout_y")
    dy_y = y_swap(after(dy_own, w_half), "dy_y")
    w_half_got = core_swap(w_half, "wout_core")
    q_far, kv_far = project(normed_far)
    kv_far_x = x_swap(kv_far, "kv_far_x")
    dy_x = x_swap(after(dy_own, kv_far_x), "dy_x")
    queries = jnp.concatenate([q_own, q_far], axis=1)
    kvs = (kv_own, kv_far, kv_own_x, kv_far_x)

    probs, mixed = attn_fwd(queries, kvs, bias, heads, block)
    mixed_far = y_swap(mixed[:, block:], "mixed_y")
    dy_d = relay(dy_x, dy_y, "dy_d")
    mixed_own = mixed[:, :block]
    residual, normed_two, inv_two = call(
        mid_kernel,
        (hbm((width, block), F32), sds((width, block), BF), sds((1, block), F32)),
        (x_rows, mixed_own, mixed_far, w_out, w_half, w_half_got, gain_two),
        "mid",
        vmem=20,
        scalars=(c_scalar,),
    )

    n_x = x_swap(normed_two, "n2_x")
    n_y = y_swap(normed_two, "n2_y")
    def d_act_of(dy):
        shape = sds((2, hidden, block), F32)
        return call(d_act_kernel, shape, (dy, down_weight, down_other), "d_act")

    da_own = d_act_of(dy_own)
    act_o, dg_o, du_o, dn_o = ffn_chunk(normed_two, da_own, ffn_weights, BF)
    da_x = d_act_of(dy_x)
    da_y = d_act_of(dy_y)
    n_d = relay(n_x, n_y, "n2_d")
    act_x, dg_x, du_x, dn_x = ffn_chunk(n_x, da_x, ffn_weights, BF)
    got_x = x_swap(dn_x, "dn_x")
    act_y, dg_y, du_y, dn_y = ffn_chunk(n_y, da_y, ffn_weights, BF)
    got_y = y_swap(dn_y, "dn_y")
    act_d, dg_d, du_d, dn_d = ffn_chunk(n_d, d_act_of(dy_d), ffn_weights, BF)
    got_d = grid_swap(dn_d, False, "dn_d")

    n_all = (normed_two, n_x, n_y, n_d)
    dy_all = (dy_own, dy_x, dy_y, dy_d)
    pieces = (
        ((act_o, act_x, act_y, act_d), dy_all),
        ((dg_o, dg_x, dg_y, dg_d), n_all),
        ((du_o, du_x, du_y, du_d), n_all),
    )
    out_o = ffn_out(act_o, down_weight, down_other, BF)
    mids, rows = pieces[0]
    pieces = (((after(mids[0], got_x, got_y), *mids[1:]), rows), *pieces[1:])
    given = core_swap(wgrad_give(pieces), "wgrad_core")
    part_x = ffn_out(act_x, down_weight, down_other, BF)
    part_y = ffn_out(act_y, down_weight, down_other, BF)
    part_d = ffn_out(act_d, down_weight, down_other, BF)
    shares = dp_axis if dp_axis <= 8 else 1
    ffn_grads = wgrad_sum(pieces, given, shares)
    if shares > 1:
        ffn_grads = lax.psum_scatter(ffn_grads, "dp", scatter_dimension=0, tiled=True)
    else:
        ffn_grads = lax.psum(ffn_grads, "dp")


    d_residual, d_branch, gain_ffn_part, d_mixed_own, d_mixed_give = call(
        mid_back_kernel,
        (
            hbm((width, block), F32),
            sds((width, block), BF),
            sds((1, width), F32),
            sds((inner, block), BF),
            sds((inner, block), BF),
        ),
        (*map(in_hbm, (dn_o, got_x, got_y, got_d, dy_own, residual)), inv_two, gain_two, w_out, w_half, w_half_got),
        "mid_back",
        vmem=24,
        scalars=(c_scalar,),
    )
    d_mixed = jnp.concatenate([d_mixed_own, y_swap(d_mixed_give, "dmixed_y")], axis=1)

    dq, dkv_own, dkv_give, col, table_grad = attn_bwd(
        starts, probs, queries, d_mixed, kvs, heads, block
    )
    dkv_got = x_swap(dkv_give, "dkv_x")
    out_x = in_hbm(x_swap(after(part_x, got_d), "out_x"))
    out_y = in_hbm(y_swap(after(part_y, got_d), "out_y"))
    d_branch = after(d_branch, dq)
    grad_out_own, grad_out_give = call(
        out_grad_kernel,
        (hbm((inner, width), F32), hbm((inner, width), BF)),
        (mixed_own, mixed_far, d_branch),
        "out_grad",
        vmem=20,
    )
    grad_out_got = y_swap(grad_out_give, "gout_y")
    dkv_got = after(dkv_got, out_x, out_y)
    table_grad = sum(jnp.roll(table_grad[:, i], -i, axis=1) for i in range(8))
    grad_rel = jnp.sum(jnp.where(hot[None], table_grad[:, None, :], 0.0), axis=2).T
    grad_rel = lax.dynamic_update_slice_in_dim(
        jnp.zeros((bucket_count, total_heads), F32), grad_rel, h_at * heads, 1
    )
    d_kv, back_own, back_give, small = call(
        kv_sum_kernel,
        (
            sds((2 * inner, 2 * block), BF),
            hbm((width, block), F32),
            hbm((width + 2 * EXTRA, block), BF),
            sds((EXTRA, block), F32),
        ),
        (
            *map(in_hbm, (dkv_own, dkv_got)), col,
            dq, *map(in_hbm, (normed_one, normed_far)), wq, wk, wv,
            gain_one, gain_ffn_part, grad_rel.reshape(1, -1),
        ),
        "kv_sum",
        vmem=24,
    )
    back_got = y_swap(back_give, "back_y")

    pair_f32, pair_bf = sds((2, inner, width), F32), sds((2, inner, width), BF)
    one_f32, one_bf = sds((inner, width), F32), sds((inner, width), BF)
    keep, give = call(
        fold_core_kernel,
        (hbm(pair_f32.shape, F32), hbm(pair_bf.shape, BF)),
        (dq, d_kv, *map(in_hbm, (normed_one, normed_far, grad_out_own, grad_out_got))),
        "fold_core",
        scalars=(c_scalar,),
        vmem=28,
    )
    keep, give = call(
        fold_x_kernel,
        (one_f32, one_bf),
        (in_hbm(keep), in_hbm(core_swap(give, "fold_core"))),
        "fold_x",
        vmem=20,
        scalars=(x_scalar,),
    )
    got = x_swap(give, "fold_x")
    steps = [1 << k for k in range(dp_axis.bit_length() - 1)]
    short = shares > 1 and 1 << len(steps) == dp_axis
    if short:
        keep, got = z_share(keep, got, steps[0], dp_axis, z_at)
    rows_keep, rows_give, small, _ = call(
        last_kernel,
        (
            sds((width, row_count), F32),
            sds((width + 2 * EXTRA, row_count), F32),
            sds((2 * EXTRA, row_count), F32),
            sds((width + EXTRA, block), F32),
        ),
        (in_hbm(back_own), in_hbm(back_got), small, in_hbm(x_rows), inv_one, gain_one, in_hbm(d_residual)),
        "last",
        vmem=24,
        scalars=(c_scalar,),
    )
    rows_got = core_swap(rows_give, "grad_core")
    small_got = rows_got[width:]
    if shares > 1:
        ffn_grads = lax.all_gather(after(ffn_grads, rows_keep), "dp", axis=0, tiled=True)
    if short:
        for step in steps[1:]:
            keep, got = z_share(keep, got, step, dp_axis, z_at)
        folded = z_join(keep, got, small, small_got, dp_axis, z_scalar)
    else:
        folded = z_psum(keep, got, small, small_got)

    part_d = after(part_d, rows_keep)
    out_d = grid_swap(part_d, False, "out_d")
    out_keep, out_give, _ = call(
        out_rows_kernel,
        (
            sds((width, row_count), BF),
            sds((width, row_count), BF),
            sds((width, block), BF),
        ),
        tuple(map(in_hbm, (residual, out_o, out_x, out_y, out_d))),
        "out_rows",
        vmem=24,
        scalars=(c_scalar,),
    )

    joined = x_swap(folded, "join_x")
    grad_inputs = place(rows_keep, rows_got)
    folded, sums = call(
        join_x_kernel,
        (pair_bf, sds((8, width), F32)),
        (folded, joined),
        "join_x",
        scalars=(x_scalar,),
    )
    joined = core_swap(folded, "join_core")
    output = place(out_keep, core_swap(out_give, "out_core"))
    grad_w_query, grad_w_key, grad_w_value, grad_w_out = call(
        join_core_kernel,
        (one_f32,) * 4,
        (folded, joined),
        "join_core",
        scalars=(c_scalar,),
    )
    mask_keep, mask_got = small[:1], small_got[:1]
    grad_mask = jnp.where(c_at == 0, stack(mask_keep, mask_got), stack(mask_got, mask_keep))
    grad_down, grad_gate, grad_up = widen(ffn_grads)
    return (
        jnp.swapaxes(output, 1, 2),
        jnp.swapaxes(grad_inputs, 1, 2),
        grad_mask,
        sums[0],
        grad_w_query.T,
        grad_w_key.T,
        grad_w_value.T,
        grad_w_out,
        sums[2, : bucket_count * total_heads].reshape(bucket_count, total_heads),
        sums[1],
        grad_gate.T,
        grad_up.T,
        grad_down,
    )


def z_swap(v, step, n, name):
    return move(v, "dp", [(i, i ^ step) for i in range(n)], name)


def z_share(mine, got, step, n, z_at):
    bit = ((z_at // step) % 2).astype(jnp.int32).reshape(1)
    rows, width = mine.shape
    half = (rows // 2, width)
    mine, give, _ = call(
        share_kernel,
        (sds(half, F32), sds(half, BF), sds((rows, width), F32)),
        (mine, got),
        "share",
        scalars=(bit,),
    )
    return mine, z_swap(give, step, n, "share_z")


def z_join(mine, got, small, small_got, n, z_scalar):
    rows, width = mine.shape
    total = call(
        share_sum_kernel,
        sds((rows + EXTRA, width), BF),
        (mine, got, small, small_got),
        "share_sum",
    )
    gots = [
        move(total, "dp", [(i, (i + k) % n) for i in range(n)], "join_z") for k in range(1, n)
    ]
    joined, _ = call(
        share_join_kernel,
        (sds((n * rows + EXTRA, width), BF), sds((n, 8, width), F32)),
        (total, *gots),
        "share_join",
        scalars=(z_scalar,),
    )
    return joined


def z_psum(mine, got, small, small_got):
    width = mine.shape[1]
    total = lax.psum((mine + got.astype(F32)).astype(BF), "dp")
    small = lax.psum(small + small_got, "dp")
    half = small.shape[0] // 2

    def row(first):
        both = jnp.concatenate([small[first:half], small[half + first :]], axis=1)
        return both.reshape(1, -1)[:, :width]

    three = jnp.concatenate([row(2), row(8), row(1), jnp.zeros((5, width), F32)], axis=0)
    return jnp.concatenate([total, *split(three)], axis=0)


def solution(mesh):
    rows = P("dp", ("head", "hid"), None)
    return jax.shard_map(
        per_device,
        mesh=mesh,
        in_specs=(
            rows,
            P("dp"),
            P("dp", None),
            P(),
            P(),
            P(None, "head"),
            P(None, "head"),
            P(None, "head"),
            P("head", None),
            P(),
            P(),
            P(None, ("head", "hid")),
            P(None, ("head", "hid")),
            P(("head", "hid"), None),
            rows,
        ),
        out_specs=(
            rows,
            rows,
            P("dp", ("head", "hid")),
            P(),
            P(None, "head"),
            P(None, "head"),
            P(None, "head"),
            P("head", None),
            P(),
            P(),
            P(None, ("head", "hid")),
            P(None, ("head", "hid")),
            P(("head", "hid"), None),
        ),
        check_vma=False,
    )
```

```python
import functools

import jax
import jax.numpy as jnp
from jax import lax
from jax.experimental import pallas as pl
from jax.experimental.pallas import tpu as pltpu
from jax.sharding import PartitionSpec as P


DH = 64
EPS = 1e-06
NEG = -1e30
BF = jnp.bfloat16
F32 = jnp.float32
GELU_C = 0.7978845608028654
GELU_K = 0.044715
LANES = 128
EXTRA = 16


def cost(us):
    return pl.CostEstimate(flops=0, bytes_accessed=int(us * 3.0e6), transcendentals=0)


NT = (((1,), (1,)), ((), ()))
TN = (((0,), (0,)), ((), ()))


def dot(a, b):
    return jnp.dot(a, b, preferred_element_type=F32)


def dot_nt(a, b):
    return lax.dot_general(a, b, NT, preferred_element_type=F32)


def dot_tn(a, b):
    return lax.dot_general(a, b, TN, preferred_element_type=F32)


def sds(shape, dtype):
    return jax.ShapeDtypeStruct(shape, dtype)


class Order:
    last = None

    @classmethod
    def follow(cls, v):
        return v if cls.last is None else lax.optimization_barrier((v, cls.last))[0]

    @classmethod
    def done(cls, outs):
        cls.last = min(jax.tree.leaves(outs), key=lambda v: v.size)
        return outs


def call(kernel, out_shape, args, name, scalars=(), vmem=12, us=0.01, **kw):
    args = (Order.follow(args[0]), *args[1:])
    in_specs = [pl.BlockSpec(memory_space=pltpu.SMEM)] * len(scalars)
    in_specs += [pl.BlockSpec(memory_space=pltpu.VMEM)] * len(args)
    outs = pl.pallas_call(
        kernel,
        out_shape=out_shape,
        in_specs=in_specs,
        out_specs=jax.tree.map(lambda _: pl.BlockSpec(memory_space=pltpu.VMEM), out_shape),
        compiler_params=pltpu.CompilerParams(vmem_limit_bytes=vmem << 20),
        cost_estimate=cost(us),
        name=name,
        **kw,
    )(*scalars, *args)
    return Order.done(outs)


def hbm(shape, dtype):
    return pltpu.HBM(shape, dtype)


def in_hbm(v):
    return pltpu.with_memory_space_constraint(v, pltpu.HBM)


def move(v, axes, pairs, name):
    with jax.named_scope(name):
        return lax.ppermute(v, axes, pairs)


def lane_sum(v):
    total = v[:, :LANES]
    for at in range(LANES, v.shape[1], LANES):
        total = total + v[:, at : at + LANES]
    return jnp.sum(total.T, axis=0, keepdims=True)


def column(row, width):
    wide = jnp.broadcast_to(row, (LANES, row.shape[1])).T
    return jnp.concatenate([wide] * (width // LANES), axis=1)


def pair_rows(c, own_ref, far_ref):
    own = own_ref[c]
    far = far_ref[c]
    first = c == 0
    return jnp.concatenate([jnp.where(first, own, far), jnp.where(first, far, own)], axis=1)


def pick_kernel(c_ref, first_ref, second_ref, out_ref):
    out_ref[...] = jnp.where(c_ref[0] == 0, first_ref[...], second_ref[...])


def pair_kernel(c_ref, own_ref, far_ref, out_ref):
    out_ref[...] = pair_rows(c_ref[0], own_ref, far_ref)


def prep_kernel(c_ref, own_ref, far_ref, gain_ref, x_ref, n_ref, inv_ref):
    rows = pair_rows(c_ref[0], own_ref, far_ref)
    x_ref[...] = rows
    x = rows.astype(F32)
    inverse = lax.rsqrt(jnp.mean(x * x, axis=0, keepdims=True) + EPS)
    inv_ref[...] = inverse
    n_ref[...] = (x * inverse * column(gain_ref[...], x.shape[1])).astype(BF)


def qkv_kernel(n_ref, wq_ref, wk_ref, wv_ref, q_ref, kv_ref):
    n = n_ref[...]
    inner = wq_ref.shape[0]
    q_ref[...] = dot(wq_ref[...], n).astype(BF)
    kv_ref[:inner] = dot(wk_ref[...], n).astype(BF)
    kv_ref[inner:] = dot(wv_ref[...], n).astype(BF)


def bias_kernel(start_ref, table_ref, mask_ref, out_ref, *, heads, block, q_blocks):
    kb = pl.program_id(0)
    qb = pl.program_id(1)
    start = pl.multiple_of(start_ref[kb * q_blocks + qb], block)
    k_at = pl.multiple_of(kb * block, block)
    mask = column(mask_ref[:, pl.ds(k_at, block)], block)
    for h in range(heads):
        window = table_ref[h : h + 1, pl.ds(start, 2 * block)]
        window = jnp.broadcast_to(window, (block, 2 * block))
        rolled = pltpu.roll(window, block, 1, stride=1, stride_axis=0)
        out_ref[h] = rolled[:, :block] + mask


def make_bias(starts, table, mask_row, heads, block, k_blocks, q_blocks):
    length = k_blocks * block
    outs = pl.pallas_call(
        functools.partial(bias_kernel, heads=heads, block=block, q_blocks=q_blocks),
        out_shape=pltpu.HBM((heads, length, q_blocks * block), F32),
        grid_spec=pltpu.PrefetchScalarGridSpec(
            num_scalar_prefetch=1,
            grid=(k_blocks, q_blocks),
            in_specs=[
                pl.BlockSpec(table.shape, lambda k, q, s: (0, 0)),
                pl.BlockSpec((1, length), lambda k, q, s: (0, 0)),
            ],
            out_specs=pl.BlockSpec((heads, block, block), lambda k, q, s: (0, k, q)),
        ),
        compiler_params=pltpu.CompilerParams(vmem_limit_bytes=16 << 20),
        cost_estimate=cost(0.01),
        name="bias",
    )(starts, table, Order.follow(mask_row))
    return Order.done(outs)


def attn_fwd_kernel(q_ref, k0, k1, k2, k3, bias_ref, p_ref, o_ref, *, inner):
    h = pl.program_id(1)
    at_k = pl.ds(pl.multiple_of(h * DH, DH), DH)
    at_v = pl.ds(pl.multiple_of(inner + h * DH, DH), DH)
    q = q_ref[...]
    parts = [dot_tn(ref[at_k, :], q) for ref in (k0, k1, k2, k3)]
    s = jnp.concatenate(parts, axis=0) + bias_ref[0]
    top = jnp.max(s, axis=0, keepdims=True)
    e = jnp.exp(s - top)
    total = jnp.sum(e, axis=0, keepdims=True)
    p = e * (1.0 / total)
    p_ref[0] = p
    pb = p.astype(BF)
    values = jnp.concatenate([ref[at_v, :] for ref in (k0, k1, k2, k3)], axis=1)
    o_ref[...] = dot(values, pb).astype(BF)


def attn_fwd(q, kvs, bias, heads, block):
    inner, rows = q.shape
    length = bias.shape[1]
    full = lambda i, h: (0, 0)
    slab = pl.BlockSpec((1, length, block), lambda i, h: (h, 0, i))
    head = pl.BlockSpec((DH, block), lambda i, h: (h, i))
    outs = pl.pallas_call(
        functools.partial(attn_fwd_kernel, inner=inner),
        out_shape=(pltpu.HBM((heads, length, rows), F32), sds((inner, rows), BF)),
        grid=(rows // block, heads),
        in_specs=[head] + [pl.BlockSpec(kv.shape, full) for kv in kvs] + [slab],
        out_specs=(slab, head),
        compiler_params=pltpu.CompilerParams(vmem_limit_bytes=14 << 20),
        cost_estimate=cost(0.01),
        name="attn_fwd",
    )(Order.follow(q), *kvs, in_hbm(bias))
    return Order.done(outs)


def diagonals(piece, block):
    total = None
    for shift in range(0, LANES, 8):
        wide = None
        for part in range(block // LANES):
            rows = piece[part * LANES + shift : part * LANES + shift + 8]
            pieces = [jnp.zeros((8, block - part * LANES), F32), rows]
            if part:
                pieces.append(jnp.zeros((8, part * LANES), F32))
            rows = jnp.concatenate(pieces, axis=1)
            wide = rows if wide is None else wide + rows
        if shift:
            wide = pltpu.roll(wide, 2 * block - shift, 1)
        total = wide if total is None else total + wide
    return total


def attn_bwd_kernel(
    start_ref, p_ref, q_ref, do_ref, k0, k1, k2, k3, dq_ref, own_ref, give_ref, col_ref, table_ref,
    acc, col_acc, *, inner, heads, block, q_blocks,
):
    qb = pl.program_id(0)
    h = pl.program_id(1)
    kvs = (k0, k1, k2, k3)
    at_k = pl.ds(pl.multiple_of(h * DH, DH), DH)
    at_v = pl.ds(pl.multiple_of(inner + h * DH, DH), DH)
    half = len(kvs) * block // 2

    @pl.when((qb == 0) & (h == 0))
    def _():
        acc[...] = jnp.zeros_like(acc)
        col_acc[...] = jnp.zeros_like(col_acc)
        table_ref[...] = jnp.zeros_like(table_ref)

    q = q_ref[...]
    do = do_ref[...]
    dp = jnp.concatenate([dot_tn(ref[at_v, :], do) for ref in kvs], axis=0)
    p = p_ref[0]
    inside = jnp.sum(p * dp, axis=0, keepdims=True)
    ds = p * (dp - inside)
    col_acc[...] += ds
    for kb in range(len(kvs)):
        start = pl.multiple_of(start_ref[kb * q_blocks + qb], block)
        piece = ds[kb * block : (kb + 1) * block]
        table_ref[h, :, pl.ds(start, 2 * block)] += diagonals(piece, block)
    dsb = ds.astype(BF)
    pb = p.astype(BF)
    acc[at_k, :] += dot_nt(q, dsb)
    acc[at_v, :] += dot_nt(do, pb)
    keys = jnp.concatenate([ref[at_k, :] for ref in kvs], axis=1)
    dq_ref[...] = dot(keys, dsb).astype(BF)

    @pl.when((qb == q_blocks - 1) & (h == heads - 1))
    def _():
        own_ref[...] = acc[:, :half]
        col = lane_sum(col_acc[...])
        col_ref[...] = col[:, :half]
        give_ref[: 2 * inner] = acc[:, half:].astype(BF)
        give_ref[2 * inner :] = split_rows(col[:, half:])


def split(v):
    high = v.astype(BF)
    return high, (v - high.astype(F32)).astype(BF)


def merge(high, low):
    return high.astype(F32) + low.astype(F32)


def split_rows(row):
    high = row.astype(BF)
    low = (row - high.astype(F32)).astype(BF)
    at = lax.broadcasted_iota(jnp.int32, (EXTRA, row.shape[1]), 0)
    wide = jnp.where(at == 0, high.astype(F32), jnp.where(at == 1, low.astype(F32), 0.0))
    return wide.astype(BF)


def attn_bwd(starts, p, q, do, kvs, heads, block):
    inner, rows = q.shape
    length = p.shape[1]
    half = length // 2
    q_blocks = rows // block
    full = lambda i, h, s: (0, 0)
    head = pl.BlockSpec((DH, block), lambda i, h, s: (h, i))
    outs = pl.pallas_call(
        functools.partial(
            attn_bwd_kernel, inner=inner, heads=heads, block=block, q_blocks=q_blocks
        ),
        out_shape=(
            sds((inner, rows), BF),
            hbm((2 * inner, half), F32),
            hbm((2 * inner + EXTRA, half), BF),
            sds((1, half), F32),
            sds((heads, 8, 2 * length), F32),
        ),
        grid_spec=pltpu.PrefetchScalarGridSpec(
            num_scalar_prefetch=1,
            grid=(q_blocks, heads),
            in_specs=[pl.BlockSpec((1, length, block), lambda i, h, s: (h, 0, i)), head, head]
            + [pl.BlockSpec(kv.shape, full) for kv in kvs],
            out_specs=(
                head,
                pl.BlockSpec((2 * inner, half), full),
                pl.BlockSpec((2 * inner + EXTRA, half), full),
                pl.BlockSpec((1, half), full),
                pl.BlockSpec((heads, 8, 2 * length), lambda i, h, s: (0, 0, 0)),
            ),
            scratch_shapes=[
                pltpu.VMEM((2 * inner, length), F32),
                pltpu.VMEM((length, block), F32),
            ],
        ),
        compiler_params=pltpu.CompilerParams(vmem_limit_bytes=28 << 20),
        cost_estimate=cost(500),
        name="attn_bwd",
    )(starts, in_hbm(p), Order.follow(q), do, *kvs)
    return Order.done(outs)


def halves(c_ref, half):
    return [pl.ds(pl.multiple_of(at * half, half), half) for at in (c_ref[0], 1 - c_ref[0])]


def mid_kernel(
    c_ref, x_ref, m0_ref, m1_ref, w0_ref, w1_ref, w2_ref, gain_ref, res_ref, n_ref, inv_ref
):
    attended = dot_tn(w0_ref[...], m0_ref[...])
    for at, w_ref in zip(halves(c_ref, w1_ref.shape[0]), (w1_ref, w2_ref)):
        attended = attended + dot_tn(w_ref[...], m1_ref[at, :])
    res = x_ref[...].astype(F32) + attended
    res_ref[...] = res
    inverse = lax.rsqrt(jnp.mean(res * res, axis=0, keepdims=True) + EPS)
    inv_ref[...] = inverse
    n_ref[...] = (res * inverse * column(gain_ref[...], res.shape[1])).astype(BF)


def rms_back(rows, inverse, gain, grad):
    scaled = grad * gain
    inside = jnp.mean(rows * scaled, axis=0, keepdims=True)
    return inverse * scaled - rows * (inverse * inverse * inverse * inside)


def mid_back_kernel(
    c_ref, own_ref, ga_ref, gb_ref, gd_ref, dy_ref, res_ref, inv_ref, gain_ref, w0_ref, w1_ref, w2_ref,
    dres_ref, branch_ref, gain_grad_ref, dm0_ref, dm1_ref,
):
    grad = own_ref[...].astype(F32) + ga_ref[...].astype(F32) + gb_ref[...].astype(F32)
    grad = grad + gd_ref[...].astype(F32)
    res = res_ref[...]
    inverse = inv_ref[...]
    gain_grad_ref[...] = lane_sum(grad * (res * inverse))
    gain = column(gain_ref[...], res.shape[1])
    d_res = dy_ref[...].astype(F32) + rms_back(res, inverse, gain, grad)
    dres_ref[...] = d_res
    branch = d_res.astype(BF)
    branch_ref[...] = branch
    dm0_ref[...] = dot(w0_ref[...], branch).astype(BF)
    for at, w_ref in zip(halves(c_ref, w1_ref.shape[0]), (w1_ref, w2_ref)):
        dm1_ref[at, :] = dot(w_ref[...], branch).astype(BF)


def out_grad_kernel(m0_ref, m1_ref, branch_ref, own_ref, far_ref):
    branch = branch_ref[...]
    own_ref[...] = dot_nt(m0_ref[...], branch)
    far_ref[...] = dot_nt(m1_ref[...], branch).astype(BF)


def d_act_kernel(dy_ref, d0, d1, out_ref):
    dy = dy_ref[...]
    for part, w_ref in enumerate((d0, d1)):
        out_ref[part] = dot(w_ref[...], dy)


def ffn_kernel(n_ref, da_ref, g0, g1, u0, u1, a_ref, dg_ref, du_ref, dn_ref):
    n = n_ref[...]
    total = None
    for part, (g_w, u_w) in enumerate(((g0, u0), (g1, u1))):
        gate = dot(g_w[...], n)
        up = dot(u_w[...], n)
        d_act = da_ref[part]
        square = gate * gate
        t = jnp.tanh(gate * (GELU_C + (GELU_C * GELU_K) * square))
        half = 0.5 + 0.5 * t
        gelu = gate * half
        slope = half + gelu * (1.0 - t) * (GELU_C + (3.0 * GELU_C * GELU_K) * square)
        a_ref[part] = (gelu * up).astype(BF)
        d_gate = (d_act * up * slope).astype(BF)
        d_up = (d_act * gelu).astype(BF)
        dg_ref[part] = d_gate
        du_ref[part] = d_up
        more = dot_tn(g_w[...], d_gate) + dot_tn(u_w[...], d_up)
        total = more if total is None else total + more
    dn_ref[...] = total.astype(dn_ref.dtype)


def ffn_chunk(n, d_act, weights, out_dtype):
    width, rows = n.shape
    hidden = weights[0].shape[0]
    mid = sds((2, hidden, rows), BF)
    return call(
        ffn_kernel,
        (mid, mid, mid, sds((width, rows), out_dtype)),
        (n, d_act, *weights[:4]),
        "ffn",
        vmem=20,
    )


def ffn_out_kernel(a_ref, d0, d1, o_ref):
    total = dot_tn(d0[...], a_ref[0]) + dot_tn(d1[...], a_ref[1])
    o_ref[...] = total.astype(o_ref.dtype)


def ffn_out(act, d0, d1, dtype):
    _, hidden, rows = act.shape
    width = d0.shape[1]
    return call(
        ffn_out_kernel, hbm((width, rows), dtype), (act, d0, d1), "ffn_out", vmem=16,
    )


def mids_shape(refs):
    return refs[0].shape[1], refs[4].shape[0]


def packing(rows, width):
    full, rest = divmod(width, LANES)
    assert 2 * rest == LANES and rows % 16 == 0
    half = rows // 2
    plan = []
    for at in range(full):
        lanes = slice(at * LANES, (at + 1) * LANES)
        plan.append((lanes, (slice(at * rows, (at + 1) * rows), ((0, rows),))))
    lanes = slice(full * LANES, width)
    plan.append((lanes, (slice(full * rows, full * rows + half), ((0, half), (half, half)))))
    return plan


def wgrad_sum_kernel(*refs):
    out_ref = refs[-1]
    n, pieces = out_ref.shape[:2]
    hidden, width = mids_shape(refs)
    rows = hidden // n
    gots = [(ref, at) for ref in refs[8 * pieces : -1] for at in range(ref.shape[0])]
    for at in range(pieces):
        mids, blocks = refs[8 * at : 8 * at + 4], refs[8 * at + 4 : 8 * at + 8]
        total = None
        for mid, block in zip(mids, blocks):
            more = dot_nt(mid[0], block[...])
            total = more if total is None else total + more
        got, line = gots[at]
        total = total + got[line].astype(F32)
        for q in range(n):
            share = total[q * rows : (q + 1) * rows]
            for lanes, places in packing(rows, width):
                piece = [share[first : first + size, lanes] for first, size in places[1]]
                out_ref[q, at, places[0]] = jnp.concatenate(piece, axis=1).astype(BF)


def wgrad_stack_kernel(part, *refs):
    out_ref = refs[-1]
    for at in range(out_ref.shape[0]):
        mids, rows = refs[8 * at : 8 * at + 4], refs[8 * at + 4 : 8 * at + 8]
        total = None
        for mid, row in zip(mids, rows):
            more = dot_nt(mid[part], row[...])
            total = more if total is None else total + more
        out_ref[at] = total.astype(BF)


def wgrad_give(pieces):
    mids, rows = pieces[0]
    shape = (len(pieces), mids[0].shape[1], rows[0].shape[0])
    args = [v for mids, rows in pieces for v in (*mids, *rows)]
    return call(
        functools.partial(wgrad_stack_kernel, 1), sds(shape, BF), args, "wgrad_give",
        vmem=20,
    )


def wgrad_sum(pieces, gots, shares):
    mids, rows = pieces[0]
    size = mids[0].shape[1] // shares * rows[0].shape[0]
    shape = (shares, len(pieces), size // LANES, LANES)
    args = [v for mids, rows in pieces for v in (*mids, *rows)]
    return call(
        wgrad_sum_kernel, hbm(shape, BF), (*args, *gots), "wgrad_sum", vmem=28,
    )


def kv_sum_kernel(
    own_ref, got_ref, col_ref, dq_ref, n0_ref, n1_ref, wq_ref, wk_ref, wv_ref,
    gain_ref, gain_ffn_ref, rel_ref, dkv_ref, total_ref, give_ref, small_ref,
):
    inner = wk_ref.shape[0]
    width, block = n0_ref.shape
    dq = dq_ref[...]
    d_kv = (own_ref[...] + got_ref[: 2 * inner].astype(F32)).astype(BF)
    dkv_ref[...] = d_kv
    col = col_ref[...] + merge(got_ref[2 * inner : 2 * inner + 1], got_ref[2 * inner + 1 : 2 * inner + 2])
    far = dot_tn(wq_ref[...], dq[:, block:]) + dot_tn(wk_ref[...], d_kv[:inner, block:])
    far = far + dot_tn(wv_ref[...], d_kv[inner:, block:])
    give_ref[:width] = far.astype(BF)
    own = dot_tn(wq_ref[...], dq[:, :block]) + dot_tn(wk_ref[...], d_kv[:inner, :block])
    own = own + dot_tn(wv_ref[...], d_kv[inner:, :block])
    total_ref[...] = own
    gain = lane_sum(own * n0_ref[...].astype(F32) + far * n1_ref[...].astype(F32)) / gain_ref[...]
    small_ref[...] = jnp.zeros_like(small_ref)
    for first, row in ((2, gain), (8, gain_ffn_ref[...])):
        for at in range(0, width, block):
            size = min(block, width - at)
            line = first + at // block
            small_ref[line : line + 1, :size] = row[:, at : at + size]
    small_ref[1:2, : rel_ref.shape[1]] = rel_ref[...]
    small_ref[0:1] = col[:, block:]
    high, low = split(small_ref[...])
    give_ref[width : width + EXTRA] = high
    give_ref[width + EXTRA :] = low
    small_ref[...] = merge(high, low)
    small_ref[0:1] = col[:, :block]


def last_kernel(
    c_ref, own_ref, got_ref, small_ref, x_ref, inv_ref, gain_ref, dres_ref,
    keep_ref, give_ref, keep_small_ref, rows_ref,
):
    width = x_ref.shape[0]
    grad = own_ref[...] + got_ref[:width].astype(F32)
    small = small_ref[...] + merge(got_ref[width : width + EXTRA], got_ref[width + EXTRA :])
    x = x_ref[...].astype(F32)
    gain = column(gain_ref[...], x.shape[1])
    rows_ref[:width] = dres_ref[...] + rms_back(x, inv_ref[...], gain, grad)
    rows_ref[width:] = small
    rows = keep_ref.shape[1]
    mine = pl.ds(pl.multiple_of(c_ref[0] * rows, rows), rows)
    theirs = pl.ds(pl.multiple_of((1 - c_ref[0]) * rows, rows), rows)
    keep_ref[...] = rows_ref[:width, mine]
    give_ref[:width] = rows_ref[:width, theirs]
    keep_small_ref[:EXTRA] = small[:, :rows]
    keep_small_ref[EXTRA:] = small[:, rows:]
    give_ref[width:] = keep_small_ref[...]
    give_ref[width : width + 1] = rows_ref[width : width + 1, theirs]
    keep_small_ref[0:1] = rows_ref[width : width + 1, mine]


def out_rows_kernel(c_ref, res_ref, own_ref, ga_ref, gb_ref, gd_ref, keep_ref, give_ref, rows_ref):
    total = res_ref[...] + (
        own_ref[...].astype(F32)
        + ga_ref[...].astype(F32)
        + gb_ref[...].astype(F32)
        + gd_ref[...].astype(F32)
    )
    rows_ref[...] = total.astype(BF)
    rows = keep_ref.shape[1]
    keep_ref[...] = rows_ref[:, pl.ds(pl.multiple_of(c_ref[0] * rows, rows), rows)]
    give_ref[...] = rows_ref[:, pl.ds(pl.multiple_of((1 - c_ref[0]) * rows, rows), rows)]


def fold_core_kernel(
    c_ref, dq_ref, dkv_ref, n0_ref, n1_ref, go_ref, got_ref, keep_ref, give_ref
):
    inner = dq_ref.shape[0]
    block = n0_ref.shape[1]
    n0 = n0_ref[...]
    n1 = n1_ref[...]

    def gradient(rows):
        return dot_nt(rows[:, :block], n0) + dot_nt(rows[:, block:], n1)

    first = c_ref[0] == 0
    gq = gradient(dq_ref[...])
    gv = gradient(dkv_ref[inner:])
    keep_ref[0] = jnp.where(first, gq, gv)
    give_ref[0] = jnp.where(first, gv, gq).astype(BF)
    gk = gradient(dkv_ref[:inner])
    go = go_ref[...] + got_ref[...].astype(F32)
    keep_ref[1] = jnp.where(first, gk, go)
    give_ref[1] = jnp.where(first, go, gk).astype(BF)


def fold_x_kernel(x_ref, mine_ref, got_ref, keep_ref, give_ref):
    total = mine_ref[...] + got_ref[...].astype(F32)
    first = x_ref[0] == 0
    keep_ref[...] = jnp.where(first, total[0], total[1])
    give_ref[...] = jnp.where(first, total[1], total[0]).astype(BF)


def share_kernel(bit_ref, mine_ref, got_ref, own_ref, give_ref, sum_ref):
    sum_ref[...] = mine_ref[...] + got_ref[...].astype(F32)
    keep, give = halves(bit_ref, own_ref.shape[0])
    own_ref[...] = sum_ref[keep, :]
    give_ref[...] = sum_ref[give, :].astype(BF)


def lines(small, first, width):
    half = small.shape[0] // 2
    pieces = []
    for at in range(-(-width // (2 * LANES))):
        line = first + at
        pieces += [small[line : line + 1], small[half + line : half + line + 1]]
    return jnp.concatenate(pieces, axis=1)[:, :width]


def share_sum_kernel(mine_ref, got_ref, small_ref, small_got_ref, out_ref):
    rows, width = mine_ref.shape
    out_ref[:rows] = (mine_ref[...] + got_ref[...].astype(F32)).astype(BF)
    small = small_ref[...] + small_got_ref[...]
    rel = small[1:2]
    rel = jnp.concatenate([rel, small[EXTRA + 1 : EXTRA + 2]], axis=1)
    rel = jnp.concatenate([rel, jnp.zeros((1, width - rel.shape[1]), F32)], axis=1)
    three = jnp.concatenate(
        [lines(small, 2, width), lines(small, 8, width), rel, jnp.zeros((5, width), F32)], axis=0
    )
    out_ref[rows:] = jnp.concatenate(split(three), axis=0)


def share_join_kernel(z_ref, *refs):
    shares, (out_ref, hold_ref) = refs[:-2], refs[-2:]
    n = len(shares)
    rows = shares[0].shape[0] - EXTRA
    for k, ref in enumerate(shares):
        at = lax.rem(z_ref[0] + n - k, n)
        line, rest, size = 0, at, n
        while size > 1:
            size //= 2
            line = line + lax.rem(rest, 2) * size
            rest = rest // 2
        out_ref[pl.ds(pl.multiple_of(line * rows, rows), rows), :] = ref[:rows]
        hold_ref[at] = merge(ref[rows : rows + 8], ref[rows + 8 :])
    total = hold_ref[0]
    for k in range(1, n):
        total = total + hold_ref[k]
    out_ref[n * rows :] = jnp.concatenate(split(total), axis=0)


def join_x_kernel(x_ref, own_ref, got_ref, out_ref, small_ref):
    inner = out_ref.shape[1]
    first = x_ref[0] == 0
    own = own_ref[:inner]
    got = got_ref[:inner]
    out_ref[0] = jnp.where(first, own, got)
    out_ref[1] = jnp.where(first, got, own)
    small_ref[...] = merge(own_ref[inner : inner + 8], own_ref[inner + 8 :]) + merge(
        got_ref[inner : inner + 8], got_ref[inner + 8 :]
    )


def join_core_kernel(c_ref, own_ref, got_ref, *outs):
    first = c_ref[0] == 0
    own = own_ref[...]
    got = got_ref[...]
    pair = (jnp.where(first, own, got), jnp.where(first, got, own))
    for at, out in enumerate(outs):
        out[...] = pair[at // 2][at % 2].astype(F32)


def place_kernel(c_ref, own_ref, got_ref, out_ref):
    out_ref[c_ref[0]] = own_ref[...]
    out_ref[1 - c_ref[0]] = got_ref[: own_ref.shape[0]]


def widen_kernel(src, *outs):
    for at, out in enumerate(outs):
        for lanes, (lines, places) in packing(*out.shape):
            piece = src[0, at, lines].astype(F32)
            lane = 0
            for first, size in places:
                wide = lanes.stop - lanes.start
                out[first : first + size, lanes] = piece[:, lane : lane + wide]
                lane += wide


def widen(v, rows, width):
    n, pieces, lines, _ = v.shape
    outs = pl.pallas_call(
        widen_kernel,
        out_shape=[sds((n * rows, width), F32)] * pieces,
        grid=(n,),
        in_specs=[pl.BlockSpec((1, pieces, lines, LANES), lambda i: (i, 0, 0, 0))],
        out_specs=[pl.BlockSpec((rows, width), lambda i: (i, 0))] * pieces,
        compiler_params=pltpu.CompilerParams(vmem_limit_bytes=32 << 20),
        cost_estimate=cost(500),
        name="widen",
    )(in_hbm(Order.follow(v)))
    return Order.done(outs)


def per_device(*args):
    Order.last = None
    return run(*args)


def run(
    inputs,
    lengths,
    delete_mask,
    buckets,
    gain_attn,
    w_query,
    w_key,
    w_value,
    w_out,
    rel_bias,
    gain_ffn,
    gate_weight,
    up_weight,
    down_weight,
    cotangent,
):
    seqs, row_count, width = inputs.shape
    dp_axis = lax.axis_size("dp")
    heads_axis = lax.axis_size("head")
    hid_axis = lax.axis_size("hid")
    assert seqs == 2 and heads_axis == 2 and hid_axis == 4
    z_at = lax.axis_index("dp")
    h_at = lax.axis_index("head")
    hid_at = lax.axis_index("hid")
    c_at = hid_at % 2
    x_at = hid_at // 2
    length = row_count * heads_axis * hid_axis
    block = 2 * row_count
    inner = w_query.shape[1]
    heads = inner // DH
    hidden = gate_weight.shape[1]
    bucket_count, total_heads = rel_bias.shape
    c_scalar = c_at.astype(jnp.int32).reshape(1)
    x_scalar = x_at.astype(jnp.int32).reshape(1)
    z_scalar = z_at.astype(jnp.int32).reshape(1)

    def core_swap(v, name):
        return move(v, "hid", [(i, i ^ 1) for i in range(hid_axis)], name)

    def x_swap(v, name):
        return move(v, "hid", [(i, i ^ 2) for i in range(hid_axis)], name)

    def y_swap(v, name):
        return move(v, "head", [(0, 1), (1, 0)], name)

    def grid_swap(v, relayed, name):
        pairs = []
        for h in range(heads_axis):
            for i in range(hid_axis):
                along_x = not relayed or i % 2 == 1
                along_y = not relayed or i % 2 == 0
                to = ((1 - h) if along_y else h) * hid_axis + ((i ^ 2) if along_x else i)
                pairs.append((h * hid_axis + i, to))
        return move(v, ("head", "hid"), pairs, name)

    def relay(from_x, from_y, name):
        picked = call(
            pick_kernel, sds(from_x.shape, BF), (from_x, from_y), "pick", scalars=(c_scalar,),
        )
        return grid_swap(picked, True, name)

    def stack(a, b):
        return jnp.concatenate([a, b], axis=0)

    def place(own, got):
        shape = sds((2, *own.shape), own.dtype)
        return call(place_kernel, shape, (own, got), "place", scalars=(c_scalar,), us=100)

    def after(v, *earlier):
        return lax.optimization_barrier((v, *earlier))[0]

    x_in = jnp.swapaxes(inputs, 1, 2)
    dy_in = jnp.swapaxes(cotangent, 1, 2)
    wq, wk, wv = w_query.T, w_key.T, w_value.T
    gate_w, up_w = gate_weight.T, up_weight.T
    gain_one = gain_attn.reshape(1, width)
    gain_two = gain_ffn.reshape(1, width)

    w_half = w_out.reshape(2, inner // 2, width)
    w_half = lax.dynamic_index_in_dim(w_half, c_at, 0, keepdims=False)
    x_rows, normed_one, inv_one = call(
        prep_kernel,
        (sds((width, block), BF), sds((width, block), BF), sds((1, block), F32)),
        (in_hbm(x_in), core_swap(x_in, "x_core"), gain_one),
        "prep",
        vmem=20,
        scalars=(c_scalar,),
    )
    normed_far_raw = y_swap(normed_one, "n1_y")

    dy_own = call(
        pair_kernel,
        sds((width, block), BF),
        (in_hbm(dy_in), in_hbm(core_swap(dy_in, "dy_core"))),
        "pair",
        vmem=16,
        scalars=(c_scalar,),
    )

    gate_other = core_swap(gate_w, "gate_core")
    up_other = core_swap(up_w, "up_core")
    down_other = core_swap(down_weight, "down_core")
    ffn_weights = (gate_w, gate_other, up_w, up_other, down_weight, down_other)
    def project(n):
        return call(
            qkv_kernel,
            (sds((inner, block), BF), sds((2 * inner, block), BF)),
            (n, wq, wk, wv),
            "qkv",
        )

    q_own, kv_own = project(normed_one)
    base = jnp.stack(
        [(h * 2 + x) * block for x in (x_at, 1 - x_at) for h in (h_at, 1 - h_at)]
    ).astype(jnp.int32)
    starts = (length - block - (base[:, None] - base[None, :2])).reshape(-1).astype(jnp.int32)
    bucket_rev = jnp.concatenate([jnp.full((1,), -1, jnp.int32), buckets[::-1]])
    hot = bucket_rev[None, :] == jnp.arange(bucket_count, dtype=jnp.int32)[:, None]
    local_bias = lax.dynamic_slice_in_dim(rel_bias, h_at * heads, heads, 1)
    table = jnp.sum(jnp.where(hot[None], local_bias.T[:, :, None], 0.0), axis=1)
    table = jnp.concatenate([table, jnp.zeros((8 - heads, 2 * length), F32)], axis=0)
    seq_mask = lax.dynamic_index_in_dim(delete_mask, c_at, 0, keepdims=False)
    seq_len = lax.dynamic_index_in_dim(lengths, c_at, 0, keepdims=False)
    seq_mask = jnp.where(jnp.arange(length, dtype=jnp.int32) < seq_len, seq_mask, NEG)
    seq_mask = seq_mask.reshape(2, 2, block)
    seq_mask = jnp.where(h_at == 0, seq_mask, seq_mask[::-1])
    seq_mask = jnp.where(x_at == 0, seq_mask, seq_mask[:, ::-1])
    seq_mask = jnp.swapaxes(seq_mask, 0, 1).reshape(1, length)
    seq_mask = after(seq_mask, gate_other, up_other)
    bias = make_bias(starts, table, seq_mask, heads, block, 4, 2)

    kv_own_x = x_swap(kv_own, "kv_own_x")
    normed_far_raw = after(normed_far_raw, bias, kv_own)
    normed_far = after(normed_far_raw, down_other, kv_own_x)
    w_half = y_swap(after(w_half, normed_far_raw), "wout_y")
    dy_y = y_swap(after(dy_own, w_half), "dy_y")
    w_half_got = core_swap(w_half, "wout_core")
    q_far, kv_far = project(normed_far)
    kv_far_x = x_swap(kv_far, "kv_far_x")
    dy_x = x_swap(after(dy_own, kv_far_x), "dy_x")
    queries = jnp.concatenate([q_own, q_far], axis=1)
    kvs = (kv_own, kv_far, kv_own_x, kv_far_x)

    probs, mixed = attn_fwd(queries, kvs, bias, heads, block)
    mixed_far = y_swap(mixed[:, block:], "mixed_y")
    mixed_far = after(mixed_far, dy_x, dy_y)
    mixed_own = mixed[:, :block]
    residual, normed_two, inv_two = call(
        mid_kernel,
        (hbm((width, block), F32), sds((width, block), BF), sds((1, block), F32)),
        (x_rows, mixed_own, mixed_far, w_out, w_half, w_half_got, gain_two),
        "mid",
        vmem=20,
        scalars=(c_scalar,),
    )

    n_x = x_swap(normed_two, "n2_x")
    n_y = y_swap(normed_two, "n2_y")
    dy_d = relay(dy_x, dy_y, "dy_d")
    def d_act_of(dy):
        shape = sds((2, hidden, block), F32)
        return call(d_act_kernel, shape, (dy, down_weight, down_other), "d_act")

    da_own = d_act_of(dy_own)
    act_o, dg_o, du_o, dn_o = ffn_chunk(normed_two, da_own, ffn_weights, BF)
    da_x = d_act_of(dy_x)
    da_y = d_act_of(dy_y)
    n_d = relay(n_x, n_y, "n2_d")
    act_x, dg_x, du_x, dn_x = ffn_chunk(n_x, da_x, ffn_weights, BF)
    got_x = x_swap(dn_x, "dn_x")
    act_y, dg_y, du_y, dn_y = ffn_chunk(n_y, da_y, ffn_weights, BF)
    got_y = y_swap(dn_y, "dn_y")
    act_d, dg_d, du_d, dn_d = ffn_chunk(n_d, d_act_of(dy_d), ffn_weights, BF)
    got_d = grid_swap(dn_d, False, "dn_d")

    n_all = (normed_two, n_x, n_y, n_d)
    dy_all = (dy_own, dy_x, dy_y, dy_d)
    pieces = (
        ((act_o, act_x, act_y, act_d), dy_all),
        ((dg_o, dg_x, dg_y, dg_d), n_all),
        ((du_o, du_x, du_y, du_d), n_all),
    )
    given_d = core_swap(wgrad_give(pieces[:1]), "wgrad_core")
    out_o = ffn_out(act_o, down_weight, down_other, BF)
    mids, rows = pieces[1]
    gated = (((after(mids[0], got_x, got_y), *mids[1:]), rows), pieces[2])
    given_gu = core_swap(wgrad_give(gated), "wgrad_core")
    part_x = ffn_out(act_x, down_weight, down_other, BF)
    part_y = ffn_out(act_y, down_weight, down_other, BF)
    part_d = ffn_out(act_d, down_weight, down_other, BF)
    shares = dp_axis if dp_axis <= 8 else 1
    ffn_grads = wgrad_sum(pieces, (given_d, given_gu), shares)
    if shares > 1:
        ffn_grads = lax.psum_scatter(ffn_grads, "dp", scatter_dimension=0, tiled=True)
    else:
        ffn_grads = lax.psum(ffn_grads, "dp")


    d_residual, d_branch, gain_ffn_part, d_mixed_own, d_mixed_give = call(
        mid_back_kernel,
        (
            hbm((width, block), F32),
            sds((width, block), BF),
            sds((1, width), F32),
            sds((inner, block), BF),
            sds((inner, block), BF),
        ),
        (*map(in_hbm, (dn_o, got_x, got_y, got_d, dy_own, residual)), inv_two, gain_two, w_out, w_half, w_half_got),
        "mid_back",
        vmem=24,
        scalars=(c_scalar,),
    )
    d_mixed = jnp.concatenate([d_mixed_own, y_swap(d_mixed_give, "dmixed_y")], axis=1)

    dq, dkv_own, dkv_give, col, table_grad = attn_bwd(
        starts, probs, queries, d_mixed, kvs, heads, block
    )
    dkv_got = x_swap(dkv_give, "dkv_x")
    out_x = in_hbm(x_swap(after(part_x, got_d), "out_x"))
    out_y = in_hbm(y_swap(after(part_y, got_d), "out_y"))
    d_branch = after(d_branch, dq)
    grad_out_own, grad_out_give = call(
        out_grad_kernel,
        (hbm((inner, width), F32), hbm((inner, width), BF)),
        (mixed_own, mixed_far, d_branch),
        "out_grad",
        vmem=20,
    )
    grad_out_got = y_swap(grad_out_give, "gout_y")
    dkv_got = after(dkv_got, out_x, out_y)
    table_grad = sum(jnp.roll(table_grad[:, i], -i, axis=1) for i in range(8))
    grad_rel = jnp.sum(jnp.where(hot[None], table_grad[:, None, :], 0.0), axis=2).T
    grad_rel = lax.dynamic_update_slice_in_dim(
        jnp.zeros((bucket_count, total_heads), F32), grad_rel, h_at * heads, 1
    )
    d_kv, back_own, back_give, small = call(
        kv_sum_kernel,
        (
            sds((2 * inner, 2 * block), BF),
            hbm((width, block), F32),
            hbm((width + 2 * EXTRA, block), BF),
            sds((EXTRA, block), F32),
        ),
        (
            *map(in_hbm, (dkv_own, dkv_got)), col,
            dq, *map(in_hbm, (normed_one, normed_far)), wq, wk, wv,
            gain_one, gain_ffn_part, grad_rel.reshape(1, -1),
        ),
        "kv_sum",
        vmem=24,
    )
    back_got = y_swap(back_give, "back_y")

    pair_f32, pair_bf = sds((2, inner, width), F32), sds((2, inner, width), BF)
    one_f32, one_bf = sds((inner, width), F32), sds((inner, width), BF)
    keep, give = call(
        fold_core_kernel,
        (hbm(pair_f32.shape, F32), hbm(pair_bf.shape, BF)),
        (dq, d_kv, *map(in_hbm, (normed_one, normed_far, grad_out_own, grad_out_got))),
        "fold_core",
        scalars=(c_scalar,),
        vmem=28,
    )
    keep, give = call(
        fold_x_kernel,
        (one_f32, one_bf),
        (in_hbm(keep), in_hbm(core_swap(give, "fold_core"))),
        "fold_x",
        vmem=20,
        scalars=(x_scalar,),
    )
    got = x_swap(give, "fold_x")
    steps = [1 << k for k in range(dp_axis.bit_length() - 1)]
    short = shares > 1 and 1 << len(steps) == dp_axis
    if short:
        keep, got = z_share(keep, got, steps[0], dp_axis, z_at)
    rows_keep, rows_give, small, _ = call(
        last_kernel,
        (
            sds((width, row_count), F32),
            sds((width + 2 * EXTRA, row_count), F32),
            sds((2 * EXTRA, row_count), F32),
            sds((width + EXTRA, block), F32),
        ),
        (in_hbm(back_own), in_hbm(back_got), small, in_hbm(x_rows), inv_one, gain_one, in_hbm(d_residual)),
        "last",
        vmem=24,
        scalars=(c_scalar,),
    )
    rows_got = core_swap(rows_give, "grad_core")
    small_got = rows_got[width:]
    if shares > 1:
        ffn_grads = lax.all_gather(after(ffn_grads, rows_keep), "dp", axis=0, tiled=True)
    if short:
        for step in steps[1:]:
            keep, got = z_share(keep, got, step, dp_axis, z_at)
        folded = z_join(keep, got, small, small_got, dp_axis, z_scalar)
    else:
        folded = z_psum(keep, got, small, small_got)

    part_d = after(part_d, rows_keep)
    out_d = grid_swap(part_d, False, "out_d")
    out_keep, out_give, _ = call(
        out_rows_kernel,
        (
            sds((width, row_count), BF),
            sds((width, row_count), BF),
            sds((width, block), BF),
        ),
        tuple(map(in_hbm, (residual, out_o, out_x, out_y, out_d))),
        "out_rows",
        vmem=24,
        scalars=(c_scalar,),
    )

    joined = x_swap(folded, "join_x")
    grad_inputs = place(rows_keep, rows_got)
    folded, sums = call(
        join_x_kernel,
        (pair_bf, sds((8, width), F32)),
        (folded, joined),
        "join_x",
        scalars=(x_scalar,),
    )
    joined = core_swap(folded, "join_core")
    output = place(out_keep, core_swap(out_give, "out_core"))
    grad_w_query, grad_w_key, grad_w_value, grad_w_out = call(
        join_core_kernel,
        (one_f32,) * 4,
        (folded, joined),
        "join_core",
        scalars=(c_scalar,),
    )
    mask_keep, mask_got = small[:1], small_got[:1]
    grad_mask = jnp.where(c_at == 0, stack(mask_keep, mask_got), stack(mask_got, mask_keep))
    grad_down, grad_gate, grad_up = widen(ffn_grads, hidden // shares, width)
    return (
        jnp.swapaxes(output, 1, 2),
        jnp.swapaxes(grad_inputs, 1, 2),
        grad_mask,
        sums[0],
        grad_w_query.T,
        grad_w_key.T,
        grad_w_value.T,
        grad_w_out,
        sums[2, : bucket_count * total_heads].reshape(bucket_count, total_heads),
        sums[1],
        grad_gate.T,
        grad_up.T,
        grad_down,
    )


def z_swap(v, step, n, name):
    return move(v, "dp", [(i, i ^ step) for i in range(n)], name)


def z_share(mine, got, step, n, z_at):
    bit = ((z_at // step) % 2).astype(jnp.int32).reshape(1)
    rows, width = mine.shape
    half = (rows // 2, width)
    mine, give, _ = call(
        share_kernel,
        (sds(half, F32), sds(half, BF), sds((rows, width), F32)),
        (mine, got),
        "share",
        scalars=(bit,),
    )
    return mine, z_swap(give, step, n, "share_z")


def z_join(mine, got, small, small_got, n, z_scalar):
    rows, width = mine.shape
    total = call(
        share_sum_kernel,
        sds((rows + EXTRA, width), BF),
        (mine, got, small, small_got),
        "share_sum",
    )
    gots = [
        move(total, "dp", [(i, (i + k) % n) for i in range(n)], "join_z") for k in range(1, n)
    ]
    joined, _ = call(
        share_join_kernel,
        (sds((n * rows + EXTRA, width), BF), sds((n, 8, width), F32)),
        (total, *gots),
        "share_join",
        scalars=(z_scalar,),
    )
    return joined


def z_psum(mine, got, small, small_got):
    width = mine.shape[1]
    total = lax.psum((mine + got.astype(F32)).astype(BF), "dp")
    small = lax.psum(small + small_got, "dp")
    half = small.shape[0] // 2

    def row(first):
        both = jnp.concatenate([small[first:half], small[half + first :]], axis=1)
        return both.reshape(1, -1)[:, :width]

    three = jnp.concatenate([row(2), row(8), row(1), jnp.zeros((5, width), F32)], axis=0)
    return jnp.concatenate([total, *split(three)], axis=0)


def solution(mesh):
    rows = P("dp", ("head", "hid"), None)
    return jax.shard_map(
        per_device,
        mesh=mesh,
        in_specs=(
            rows,
            P("dp"),
            P("dp", None),
            P(),
            P(),
            P(None, "head"),
            P(None, "head"),
            P(None, "head"),
            P("head", None),
            P(),
            P(),
            P(None, ("head", "hid")),
            P(None, ("head", "hid")),
            P(("head", "hid"), None),
            rows,
        ),
        out_specs=(
            rows,
            rows,
            P("dp", ("head", "hid")),
            P(),
            P(None, "head"),
            P(None, "head"),
            P(None, "head"),
            P("head", None),
            P(),
            P(),
            P(None, ("head", "hid")),
            P(None, ("head", "hid")),
            P(("head", "hid"), None),
        ),
        check_vma=False,
    )
```

```python
import functools

import jax
import jax.numpy as jnp
from jax import lax
from jax.experimental import pallas as pl
from jax.experimental.pallas import tpu as pltpu
from jax.sharding import PartitionSpec as P


DH = 64
EPS = 1e-06
NEG = -1e30
BF = jnp.bfloat16
F32 = jnp.float32
GELU_C = 0.7978845608028654
GELU_K = 0.044715
LANES = 128
EXTRA = 16


def cost(us):
    return pl.CostEstimate(flops=0, bytes_accessed=int(us * 3.0e6), transcendentals=0)


NT = (((1,), (1,)), ((), ()))
TN = (((0,), (0,)), ((), ()))


def dot(a, b):
    return jnp.dot(a, b, preferred_element_type=F32)


def dot_nt(a, b):
    return lax.dot_general(a, b, NT, preferred_element_type=F32)


def dot_tn(a, b):
    return lax.dot_general(a, b, TN, preferred_element_type=F32)


def sds(shape, dtype):
    return jax.ShapeDtypeStruct(shape, dtype)


class Order:
    last = None

    @classmethod
    def follow(cls, v):
        return v if cls.last is None else lax.optimization_barrier((v, cls.last))[0]

    @classmethod
    def done(cls, outs):
        cls.last = min(jax.tree.leaves(outs), key=lambda v: v.size)
        return outs


def call(kernel, out_shape, args, name, scalars=(), vmem=12, us=0.01, **kw):
    args = (Order.follow(args[0]), *args[1:])
    in_specs = [pl.BlockSpec(memory_space=pltpu.SMEM)] * len(scalars)
    in_specs += [pl.BlockSpec(memory_space=pltpu.VMEM)] * len(args)
    outs = pl.pallas_call(
        kernel,
        out_shape=out_shape,
        in_specs=in_specs,
        out_specs=jax.tree.map(lambda _: pl.BlockSpec(memory_space=pltpu.VMEM), out_shape),
        compiler_params=pltpu.CompilerParams(vmem_limit_bytes=vmem << 20),
        cost_estimate=cost(us),
        name=name,
        **kw,
    )(*scalars, *args)
    return Order.done(outs)


def hbm(shape, dtype):
    return pltpu.HBM(shape, dtype)


def in_hbm(v):
    return pltpu.with_memory_space_constraint(v, pltpu.HBM)


def move(v, axes, pairs, name):
    with jax.named_scope(name):
        return lax.ppermute(v, axes, pairs)


def lane_sum(v):
    total = v[:, :LANES]
    for at in range(LANES, v.shape[1], LANES):
        total = total + v[:, at : at + LANES]
    return jnp.sum(total.T, axis=0, keepdims=True)


def column(row, width):
    wide = jnp.broadcast_to(row, (LANES, row.shape[1])).T
    return jnp.concatenate([wide] * (width // LANES), axis=1)


def pair_rows(c, own_ref, far_ref):
    own = own_ref[c]
    far = far_ref[c]
    first = c == 0
    return jnp.concatenate([jnp.where(first, own, far), jnp.where(first, far, own)], axis=1)


def pick_kernel(c_ref, first_ref, second_ref, out_ref):
    out_ref[...] = jnp.where(c_ref[0] == 0, first_ref[...], second_ref[...])


def pair_kernel(c_ref, own_ref, far_ref, out_ref):
    out_ref[...] = pair_rows(c_ref[0], own_ref, far_ref)


def prep_kernel(c_ref, own_ref, far_ref, gain_ref, x_ref, n_ref, inv_ref):
    rows = pair_rows(c_ref[0], own_ref, far_ref)
    x_ref[...] = rows
    x = rows.astype(F32)
    inverse = lax.rsqrt(jnp.mean(x * x, axis=0, keepdims=True) + EPS)
    inv_ref[...] = inverse
    n_ref[...] = (x * inverse * column(gain_ref[...], x.shape[1])).astype(BF)


def qkv_kernel(n_ref, wq_ref, wk_ref, wv_ref, q_ref, kv_ref):
    n = n_ref[...]
    inner = wq_ref.shape[0]
    q_ref[...] = dot(wq_ref[...], n).astype(BF)
    kv_ref[:inner] = dot(wk_ref[...], n).astype(BF)
    kv_ref[inner:] = dot(wv_ref[...], n).astype(BF)


def bias_kernel(start_ref, table_ref, mask_ref, out_ref, *, heads, block, q_blocks):
    kb = pl.program_id(0)
    qb = pl.program_id(1)
    start = pl.multiple_of(start_ref[kb * q_blocks + qb], block)
    k_at = pl.multiple_of(kb * block, block)
    mask = column(mask_ref[:, pl.ds(k_at, block)], block)
    for h in range(heads):
        window = table_ref[h : h + 1, pl.ds(start, 2 * block)]
        window = jnp.broadcast_to(window, (block, 2 * block))
        rolled = pltpu.roll(window, block, 1, stride=1, stride_axis=0)
        out_ref[h] = rolled[:, :block] + mask


def make_bias(starts, table, mask_row, heads, block, k_blocks, q_blocks):
    length = k_blocks * block
    outs = pl.pallas_call(
        functools.partial(bias_kernel, heads=heads, block=block, q_blocks=q_blocks),
        out_shape=pltpu.HBM((heads, length, q_blocks * block), F32),
        grid_spec=pltpu.PrefetchScalarGridSpec(
            num_scalar_prefetch=1,
            grid=(k_blocks, q_blocks),
            in_specs=[
                pl.BlockSpec(table.shape, lambda k, q, s: (0, 0)),
                pl.BlockSpec((1, length), lambda k, q, s: (0, 0)),
            ],
            out_specs=pl.BlockSpec((heads, block, block), lambda k, q, s: (0, k, q)),
        ),
        compiler_params=pltpu.CompilerParams(vmem_limit_bytes=16 << 20),
        cost_estimate=cost(0.01),
        name="bias",
    )(starts, table, Order.follow(mask_row))
    return Order.done(outs)


def attn_fwd_kernel(q_ref, k0, k1, k2, k3, bias_ref, p_ref, o_ref, *, inner):
    h = pl.program_id(1)
    at_k = pl.ds(pl.multiple_of(h * DH, DH), DH)
    at_v = pl.ds(pl.multiple_of(inner + h * DH, DH), DH)
    q = q_ref[...]
    parts = [dot_tn(ref[at_k, :], q) for ref in (k0, k1, k2, k3)]
    s = jnp.concatenate(parts, axis=0) + bias_ref[0]
    top = jnp.max(s, axis=0, keepdims=True)
    e = jnp.exp(s - top)
    total = jnp.sum(e, axis=0, keepdims=True)
    p = e * (1.0 / total)
    p_ref[0] = p
    pb = p.astype(BF)
    values = jnp.concatenate([ref[at_v, :] for ref in (k0, k1, k2, k3)], axis=1)
    o_ref[...] = dot(values, pb).astype(BF)


def attn_fwd(q, kvs, bias, heads, block):
    inner, rows = q.shape
    length = bias.shape[1]
    full = lambda i, h: (0, 0)
    slab = pl.BlockSpec((1, length, block), lambda i, h: (h, 0, i))
    head = pl.BlockSpec((DH, block), lambda i, h: (h, i))
    outs = pl.pallas_call(
        functools.partial(attn_fwd_kernel, inner=inner),
        out_shape=(pltpu.HBM((heads, length, rows), F32), sds((inner, rows), BF)),
        grid=(rows // block, heads),
        in_specs=[head] + [pl.BlockSpec(kv.shape, full) for kv in kvs] + [slab],
        out_specs=(slab, head),
        compiler_params=pltpu.CompilerParams(vmem_limit_bytes=14 << 20),
        cost_estimate=cost(0.01),
        name="attn_fwd",
    )(Order.follow(q), *kvs, in_hbm(bias))
    return Order.done(outs)


def diagonals(piece, block):
    total = None
    for shift in range(0, LANES, 8):
        wide = None
        for part in range(block // LANES):
            rows = piece[part * LANES + shift : part * LANES + shift + 8]
            pieces = [jnp.zeros((8, block - part * LANES), F32), rows]
            if part:
                pieces.append(jnp.zeros((8, part * LANES), F32))
            rows = jnp.concatenate(pieces, axis=1)
            wide = rows if wide is None else wide + rows
        if shift:
            wide = pltpu.roll(wide, 2 * block - shift, 1)
        total = wide if total is None else total + wide
    return total


def attn_bwd_kernel(
    start_ref, p_ref, q_ref, do_ref, k0, k1, k2, k3, dq_ref, own_ref, give_ref, col_ref, table_ref,
    acc, col_acc, *, inner, heads, block, q_blocks,
):
    qb = pl.program_id(0)
    h = pl.program_id(1)
    kvs = (k0, k1, k2, k3)
    at_k = pl.ds(pl.multiple_of(h * DH, DH), DH)
    at_v = pl.ds(pl.multiple_of(inner + h * DH, DH), DH)
    half = len(kvs) * block // 2

    @pl.when((qb == 0) & (h == 0))
    def _():
        acc[...] = jnp.zeros_like(acc)
        col_acc[...] = jnp.zeros_like(col_acc)
        table_ref[...] = jnp.zeros_like(table_ref)

    q = q_ref[...]
    do = do_ref[...]
    dp = jnp.concatenate([dot_tn(ref[at_v, :], do) for ref in kvs], axis=0)
    p = p_ref[0]
    inside = jnp.sum(p * dp, axis=0, keepdims=True)
    ds = p * (dp - inside)
    col_acc[...] += ds
    for kb in range(len(kvs)):
        start = pl.multiple_of(start_ref[kb * q_blocks + qb], block)
        piece = ds[kb * block : (kb + 1) * block]
        table_ref[h, :, pl.ds(start, 2 * block)] += diagonals(piece, block)
    dsb = ds.astype(BF)
    pb = p.astype(BF)
    acc[at_k, :] += dot_nt(q, dsb)
    acc[at_v, :] += dot_nt(do, pb)
    keys = jnp.concatenate([ref[at_k, :] for ref in kvs], axis=1)
    dq_ref[...] = dot(keys, dsb).astype(BF)

    @pl.when((qb == q_blocks - 1) & (h == heads - 1))
    def _():
        own_ref[...] = acc[:, :half]
        col = lane_sum(col_acc[...])
        col_ref[...] = col[:, :half]
        give_ref[: 2 * inner] = acc[:, half:].astype(BF)
        give_ref[2 * inner :] = split_rows(col[:, half:])


def split(v):
    high = v.astype(BF)
    return high, (v - high.astype(F32)).astype(BF)


def merge(high, low):
    return high.astype(F32) + low.astype(F32)


def split_rows(row):
    high = row.astype(BF)
    low = (row - high.astype(F32)).astype(BF)
    at = lax.broadcasted_iota(jnp.int32, (EXTRA, row.shape[1]), 0)
    wide = jnp.where(at == 0, high.astype(F32), jnp.where(at == 1, low.astype(F32), 0.0))
    return wide.astype(BF)


def attn_bwd(starts, p, q, do, kvs, heads, block):
    inner, rows = q.shape
    length = p.shape[1]
    half = length // 2
    q_blocks = rows // block
    full = lambda i, h, s: (0, 0)
    head = pl.BlockSpec((DH, block), lambda i, h, s: (h, i))
    outs = pl.pallas_call(
        functools.partial(
            attn_bwd_kernel, inner=inner, heads=heads, block=block, q_blocks=q_blocks
        ),
        out_shape=(
            sds((inner, rows), BF),
            hbm((2 * inner, half), F32),
            hbm((2 * inner + EXTRA, half), BF),
            sds((1, half), F32),
            sds((heads, 8, 2 * length), F32),
        ),
        grid_spec=pltpu.PrefetchScalarGridSpec(
            num_scalar_prefetch=1,
            grid=(q_blocks, heads),
            in_specs=[pl.BlockSpec((1, length, block), lambda i, h, s: (h, 0, i)), head, head]
            + [pl.BlockSpec(kv.shape, full) for kv in kvs],
            out_specs=(
                head,
                pl.BlockSpec((2 * inner, half), full),
                pl.BlockSpec((2 * inner + EXTRA, half), full),
                pl.BlockSpec((1, half), full),
                pl.BlockSpec((heads, 8, 2 * length), lambda i, h, s: (0, 0, 0)),
            ),
            scratch_shapes=[
                pltpu.VMEM((2 * inner, length), F32),
                pltpu.VMEM((length, block), F32),
            ],
        ),
        compiler_params=pltpu.CompilerParams(vmem_limit_bytes=28 << 20),
        cost_estimate=cost(500),
        name="attn_bwd",
    )(starts, in_hbm(p), Order.follow(q), do, *kvs)
    return Order.done(outs)


def halves(c_ref, half):
    return [pl.ds(pl.multiple_of(at * half, half), half) for at in (c_ref[0], 1 - c_ref[0])]


def mid_kernel(
    c_ref, x_ref, m0_ref, m1_ref, w0_ref, w1_ref, w2_ref, gain_ref, res_ref, n_ref, inv_ref
):
    attended = dot_tn(w0_ref[...], m0_ref[...])
    for at, w_ref in zip(halves(c_ref, w1_ref.shape[0]), (w1_ref, w2_ref)):
        attended = attended + dot_tn(w_ref[...], m1_ref[at, :])
    res = x_ref[...].astype(F32) + attended
    res_ref[...] = res
    inverse = lax.rsqrt(jnp.mean(res * res, axis=0, keepdims=True) + EPS)
    inv_ref[...] = inverse
    n_ref[...] = (res * inverse * column(gain_ref[...], res.shape[1])).astype(BF)


def rms_back(rows, inverse, gain, grad):
    scaled = grad * gain
    inside = jnp.mean(rows * scaled, axis=0, keepdims=True)
    return inverse * scaled - rows * (inverse * inverse * inverse * inside)


def mid_back_kernel(
    c_ref, own_ref, ga_ref, gb_ref, gd_ref, dy_ref, res_ref, inv_ref, gain_ref, w0_ref, w1_ref, w2_ref,
    dres_ref, branch_ref, gain_grad_ref, dm0_ref, dm1_ref,
):
    grad = own_ref[...].astype(F32) + ga_ref[...].astype(F32) + gb_ref[...].astype(F32)
    grad = grad + gd_ref[...].astype(F32)
    res = res_ref[...]
    inverse = inv_ref[...]
    gain_grad_ref[...] = lane_sum(grad * (res * inverse))
    gain = column(gain_ref[...], res.shape[1])
    d_res = dy_ref[...].astype(F32) + rms_back(res, inverse, gain, grad)
    dres_ref[...] = d_res
    branch = d_res.astype(BF)
    branch_ref[...] = branch
    dm0_ref[...] = dot(w0_ref[...], branch).astype(BF)
    for at, w_ref in zip(halves(c_ref, w1_ref.shape[0]), (w1_ref, w2_ref)):
        dm1_ref[at, :] = dot(w_ref[...], branch).astype(BF)


def out_grad_kernel(m0_ref, m1_ref, branch_ref, own_ref, far_ref):
    branch = branch_ref[...]
    own_ref[...] = dot_nt(m0_ref[...], branch)
    far_ref[...] = dot_nt(m1_ref[...], branch).astype(BF)


def d_act_kernel(dy_ref, d0, d1, out_ref):
    dy = dy_ref[...]
    for part, w_ref in enumerate((d0, d1)):
        out_ref[part] = dot(w_ref[...], dy)


def ffn_kernel(n_ref, da_ref, g0, g1, u0, u1, a_ref, dg_ref, du_ref, dn_ref):
    n = n_ref[...]
    total = None
    for part, (g_w, u_w) in enumerate(((g0, u0), (g1, u1))):
        gate = dot(g_w[...], n)
        up = dot(u_w[...], n)
        d_act = da_ref[part]
        square = gate * gate
        t = jnp.tanh(gate * (GELU_C + (GELU_C * GELU_K) * square))
        half = 0.5 + 0.5 * t
        gelu = gate * half
        slope = half + gelu * (1.0 - t) * (GELU_C + (3.0 * GELU_C * GELU_K) * square)
        a_ref[part] = (gelu * up).astype(BF)
        d_gate = (d_act * up * slope).astype(BF)
        d_up = (d_act * gelu).astype(BF)
        dg_ref[part] = d_gate
        du_ref[part] = d_up
        more = dot_tn(g_w[...], d_gate) + dot_tn(u_w[...], d_up)
        total = more if total is None else total + more
    dn_ref[...] = total.astype(dn_ref.dtype)


def ffn_chunk(n, d_act, weights, out_dtype):
    width, rows = n.shape
    hidden = weights[0].shape[0]
    mid = sds((2, hidden, rows), BF)
    return call(
        ffn_kernel,
        (mid, mid, mid, sds((width, rows), out_dtype)),
        (n, d_act, *weights[:4]),
        "ffn",
        vmem=20,
    )


def ffn_out_kernel(a_ref, d0, d1, o_ref):
    total = dot_tn(d0[...], a_ref[0]) + dot_tn(d1[...], a_ref[1])
    o_ref[...] = total.astype(o_ref.dtype)


def ffn_out(act, d0, d1, dtype):
    _, hidden, rows = act.shape
    width = d0.shape[1]
    return call(
        ffn_out_kernel, hbm((width, rows), dtype), (act, d0, d1), "ffn_out", vmem=16,
    )


def mids_shape(refs):
    return refs[0].shape[1], refs[4].shape[0]


def packing(rows, width):
    full, rest = divmod(width, LANES)
    assert 2 * rest == LANES and rows % 16 == 0
    half = rows // 2
    plan = []
    for at in range(full):
        lanes = slice(at * LANES, (at + 1) * LANES)
        plan.append((lanes, (slice(at * rows, (at + 1) * rows), ((0, rows),))))
    lanes = slice(full * LANES, width)
    plan.append((lanes, (slice(full * rows, full * rows + half), ((0, half), (half, half)))))
    return plan


def wgrad_sum_kernel(*refs):
    out_ref = refs[-1]
    n, pieces = out_ref.shape[:2]
    hidden, width = mids_shape(refs)
    rows = hidden // n
    gots = [(ref, at) for ref in refs[8 * pieces : -1] for at in range(ref.shape[0])]
    for at in range(pieces):
        mids, blocks = refs[8 * at : 8 * at + 4], refs[8 * at + 4 : 8 * at + 8]
        total = None
        for mid, block in zip(mids, blocks):
            more = dot_nt(mid[0], block[...])
            total = more if total is None else total + more
        got, line = gots[at]
        total = total + got[line].astype(F32)
        for q in range(n):
            share = total[q * rows : (q + 1) * rows]
            for lanes, places in packing(rows, width):
                piece = [share[first : first + size, lanes] for first, size in places[1]]
                out_ref[q, at, places[0]] = jnp.concatenate(piece, axis=1).astype(BF)


def wgrad_stack_kernel(part, *refs):
    out_ref = refs[-1]
    for at in range(out_ref.shape[0]):
        mids, rows = refs[8 * at : 8 * at + 4], refs[8 * at + 4 : 8 * at + 8]
        total = None
        for mid, row in zip(mids, rows):
            more = dot_nt(mid[part], row[...])
            total = more if total is None else total + more
        out_ref[at] = total.astype(BF)


def wgrad_give(pieces):
    mids, rows = pieces[0]
    shape = (len(pieces), mids[0].shape[1], rows[0].shape[0])
    args = [v for mids, rows in pieces for v in (*mids, *rows)]
    return call(
        functools.partial(wgrad_stack_kernel, 1), sds(shape, BF), args, "wgrad_give",
        vmem=20,
    )


def wgrad_sum(pieces, gots, shares):
    mids, rows = pieces[0]
    size = mids[0].shape[1] // shares * rows[0].shape[0]
    shape = (shares, len(pieces), size // LANES, LANES)
    args = [v for mids, rows in pieces for v in (*mids, *rows)]
    return call(
        wgrad_sum_kernel, hbm(shape, BF), (*args, *gots), "wgrad_sum", vmem=28,
    )


def kv_sum_kernel(
    own_ref, got_ref, col_ref, dq_ref, n0_ref, n1_ref, wq_ref, wk_ref, wv_ref,
    gain_ref, gain_ffn_ref, rel_ref, dkv_ref, total_ref, give_ref, small_ref,
):
    inner = wk_ref.shape[0]
    width, block = n0_ref.shape
    dq = dq_ref[...]
    d_kv = (own_ref[...] + got_ref[: 2 * inner].astype(F32)).astype(BF)
    dkv_ref[...] = d_kv
    col = col_ref[...] + merge(got_ref[2 * inner : 2 * inner + 1], got_ref[2 * inner + 1 : 2 * inner + 2])
    far = dot_tn(wq_ref[...], dq[:, block:]) + dot_tn(wk_ref[...], d_kv[:inner, block:])
    far = far + dot_tn(wv_ref[...], d_kv[inner:, block:])
    give_ref[:width] = far.astype(BF)
    own = dot_tn(wq_ref[...], dq[:, :block]) + dot_tn(wk_ref[...], d_kv[:inner, :block])
    own = own + dot_tn(wv_ref[...], d_kv[inner:, :block])
    total_ref[...] = own
    gain = lane_sum(own * n0_ref[...].astype(F32) + far * n1_ref[...].astype(F32)) / gain_ref[...]
    small_ref[...] = jnp.zeros_like(small_ref)
    for first, row in ((2, gain), (8, gain_ffn_ref[...])):
        for at in range(0, width, block):
            size = min(block, width - at)
            line = first + at // block
            small_ref[line : line + 1, :size] = row[:, at : at + size]
    small_ref[1:2, : rel_ref.shape[1]] = rel_ref[...]
    small_ref[0:1] = col[:, block:]
    high, low = split(small_ref[...])
    give_ref[width : width + EXTRA] = high
    give_ref[width + EXTRA :] = low
    small_ref[...] = merge(high, low)
    small_ref[0:1] = col[:, :block]


def last_kernel(
    c_ref, own_ref, got_ref, small_ref, x_ref, inv_ref, gain_ref, dres_ref,
    keep_ref, give_ref, keep_small_ref, rows_ref,
):
    width = x_ref.shape[0]
    grad = own_ref[...] + got_ref[:width].astype(F32)
    small = small_ref[...] + merge(got_ref[width : width + EXTRA], got_ref[width + EXTRA :])
    x = x_ref[...].astype(F32)
    gain = column(gain_ref[...], x.shape[1])
    rows_ref[:width] = dres_ref[...] + rms_back(x, inv_ref[...], gain, grad)
    rows_ref[width:] = small
    rows = keep_ref.shape[1]
    mine = pl.ds(pl.multiple_of(c_ref[0] * rows, rows), rows)
    theirs = pl.ds(pl.multiple_of((1 - c_ref[0]) * rows, rows), rows)
    keep_ref[...] = rows_ref[:width, mine]
    give_ref[:width] = rows_ref[:width, theirs]
    keep_small_ref[:EXTRA] = small[:, :rows]
    keep_small_ref[EXTRA:] = small[:, rows:]
    give_ref[width:] = keep_small_ref[...]
    give_ref[width : width + 1] = rows_ref[width : width + 1, theirs]
    keep_small_ref[0:1] = rows_ref[width : width + 1, mine]


def out_rows_kernel(c_ref, res_ref, own_ref, ga_ref, gb_ref, gd_ref, keep_ref, give_ref, rows_ref):
    total = res_ref[...] + (
        own_ref[...].astype(F32)
        + ga_ref[...].astype(F32)
        + gb_ref[...].astype(F32)
        + gd_ref[...].astype(F32)
    )
    rows_ref[...] = total.astype(BF)
    rows = keep_ref.shape[1]
    keep_ref[...] = rows_ref[:, pl.ds(pl.multiple_of(c_ref[0] * rows, rows), rows)]
    give_ref[...] = rows_ref[:, pl.ds(pl.multiple_of((1 - c_ref[0]) * rows, rows), rows)]


def fold_core_kernel(
    c_ref, dq_ref, dkv_ref, n0_ref, n1_ref, go_ref, got_ref, keep_ref, give_ref
):
    inner = dq_ref.shape[0]
    block = n0_ref.shape[1]
    n0 = n0_ref[...]
    n1 = n1_ref[...]

    def gradient(rows):
        return dot_nt(rows[:, :block], n0) + dot_nt(rows[:, block:], n1)

    first = c_ref[0] == 0
    gq = gradient(dq_ref[...])
    gv = gradient(dkv_ref[inner:])
    keep_ref[0] = jnp.where(first, gq, gv)
    give_ref[0] = jnp.where(first, gv, gq).astype(BF)
    gk = gradient(dkv_ref[:inner])
    go = go_ref[...] + got_ref[...].astype(F32)
    keep_ref[1] = jnp.where(first, gk, go)
    give_ref[1] = jnp.where(first, go, gk).astype(BF)


def fold_x_kernel(x_ref, mine_ref, got_ref, keep_ref, give_ref):
    total = mine_ref[...] + got_ref[...].astype(F32)
    first = x_ref[0] == 0
    keep_ref[...] = jnp.where(first, total[0], total[1])
    give_ref[...] = jnp.where(first, total[1], total[0]).astype(BF)


def share_kernel(bit_ref, mine_ref, got_ref, own_ref, give_ref, sum_ref):
    sum_ref[...] = mine_ref[...] + got_ref[...].astype(F32)
    keep, give = halves(bit_ref, own_ref.shape[0])
    own_ref[...] = sum_ref[keep, :]
    give_ref[...] = sum_ref[give, :].astype(BF)


def lines(small, first, width):
    half = small.shape[0] // 2
    pieces = []
    for at in range(-(-width // (2 * LANES))):
        line = first + at
        pieces += [small[line : line + 1], small[half + line : half + line + 1]]
    return jnp.concatenate(pieces, axis=1)[:, :width]


def share_sum_kernel(mine_ref, got_ref, small_ref, small_got_ref, out_ref):
    rows, width = mine_ref.shape
    out_ref[:rows] = (mine_ref[...] + got_ref[...].astype(F32)).astype(BF)
    small = small_ref[...] + small_got_ref[...]
    rel = small[1:2]
    rel = jnp.concatenate([rel, small[EXTRA + 1 : EXTRA + 2]], axis=1)
    rel = jnp.concatenate([rel, jnp.zeros((1, width - rel.shape[1]), F32)], axis=1)
    three = jnp.concatenate(
        [lines(small, 2, width), lines(small, 8, width), rel, jnp.zeros((5, width), F32)], axis=0
    )
    out_ref[rows:] = jnp.concatenate(split(three), axis=0)


def share_join_kernel(z_ref, *refs):
    shares, (out_ref, hold_ref) = refs[:-2], refs[-2:]
    n = len(shares)
    rows = shares[0].shape[0] - EXTRA
    for k, ref in enumerate(shares):
        at = lax.rem(z_ref[0] + n - k, n)
        line, rest, size = 0, at, n
        while size > 1:
            size //= 2
            line = line + lax.rem(rest, 2) * size
            rest = rest // 2
        out_ref[pl.ds(pl.multiple_of(line * rows, rows), rows), :] = ref[:rows]
        hold_ref[at] = merge(ref[rows : rows + 8], ref[rows + 8 :])
    total = hold_ref[0]
    for k in range(1, n):
        total = total + hold_ref[k]
    out_ref[n * rows :] = jnp.concatenate(split(total), axis=0)


def join_x_kernel(x_ref, own_ref, got_ref, out_ref, small_ref):
    inner = out_ref.shape[1]
    first = x_ref[0] == 0
    own = own_ref[:inner]
    got = got_ref[:inner]
    out_ref[0] = jnp.where(first, own, got)
    out_ref[1] = jnp.where(first, got, own)
    small_ref[...] = merge(own_ref[inner : inner + 8], own_ref[inner + 8 :]) + merge(
        got_ref[inner : inner + 8], got_ref[inner + 8 :]
    )


def join_core_kernel(c_ref, own_ref, got_ref, *outs):
    first = c_ref[0] == 0
    own = own_ref[...]
    got = got_ref[...]
    pair = (jnp.where(first, own, got), jnp.where(first, got, own))
    for at, out in enumerate(outs):
        out[...] = pair[at // 2][at % 2].astype(F32)


def place_kernel(c_ref, own_ref, got_ref, out_ref):
    out_ref[c_ref[0]] = own_ref[...]
    out_ref[1 - c_ref[0]] = got_ref[: own_ref.shape[0]]


def widen_kernel(src, *outs):
    for at, out in enumerate(outs):
        for lanes, (lines, places) in packing(*out.shape):
            piece = src[0, at, lines].astype(F32)
            lane = 0
            for first, size in places:
                wide = lanes.stop - lanes.start
                out[first : first + size, lanes] = piece[:, lane : lane + wide]
                lane += wide


def widen(v, rows, width):
    n, pieces, lines, _ = v.shape
    outs = pl.pallas_call(
        widen_kernel,
        out_shape=[sds((n * rows, width), F32)] * pieces,
        grid=(n,),
        in_specs=[pl.BlockSpec((1, pieces, lines, LANES), lambda i: (i, 0, 0, 0))],
        out_specs=[pl.BlockSpec((rows, width), lambda i: (i, 0))] * pieces,
        compiler_params=pltpu.CompilerParams(vmem_limit_bytes=32 << 20),
        cost_estimate=cost(500),
        name="widen",
    )(in_hbm(Order.follow(v)))
    return Order.done(outs)


def per_device(*args):
    Order.last = None
    return run(*args)


def run(
    inputs,
    lengths,
    delete_mask,
    buckets,
    gain_attn,
    w_query,
    w_key,
    w_value,
    w_out,
    rel_bias,
    gain_ffn,
    gate_weight,
    up_weight,
    down_weight,
    cotangent,
):
    seqs, row_count, width = inputs.shape
    dp_axis = lax.axis_size("dp")
    heads_axis = lax.axis_size("head")
    hid_axis = lax.axis_size("hid")
    assert seqs == 2 and heads_axis == 2 and hid_axis == 4
    z_at = lax.axis_index("dp")
    h_at = lax.axis_index("head")
    hid_at = lax.axis_index("hid")
    c_at = hid_at % 2
    x_at = hid_at // 2
    length = row_count * heads_axis * hid_axis
    block = 2 * row_count
    inner = w_query.shape[1]
    heads = inner // DH
    hidden = gate_weight.shape[1]
    bucket_count, total_heads = rel_bias.shape
    c_scalar = c_at.astype(jnp.int32).reshape(1)
    x_scalar = x_at.astype(jnp.int32).reshape(1)
    z_scalar = z_at.astype(jnp.int32).reshape(1)

    def core_swap(v, name):
        return move(v, "hid", [(i, i ^ 1) for i in range(hid_axis)], name)

    def x_swap(v, name):
        return move(v, "hid", [(i, i ^ 2) for i in range(hid_axis)], name)

    def y_swap(v, name):
        return move(v, "head", [(0, 1), (1, 0)], name)

    def grid_swap(v, relayed, name):
        pairs = []
        for h in range(heads_axis):
            for i in range(hid_axis):
                along_x = not relayed or i % 2 == 1
                along_y = not relayed or i % 2 == 0
                to = ((1 - h) if along_y else h) * hid_axis + ((i ^ 2) if along_x else i)
                pairs.append((h * hid_axis + i, to))
        return move(v, ("head", "hid"), pairs, name)

    def relay(from_x, from_y, name):
        picked = call(
            pick_kernel, sds(from_x.shape, BF), (from_x, from_y), "pick", scalars=(c_scalar,),
        )
        return grid_swap(picked, True, name)

    def stack(a, b):
        return jnp.concatenate([a, b], axis=0)

    def place(own, got):
        shape = sds((2, *own.shape), own.dtype)
        return call(place_kernel, shape, (own, got), "place", scalars=(c_scalar,), us=100)

    def after(v, *earlier):
        return lax.optimization_barrier((v, *earlier))[0]

    x_in = jnp.swapaxes(inputs, 1, 2)
    dy_in = jnp.swapaxes(cotangent, 1, 2)
    wq, wk, wv = w_query.T, w_key.T, w_value.T
    gate_w, up_w = gate_weight.T, up_weight.T
    gain_one = gain_attn.reshape(1, width)
    gain_two = gain_ffn.reshape(1, width)

    w_half = w_out.reshape(2, inner // 2, width)
    w_half = lax.dynamic_index_in_dim(w_half, c_at, 0, keepdims=False)
    x_rows, normed_one, inv_one = call(
        prep_kernel,
        (sds((width, block), BF), sds((width, block), BF), sds((1, block), F32)),
        (in_hbm(x_in), core_swap(x_in, "x_core"), gain_one),
        "prep",
        vmem=20,
        scalars=(c_scalar,),
    )
    normed_far_raw = y_swap(normed_one, "n1_y")

    dy_own = call(
        pair_kernel,
        sds((width, block), BF),
        (in_hbm(dy_in), in_hbm(core_swap(dy_in, "dy_core"))),
        "pair",
        vmem=16,
        scalars=(c_scalar,),
    )

    gate_other = core_swap(gate_w, "gate_core")
    up_other = core_swap(up_w, "up_core")
    down_other = core_swap(down_weight, "down_core")
    ffn_weights = (gate_w, gate_other, up_w, up_other, down_weight, down_other)
    def project(n):
        return call(
            qkv_kernel,
            (sds((inner, block), BF), sds((2 * inner, block), BF)),
            (n, wq, wk, wv),
            "qkv",
        )

    q_own, kv_own = project(normed_one)
    base = jnp.stack(
        [(h * 2 + x) * block for x in (x_at, 1 - x_at) for h in (h_at, 1 - h_at)]
    ).astype(jnp.int32)
    starts = (length - block - (base[:, None] - base[None, :2])).reshape(-1).astype(jnp.int32)
    bucket_rev = jnp.concatenate([jnp.full((1,), -1, jnp.int32), buckets[::-1]])
    hot = bucket_rev[None, :] == jnp.arange(bucket_count, dtype=jnp.int32)[:, None]
    local_bias = lax.dynamic_slice_in_dim(rel_bias, h_at * heads, heads, 1)
    table = jnp.sum(jnp.where(hot[None], local_bias.T[:, :, None], 0.0), axis=1)
    table = jnp.concatenate([table, jnp.zeros((8 - heads, 2 * length), F32)], axis=0)
    seq_mask = lax.dynamic_index_in_dim(delete_mask, c_at, 0, keepdims=False)
    seq_len = lax.dynamic_index_in_dim(lengths, c_at, 0, keepdims=False)
    seq_mask = jnp.where(jnp.arange(length, dtype=jnp.int32) < seq_len, seq_mask, NEG)
    seq_mask = seq_mask.reshape(2, 2, block)
    seq_mask = jnp.where(h_at == 0, seq_mask, seq_mask[::-1])
    seq_mask = jnp.where(x_at == 0, seq_mask, seq_mask[:, ::-1])
    seq_mask = jnp.swapaxes(seq_mask, 0, 1).reshape(1, length)
    seq_mask = after(seq_mask, gate_other, up_other)
    bias = make_bias(starts, table, seq_mask, heads, block, 4, 2)

    kv_own_x = x_swap(kv_own, "kv_own_x")
    normed_far_raw = after(normed_far_raw, bias, kv_own)
    normed_far = after(normed_far_raw, down_other, kv_own_x)
    w_half = y_swap(after(w_half, normed_far_raw), "wout_y")
    dy_y = y_swap(after(dy_own, w_half), "dy_y")
    w_half_got = core_swap(w_half, "wout_core")
    q_far, kv_far = project(normed_far)
    kv_far_x = x_swap(kv_far, "kv_far_x")
    dy_x = x_swap(after(dy_own, kv_far_x), "dy_x")
    queries = jnp.concatenate([q_own, q_far], axis=1)
    kvs = (kv_own, kv_far, kv_own_x, kv_far_x)

    probs, mixed = attn_fwd(queries, kvs, bias, heads, block)
    mixed_far = y_swap(mixed[:, block:], "mixed_y")
    mixed_far = after(mixed_far, dy_x, dy_y)
    mixed_own = mixed[:, :block]
    residual, normed_two, inv_two = call(
        mid_kernel,
        (hbm((width, block), F32), sds((width, block), BF), sds((1, block), F32)),
        (x_rows, mixed_own, mixed_far, w_out, w_half, w_half_got, gain_two),
        "mid",
        vmem=20,
        scalars=(c_scalar,),
    )

    n_x = x_swap(normed_two, "n2_x")
    n_y = y_swap(normed_two, "n2_y")
    dy_d = relay(dy_x, dy_y, "dy_d")
    def d_act_of(dy):
        shape = sds((2, hidden, block), F32)
        return call(d_act_kernel, shape, (dy, down_weight, down_other), "d_act")

    da_own = d_act_of(dy_own)
    act_o, dg_o, du_o, dn_o = ffn_chunk(normed_two, da_own, ffn_weights, BF)
    da_x = d_act_of(dy_x)
    da_y = d_act_of(dy_y)
    n_d = relay(n_x, n_y, "n2_d")
    act_x, dg_x, du_x, dn_x = ffn_chunk(n_x, da_x, ffn_weights, BF)
    got_x = x_swap(dn_x, "dn_x")
    act_y, dg_y, du_y, dn_y = ffn_chunk(n_y, da_y, ffn_weights, BF)
    got_y = y_swap(dn_y, "dn_y")
    act_d, dg_d, du_d, dn_d = ffn_chunk(n_d, d_act_of(dy_d), ffn_weights, BF)
    got_d = grid_swap(dn_d, False, "dn_d")

    n_all = (normed_two, n_x, n_y, n_d)
    dy_all = (dy_own, dy_x, dy_y, dy_d)
    pieces = (
        ((act_o, act_x, act_y, act_d), dy_all),
        ((dg_o, dg_x, dg_y, dg_d), n_all),
        ((du_o, du_x, du_y, du_d), n_all),
    )
    given_d = core_swap(wgrad_give(pieces[:1]), "wgrad_core")
    out_o = ffn_out(act_o, down_weight, down_other, BF)
    mids, rows = pieces[1]
    gated = (((after(mids[0], got_x, got_y), *mids[1:]), rows), pieces[2])
    given_gu = core_swap(wgrad_give(gated), "wgrad_core")
    part_x = ffn_out(act_x, down_weight, down_other, BF)
    part_y = ffn_out(act_y, down_weight, down_other, BF)
    part_d = ffn_out(act_d, down_weight, down_other, BF)
    shares = dp_axis if dp_axis <= 8 else 1
    ffn_grads = wgrad_sum(pieces, (given_d, given_gu), shares)
    if shares > 1:
        ffn_grads = lax.psum_scatter(ffn_grads, "dp", scatter_dimension=0, tiled=True)
    else:
        ffn_grads = lax.psum(ffn_grads, "dp")


    d_residual, d_branch, gain_ffn_part, d_mixed_own, d_mixed_give = call(
        mid_back_kernel,
        (
            hbm((width, block), F32),
            sds((width, block), BF),
            sds((1, width), F32),
            sds((inner, block), BF),
            sds((inner, block), BF),
        ),
        (*map(in_hbm, (dn_o, got_x, got_y, got_d, dy_own, residual)), inv_two, gain_two, w_out, w_half, w_half_got),
        "mid_back",
        vmem=24,
        scalars=(c_scalar,),
    )
    d_mixed = jnp.concatenate([d_mixed_own, y_swap(d_mixed_give, "dmixed_y")], axis=1)

    dq, dkv_own, dkv_give, col, table_grad = attn_bwd(
        starts, probs, queries, d_mixed, kvs, heads, block
    )
    dkv_got = x_swap(dkv_give, "dkv_x")
    out_x = in_hbm(x_swap(after(part_x, got_d), "out_x"))
    out_y = in_hbm(y_swap(after(part_y, got_d), "out_y"))
    d_branch = after(d_branch, dq)
    grad_out_own, grad_out_give = call(
        out_grad_kernel,
        (hbm((inner, width), F32), hbm((inner, width), BF)),
        (mixed_own, mixed_far, d_branch),
        "out_grad",
        vmem=20,
    )
    grad_out_got = y_swap(grad_out_give, "gout_y")
    dkv_got = after(dkv_got, out_x, out_y)
    table_grad = sum(jnp.roll(table_grad[:, i], -i, axis=1) for i in range(8))
    grad_rel = jnp.sum(jnp.where(hot[None], table_grad[:, None, :], 0.0), axis=2).T
    grad_rel = lax.dynamic_update_slice_in_dim(
        jnp.zeros((bucket_count, total_heads), F32), grad_rel, h_at * heads, 1
    )
    d_kv, back_own, back_give, small = call(
        kv_sum_kernel,
        (
            sds((2 * inner, 2 * block), BF),
            hbm((width, block), F32),
            hbm((width + 2 * EXTRA, block), BF),
            sds((EXTRA, block), F32),
        ),
        (
            *map(in_hbm, (dkv_own, dkv_got)), col,
            dq, *map(in_hbm, (normed_one, normed_far)), wq, wk, wv,
            gain_one, gain_ffn_part, grad_rel.reshape(1, -1),
        ),
        "kv_sum",
        vmem=24,
    )
    back_got = y_swap(back_give, "back_y")

    pair_f32, pair_bf = sds((2, inner, width), F32), sds((2, inner, width), BF)
    one_f32, one_bf = sds((inner, width), F32), sds((inner, width), BF)
    keep, give = call(
        fold_core_kernel,
        (hbm(pair_f32.shape, F32), hbm(pair_bf.shape, BF)),
        (dq, d_kv, *map(in_hbm, (normed_one, normed_far, grad_out_own, grad_out_got))),
        "fold_core",
        scalars=(c_scalar,),
        vmem=28,
    )
    keep, give = call(
        fold_x_kernel,
        (one_f32, one_bf),
        (in_hbm(keep), in_hbm(core_swap(give, "fold_core"))),
        "fold_x",
        vmem=20,
        scalars=(x_scalar,),
    )
    got = x_swap(give, "fold_x")
    steps = [1 << k for k in range(dp_axis.bit_length() - 1)]
    short = shares > 1 and 1 << len(steps) == dp_axis
    if short:
        keep, got = z_share(after(keep, back_got), got, steps[0], dp_axis, z_at)
    if shares > 1:
        ffn_grads = lax.all_gather(after(ffn_grads, keep), "dp", axis=0, tiled=True)
    rows_keep, rows_give, small, _ = call(
        last_kernel,
        (
            sds((width, row_count), F32),
            sds((width + 2 * EXTRA, row_count), F32),
            sds((2 * EXTRA, row_count), F32),
            sds((width + EXTRA, block), F32),
        ),
        (in_hbm(back_own), in_hbm(back_got), small, in_hbm(x_rows), inv_one, gain_one, in_hbm(d_residual)),
        "last",
        vmem=24,
        scalars=(c_scalar,),
    )
    rows_got = core_swap(rows_give, "grad_core")
    small_got = rows_got[width:]
    if short:
        for step in steps[1:]:
            keep, got = z_share(keep, got, step, dp_axis, z_at)
        folded = z_join(keep, got, small, small_got, dp_axis, z_scalar)
    else:
        folded = z_psum(keep, got, small, small_got)

    part_d = after(part_d, rows_keep)
    out_d = grid_swap(part_d, False, "out_d")
    out_keep, out_give, _ = call(
        out_rows_kernel,
        (
            sds((width, row_count), BF),
            sds((width, row_count), BF),
            sds((width, block), BF),
        ),
        tuple(map(in_hbm, (residual, out_o, out_x, out_y, out_d))),
        "out_rows",
        vmem=24,
        scalars=(c_scalar,),
    )

    joined = x_swap(folded, "join_x")
    grad_inputs = place(rows_keep, rows_got)
    output = place(out_keep, core_swap(out_give, "out_core"))
    folded, sums = call(
        join_x_kernel,
        (pair_bf, sds((8, width), F32)),
        (folded, joined),
        "join_x",
        scalars=(x_scalar,),
    )
    joined = core_swap(folded, "join_core")
    grad_w_query, grad_w_key, grad_w_value, grad_w_out = call(
        join_core_kernel,
        (one_f32,) * 4,
        (folded, joined),
        "join_core",
        scalars=(c_scalar,),
    )
    mask_keep, mask_got = small[:1], small_got[:1]
    grad_mask = jnp.where(c_at == 0, stack(mask_keep, mask_got), stack(mask_got, mask_keep))
    grad_down, grad_gate, grad_up = widen(ffn_grads, hidden // shares, width)
    return (
        jnp.swapaxes(output, 1, 2),
        jnp.swapaxes(grad_inputs, 1, 2),
        grad_mask,
        sums[0],
        grad_w_query.T,
        grad_w_key.T,
        grad_w_value.T,
        grad_w_out,
        sums[2, : bucket_count * total_heads].reshape(bucket_count, total_heads),
        sums[1],
        grad_gate.T,
        grad_up.T,
        grad_down,
    )


def z_swap(v, step, n, name):
    return move(v, "dp", [(i, i ^ step) for i in range(n)], name)


def z_share(mine, got, step, n, z_at):
    bit = ((z_at // step) % 2).astype(jnp.int32).reshape(1)
    rows, width = mine.shape
    half = (rows // 2, width)
    mine, give, _ = call(
        share_kernel,
        (sds(half, F32), sds(half, BF), sds((rows, width), F32)),
        (mine, got),
        "share",
        scalars=(bit,),
    )
    return mine, z_swap(give, step, n, "share_z")


def z_join(mine, got, small, small_got, n, z_scalar):
    rows, width = mine.shape
    total = call(
        share_sum_kernel,
        sds((rows + EXTRA, width), BF),
        (mine, got, small, small_got),
        "share_sum",
    )
    gots = [
        move(total, "dp", [(i, (i + k) % n) for i in range(n)], "join_z") for k in range(1, n)
    ]
    joined, _ = call(
        share_join_kernel,
        (sds((n * rows + EXTRA, width), BF), sds((n, 8, width), F32)),
        (total, *gots),
        "share_join",
        scalars=(z_scalar,),
    )
    return joined


def z_psum(mine, got, small, small_got):
    width = mine.shape[1]
    total = lax.psum((mine + got.astype(F32)).astype(BF), "dp")
    small = lax.psum(small + small_got, "dp")
    half = small.shape[0] // 2

    def row(first):
        both = jnp.concatenate([small[first:half], small[half + first :]], axis=1)
        return both.reshape(1, -1)[:, :width]

    three = jnp.concatenate([row(2), row(8), row(1), jnp.zeros((5, width), F32)], axis=0)
    return jnp.concatenate([total, *split(three)], axis=0)


def solution(mesh):
    rows = P("dp", ("head", "hid"), None)
    return jax.shard_map(
        per_device,
        mesh=mesh,
        in_specs=(
            rows,
            P("dp"),
            P("dp", None),
            P(),
            P(),
            P(None, "head"),
            P(None, "head"),
            P(None, "head"),
            P("head", None),
            P(),
            P(),
            P(None, ("head", "hid")),
            P(None, ("head", "hid")),
            P(("head", "hid"), None),
            rows,
        ),
        out_specs=(
            rows,
            rows,
            P("dp", ("head", "hid")),
            P(),
            P(None, "head"),
            P(None, "head"),
            P(None, "head"),
            P("head", None),
            P(),
            P(),
            P(None, ("head", "hid")),
            P(None, ("head", "hid")),
            P(("head", "hid"), None),
        ),
        check_vma=False,
    )
```

```python
import functools

import jax
import jax.numpy as jnp
from jax import lax
from jax.experimental import pallas as pl
from jax.experimental.pallas import tpu as pltpu
from jax.sharding import PartitionSpec as P


DH = 64
EPS = 1e-06
NEG = -1e30
BF = jnp.bfloat16
F32 = jnp.float32
GELU_C = 0.7978845608028654
GELU_K = 0.044715
LANES = 128
EXTRA = 16


def cost(us):
    return pl.CostEstimate(flops=0, bytes_accessed=int(us * 3.0e6), transcendentals=0)


NT = (((1,), (1,)), ((), ()))
TN = (((0,), (0,)), ((), ()))


def dot(a, b):
    return jnp.dot(a, b, preferred_element_type=F32)


def dot_nt(a, b):
    return lax.dot_general(a, b, NT, preferred_element_type=F32)


def dot_tn(a, b):
    return lax.dot_general(a, b, TN, preferred_element_type=F32)


def sds(shape, dtype):
    return jax.ShapeDtypeStruct(shape, dtype)


class Order:
    last = None

    @classmethod
    def follow(cls, v):
        return v if cls.last is None else lax.optimization_barrier((v, cls.last))[0]

    @classmethod
    def done(cls, outs):
        cls.last = min(jax.tree.leaves(outs), key=lambda v: v.size)
        return outs


def call(kernel, out_shape, args, name, scalars=(), vmem=12, us=0.01, **kw):
    args = (Order.follow(args[0]), *args[1:])
    in_specs = [pl.BlockSpec(memory_space=pltpu.SMEM)] * len(scalars)
    in_specs += [pl.BlockSpec(memory_space=pltpu.VMEM)] * len(args)
    outs = pl.pallas_call(
        kernel,
        out_shape=out_shape,
        in_specs=in_specs,
        out_specs=jax.tree.map(lambda _: pl.BlockSpec(memory_space=pltpu.VMEM), out_shape),
        compiler_params=pltpu.CompilerParams(vmem_limit_bytes=vmem << 20),
        cost_estimate=cost(us),
        name=name,
        **kw,
    )(*scalars, *args)
    return Order.done(outs)


def hbm(shape, dtype):
    return pltpu.HBM(shape, dtype)


def in_hbm(v):
    return pltpu.with_memory_space_constraint(v, pltpu.HBM)


def move(v, axes, pairs, name):
    with jax.named_scope(name):
        return lax.ppermute(v, axes, pairs)


def lane_sum(v):
    total = v[:, :LANES]
    for at in range(LANES, v.shape[1], LANES):
        total = total + v[:, at : at + LANES]
    return jnp.sum(total.T, axis=0, keepdims=True)


def column(row, width):
    wide = jnp.broadcast_to(row, (LANES, row.shape[1])).T
    return jnp.concatenate([wide] * (width // LANES), axis=1)


def pair_rows(c, own_ref, far_ref):
    own = own_ref[c]
    far = far_ref[c]
    first = c == 0
    return jnp.concatenate([jnp.where(first, own, far), jnp.where(first, far, own)], axis=1)


def pick_kernel(c_ref, first_ref, second_ref, out_ref):
    out_ref[...] = jnp.where(c_ref[0] == 0, first_ref[...], second_ref[...])


def pair_kernel(c_ref, own_ref, far_ref, out_ref):
    out_ref[...] = pair_rows(c_ref[0], own_ref, far_ref)


def prep_kernel(c_ref, own_ref, far_ref, gain_ref, x_ref, n_ref, inv_ref):
    rows = pair_rows(c_ref[0], own_ref, far_ref)
    x_ref[...] = rows
    x = rows.astype(F32)
    inverse = lax.rsqrt(jnp.mean(x * x, axis=0, keepdims=True) + EPS)
    inv_ref[...] = inverse
    n_ref[...] = (x * inverse * column(gain_ref[...], x.shape[1])).astype(BF)


def qkv_kernel(n_ref, wq_ref, wk_ref, wv_ref, q_ref, kv_ref):
    n = n_ref[...]
    inner = wq_ref.shape[0]
    q_ref[...] = dot(wq_ref[...], n).astype(BF)
    kv_ref[:inner] = dot(wk_ref[...], n).astype(BF)
    kv_ref[inner:] = dot(wv_ref[...], n).astype(BF)


def bias_kernel(start_ref, table_ref, mask_ref, out_ref, *, heads, block, q_blocks):
    kb = pl.program_id(0)
    qb = pl.program_id(1)
    start = pl.multiple_of(start_ref[kb * q_blocks + qb], block)
    k_at = pl.multiple_of(kb * block, block)
    mask = column(mask_ref[:, pl.ds(k_at, block)], block)
    for h in range(heads):
        window = table_ref[h : h + 1, pl.ds(start, 2 * block)]
        window = jnp.broadcast_to(window, (block, 2 * block))
        rolled = pltpu.roll(window, block, 1, stride=1, stride_axis=0)
        out_ref[h] = rolled[:, :block] + mask


def make_bias(starts, table, mask_row, heads, block, k_blocks, q_blocks):
    length = k_blocks * block
    outs = pl.pallas_call(
        functools.partial(bias_kernel, heads=heads, block=block, q_blocks=q_blocks),
        out_shape=pltpu.HBM((heads, length, q_blocks * block), F32),
        grid_spec=pltpu.PrefetchScalarGridSpec(
            num_scalar_prefetch=1,
            grid=(k_blocks, q_blocks),
            in_specs=[
                pl.BlockSpec(table.shape, lambda k, q, s: (0, 0)),
                pl.BlockSpec((1, length), lambda k, q, s: (0, 0)),
            ],
            out_specs=pl.BlockSpec((heads, block, block), lambda k, q, s: (0, k, q)),
        ),
        compiler_params=pltpu.CompilerParams(vmem_limit_bytes=16 << 20),
        cost_estimate=cost(0.01),
        name="bias",
    )(starts, table, Order.follow(mask_row))
    return Order.done(outs)


def attn_fwd_kernel(q_ref, k0, k1, k2, k3, bias_ref, p_ref, o_ref, *, inner):
    h = pl.program_id(1)
    at_k = pl.ds(pl.multiple_of(h * DH, DH), DH)
    at_v = pl.ds(pl.multiple_of(inner + h * DH, DH), DH)
    q = q_ref[...]
    parts = [dot_tn(ref[at_k, :], q) for ref in (k0, k1, k2, k3)]
    s = jnp.concatenate(parts, axis=0) + bias_ref[0]
    top = jnp.max(s, axis=0, keepdims=True)
    e = jnp.exp(s - top)
    total = jnp.sum(e, axis=0, keepdims=True)
    p = e * (1.0 / total)
    p_ref[0] = p
    pb = p.astype(BF)
    values = jnp.concatenate([ref[at_v, :] for ref in (k0, k1, k2, k3)], axis=1)
    o_ref[...] = dot(values, pb).astype(BF)


def attn_fwd(q, kvs, bias, heads, block):
    inner, rows = q.shape
    length = bias.shape[1]
    full = lambda i, h: (0, 0)
    slab = pl.BlockSpec((1, length, block), lambda i, h: (h, 0, i))
    head = pl.BlockSpec((DH, block), lambda i, h: (h, i))
    outs = pl.pallas_call(
        functools.partial(attn_fwd_kernel, inner=inner),
        out_shape=(pltpu.HBM((heads, length, rows), F32), sds((inner, rows), BF)),
        grid=(rows // block, heads),
        in_specs=[head] + [pl.BlockSpec(kv.shape, full) for kv in kvs] + [slab],
        out_specs=(slab, head),
        compiler_params=pltpu.CompilerParams(vmem_limit_bytes=14 << 20),
        cost_estimate=cost(0.01),
        name="attn_fwd",
    )(Order.follow(q), *kvs, in_hbm(bias))
    return Order.done(outs)


def diagonals(piece, block):
    total = None
    for shift in range(0, LANES, 8):
        wide = None
        for part in range(block // LANES):
            rows = piece[part * LANES + shift : part * LANES + shift + 8]
            pieces = [jnp.zeros((8, block - part * LANES), F32), rows]
            if part:
                pieces.append(jnp.zeros((8, part * LANES), F32))
            rows = jnp.concatenate(pieces, axis=1)
            wide = rows if wide is None else wide + rows
        if shift:
            wide = pltpu.roll(wide, 2 * block - shift, 1)
        total = wide if total is None else total + wide
    return total


def attn_bwd_kernel(
    start_ref, p_ref, q_ref, do_ref, k0, k1, k2, k3, dq_ref, own_ref, give_ref, col_ref, table_ref,
    acc, col_acc, *, inner, heads, block, q_blocks,
):
    qb = pl.program_id(0)
    h = pl.program_id(1)
    kvs = (k0, k1, k2, k3)
    at_k = pl.ds(pl.multiple_of(h * DH, DH), DH)
    at_v = pl.ds(pl.multiple_of(inner + h * DH, DH), DH)
    half = len(kvs) * block // 2

    @pl.when((qb == 0) & (h == 0))
    def _():
        acc[...] = jnp.zeros_like(acc)
        col_acc[...] = jnp.zeros_like(col_acc)
        table_ref[...] = jnp.zeros_like(table_ref)

    q = q_ref[...]
    do = do_ref[...]
    dp = jnp.concatenate([dot_tn(ref[at_v, :], do) for ref in kvs], axis=0)
    p = p_ref[0]
    inside = jnp.sum(p * dp, axis=0, keepdims=True)
    ds = p * (dp - inside)
    col_acc[...] += ds
    for kb in range(len(kvs)):
        start = pl.multiple_of(start_ref[kb * q_blocks + qb], block)
        piece = ds[kb * block : (kb + 1) * block]
        table_ref[h, :, pl.ds(start, 2 * block)] += diagonals(piece, block)
    dsb = ds.astype(BF)
    pb = p.astype(BF)
    acc[at_k, :] += dot_nt(q, dsb)
    acc[at_v, :] += dot_nt(do, pb)
    keys = jnp.concatenate([ref[at_k, :] for ref in kvs], axis=1)
    dq_ref[...] = dot(keys, dsb).astype(BF)

    @pl.when((qb == q_blocks - 1) & (h == heads - 1))
    def _():
        own_ref[...] = acc[:, :half]
        col = lane_sum(col_acc[...])
        col_ref[...] = col[:, :half]
        give_ref[: 2 * inner] = acc[:, half:].astype(BF)
        give_ref[2 * inner :] = split_rows(col[:, half:])


def split(v):
    high = v.astype(BF)
    return high, (v - high.astype(F32)).astype(BF)


def merge(high, low):
    return high.astype(F32) + low.astype(F32)


def split_rows(row):
    high = row.astype(BF)
    low = (row - high.astype(F32)).astype(BF)
    at = lax.broadcasted_iota(jnp.int32, (EXTRA, row.shape[1]), 0)
    wide = jnp.where(at == 0, high.astype(F32), jnp.where(at == 1, low.astype(F32), 0.0))
    return wide.astype(BF)


def attn_bwd(starts, p, q, do, kvs, heads, block):
    inner, rows = q.shape
    length = p.shape[1]
    half = length // 2
    q_blocks = rows // block
    full = lambda i, h, s: (0, 0)
    head = pl.BlockSpec((DH, block), lambda i, h, s: (h, i))
    outs = pl.pallas_call(
        functools.partial(
            attn_bwd_kernel, inner=inner, heads=heads, block=block, q_blocks=q_blocks
        ),
        out_shape=(
            sds((inner, rows), BF),
            hbm((2 * inner, half), F32),
            hbm((2 * inner + EXTRA, half), BF),
            sds((1, half), F32),
            sds((heads, 8, 2 * length), F32),
        ),
        grid_spec=pltpu.PrefetchScalarGridSpec(
            num_scalar_prefetch=1,
            grid=(q_blocks, heads),
            in_specs=[pl.BlockSpec((1, length, block), lambda i, h, s: (h, 0, i)), head, head]
            + [pl.BlockSpec(kv.shape, full) for kv in kvs],
            out_specs=(
                head,
                pl.BlockSpec((2 * inner, half), full),
                pl.BlockSpec((2 * inner + EXTRA, half), full),
                pl.BlockSpec((1, half), full),
                pl.BlockSpec((heads, 8, 2 * length), lambda i, h, s: (0, 0, 0)),
            ),
            scratch_shapes=[
                pltpu.VMEM((2 * inner, length), F32),
                pltpu.VMEM((length, block), F32),
            ],
        ),
        compiler_params=pltpu.CompilerParams(vmem_limit_bytes=28 << 20),
        cost_estimate=cost(500),
        name="attn_bwd",
    )(starts, in_hbm(p), Order.follow(q), do, *kvs)
    return Order.done(outs)


def halves(c_ref, half):
    return [pl.ds(pl.multiple_of(at * half, half), half) for at in (c_ref[0], 1 - c_ref[0])]


def mid_kernel(
    c_ref, x_ref, m0_ref, m1_ref, w0_ref, w1_ref, w2_ref, gain_ref, res_ref, n_ref, inv_ref
):
    attended = dot_tn(w0_ref[...], m0_ref[...])
    for at, w_ref in zip(halves(c_ref, w1_ref.shape[0]), (w1_ref, w2_ref)):
        attended = attended + dot_tn(w_ref[...], m1_ref[at, :])
    res = x_ref[...].astype(F32) + attended
    res_ref[...] = res
    inverse = lax.rsqrt(jnp.mean(res * res, axis=0, keepdims=True) + EPS)
    inv_ref[...] = inverse
    n_ref[...] = (res * inverse * column(gain_ref[...], res.shape[1])).astype(BF)


def rms_back(rows, inverse, gain, grad):
    scaled = grad * gain
    inside = jnp.mean(rows * scaled, axis=0, keepdims=True)
    return inverse * scaled - rows * (inverse * inverse * inverse * inside)


def mid_back_kernel(
    c_ref, own_ref, ga_ref, gb_ref, gd_ref, dy_ref, res_ref, inv_ref, gain_ref, w0_ref, w1_ref, w2_ref,
    dres_ref, branch_ref, gain_grad_ref, dm0_ref, dm1_ref,
):
    grad = own_ref[...].astype(F32) + ga_ref[...].astype(F32) + gb_ref[...].astype(F32)
    grad = grad + gd_ref[...].astype(F32)
    res = res_ref[...]
    inverse = inv_ref[...]
    gain_grad_ref[...] = lane_sum(grad * (res * inverse))
    gain = column(gain_ref[...], res.shape[1])
    d_res = dy_ref[...].astype(F32) + rms_back(res, inverse, gain, grad)
    dres_ref[...] = d_res
    branch = d_res.astype(BF)
    branch_ref[...] = branch
    dm0_ref[...] = dot(w0_ref[...], branch).astype(BF)
    for at, w_ref in zip(halves(c_ref, w1_ref.shape[0]), (w1_ref, w2_ref)):
        dm1_ref[at, :] = dot(w_ref[...], branch).astype(BF)


def out_grad_kernel(m0_ref, m1_ref, branch_ref, own_ref, far_ref):
    branch = branch_ref[...]
    own_ref[...] = dot_nt(m0_ref[...], branch)
    far_ref[...] = dot_nt(m1_ref[...], branch).astype(BF)


def d_act_kernel(dy_ref, d0, d1, out_ref):
    dy = dy_ref[...]
    for part, w_ref in enumerate((d0, d1)):
        out_ref[part] = dot(w_ref[...], dy)


def ffn_kernel(n_ref, da_ref, g0, g1, u0, u1, a_ref, dg_ref, du_ref, dn_ref):
    n = n_ref[...]
    total = None
    for part, (g_w, u_w) in enumerate(((g0, u0), (g1, u1))):
        gate = dot(g_w[...], n)
        up = dot(u_w[...], n)
        d_act = da_ref[part]
        square = gate * gate
        t = jnp.tanh(gate * (GELU_C + (GELU_C * GELU_K) * square))
        half = 0.5 + 0.5 * t
        gelu = gate * half
        slope = half + gelu * (1.0 - t) * (GELU_C + (3.0 * GELU_C * GELU_K) * square)
        a_ref[part] = (gelu * up).astype(BF)
        d_gate = (d_act * up * slope).astype(BF)
        d_up = (d_act * gelu).astype(BF)
        dg_ref[part] = d_gate
        du_ref[part] = d_up
        more = dot_tn(g_w[...], d_gate) + dot_tn(u_w[...], d_up)
        total = more if total is None else total + more
    dn_ref[...] = total.astype(dn_ref.dtype)


def ffn_chunk(n, d_act, weights, out_dtype):
    width, rows = n.shape
    hidden = weights[0].shape[0]
    mid = sds((2, hidden, rows), BF)
    return call(
        ffn_kernel,
        (mid, mid, mid, sds((width, rows), out_dtype)),
        (n, d_act, *weights[:4]),
        "ffn",
        vmem=20,
    )


def ffn_out_kernel(a_ref, d0, d1, o_ref):
    total = dot_tn(d0[...], a_ref[0]) + dot_tn(d1[...], a_ref[1])
    o_ref[...] = total.astype(o_ref.dtype)


def ffn_out(act, d0, d1, dtype):
    _, hidden, rows = act.shape
    width = d0.shape[1]
    return call(
        ffn_out_kernel, hbm((width, rows), dtype), (act, d0, d1), "ffn_out", vmem=16,
    )


def mids_shape(refs):
    return refs[0].shape[1], refs[4].shape[0]


def packing(rows, width):
    full, rest = divmod(width, LANES)
    assert 2 * rest == LANES and rows % 16 == 0
    half = rows // 2
    plan = []
    for at in range(full):
        lanes = slice(at * LANES, (at + 1) * LANES)
        plan.append((lanes, (slice(at * rows, (at + 1) * rows), ((0, rows),))))
    lanes = slice(full * LANES, width)
    plan.append((lanes, (slice(full * rows, full * rows + half), ((0, half), (half, half)))))
    return plan


def wgrad_sum_kernel(*refs):
    out_ref = refs[-1]
    n, pieces = out_ref.shape[:2]
    hidden, width = mids_shape(refs)
    rows = hidden // n
    gots = [(ref, at) for ref in refs[8 * pieces : -1] for at in range(ref.shape[0])]
    for at in range(pieces):
        mids, blocks = refs[8 * at : 8 * at + 4], refs[8 * at + 4 : 8 * at + 8]
        total = None
        for mid, block in zip(mids, blocks):
            more = dot_nt(mid[0], block[...])
            total = more if total is None else total + more
        got, line = gots[at]
        total = total + got[line].astype(F32)
        for q in range(n):
            share = total[q * rows : (q + 1) * rows]
            for lanes, places in packing(rows, width):
                piece = [share[first : first + size, lanes] for first, size in places[1]]
                out_ref[q, at, places[0]] = jnp.concatenate(piece, axis=1).astype(BF)


def wgrad_stack_kernel(part, *refs):
    out_ref = refs[-1]
    for at in range(out_ref.shape[0]):
        mids, rows = refs[8 * at : 8 * at + 4], refs[8 * at + 4 : 8 * at + 8]
        total = None
        for mid, row in zip(mids, rows):
            more = dot_nt(mid[part], row[...])
            total = more if total is None else total + more
        out_ref[at] = total.astype(BF)


def wgrad_give(pieces):
    mids, rows = pieces[0]
    shape = (len(pieces), mids[0].shape[1], rows[0].shape[0])
    args = [v for mids, rows in pieces for v in (*mids, *rows)]
    return call(
        functools.partial(wgrad_stack_kernel, 1), sds(shape, BF), args, "wgrad_give",
        vmem=20,
    )


def wgrad_sum(pieces, gots, shares):
    mids, rows = pieces[0]
    size = mids[0].shape[1] // shares * rows[0].shape[0]
    shape = (shares, len(pieces), size // LANES, LANES)
    args = [v for mids, rows in pieces for v in (*mids, *rows)]
    return call(
        wgrad_sum_kernel, hbm(shape, BF), (*args, *gots), "wgrad_sum", vmem=28,
    )


def kv_sum_kernel(
    own_ref, got_ref, col_ref, dq_ref, n0_ref, n1_ref, wq_ref, wk_ref, wv_ref,
    gain_ref, gain_ffn_ref, rel_ref, dkv_ref, total_ref, give_ref, small_ref,
):
    inner = wk_ref.shape[0]
    width, block = n0_ref.shape
    dq = dq_ref[...]
    d_kv = (own_ref[...] + got_ref[: 2 * inner].astype(F32)).astype(BF)
    dkv_ref[...] = d_kv
    col = col_ref[...] + merge(got_ref[2 * inner : 2 * inner + 1], got_ref[2 * inner + 1 : 2 * inner + 2])
    far = dot_tn(wq_ref[...], dq[:, block:]) + dot_tn(wk_ref[...], d_kv[:inner, block:])
    far = far + dot_tn(wv_ref[...], d_kv[inner:, block:])
    give_ref[:width] = far.astype(BF)
    own = dot_tn(wq_ref[...], dq[:, :block]) + dot_tn(wk_ref[...], d_kv[:inner, :block])
    own = own + dot_tn(wv_ref[...], d_kv[inner:, :block])
    total_ref[...] = own
    gain = lane_sum(own * n0_ref[...].astype(F32) + far * n1_ref[...].astype(F32)) / gain_ref[...]
    small_ref[...] = jnp.zeros_like(small_ref)
    for first, row in ((2, gain), (8, gain_ffn_ref[...])):
        for at in range(0, width, block):
            size = min(block, width - at)
            line = first + at // block
            small_ref[line : line + 1, :size] = row[:, at : at + size]
    small_ref[1:2, : rel_ref.shape[1]] = rel_ref[...]
    small_ref[0:1] = col[:, block:]
    high, low = split(small_ref[...])
    give_ref[width : width + EXTRA] = high
    give_ref[width + EXTRA :] = low
    small_ref[...] = merge(high, low)
    small_ref[0:1] = col[:, :block]


def last_kernel(
    c_ref, own_ref, got_ref, small_ref, x_ref, inv_ref, gain_ref, dres_ref,
    keep_ref, give_ref, keep_small_ref, rows_ref,
):
    width = x_ref.shape[0]
    grad = own_ref[...] + got_ref[:width].astype(F32)
    small = small_ref[...] + merge(got_ref[width : width + EXTRA], got_ref[width + EXTRA :])
    x = x_ref[...].astype(F32)
    gain = column(gain_ref[...], x.shape[1])
    rows_ref[:width] = dres_ref[...] + rms_back(x, inv_ref[...], gain, grad)
    rows_ref[width:] = small
    rows = keep_ref.shape[1]
    mine = pl.ds(pl.multiple_of(c_ref[0] * rows, rows), rows)
    theirs = pl.ds(pl.multiple_of((1 - c_ref[0]) * rows, rows), rows)
    keep_ref[...] = rows_ref[:width, mine]
    give_ref[:width] = rows_ref[:width, theirs]
    keep_small_ref[:EXTRA] = small[:, :rows]
    keep_small_ref[EXTRA:] = small[:, rows:]
    give_ref[width:] = keep_small_ref[...]
    give_ref[width : width + 1] = rows_ref[width : width + 1, theirs]
    keep_small_ref[0:1] = rows_ref[width : width + 1, mine]


def out_rows_kernel(c_ref, res_ref, own_ref, ga_ref, gb_ref, gd_ref, keep_ref, give_ref, rows_ref):
    total = res_ref[...] + (
        own_ref[...].astype(F32)
        + ga_ref[...].astype(F32)
        + gb_ref[...].astype(F32)
        + gd_ref[...].astype(F32)
    )
    rows_ref[...] = total.astype(BF)
    rows = keep_ref.shape[1]
    keep_ref[...] = rows_ref[:, pl.ds(pl.multiple_of(c_ref[0] * rows, rows), rows)]
    give_ref[...] = rows_ref[:, pl.ds(pl.multiple_of((1 - c_ref[0]) * rows, rows), rows)]


def fold_core_kernel(
    c_ref, dq_ref, dkv_ref, n0_ref, n1_ref, go_ref, got_ref, keep_ref, give_ref
):
    inner = dq_ref.shape[0]
    block = n0_ref.shape[1]
    n0 = n0_ref[...]
    n1 = n1_ref[...]

    def gradient(rows):
        return dot_nt(rows[:, :block], n0) + dot_nt(rows[:, block:], n1)

    first = c_ref[0] == 0
    gq = gradient(dq_ref[...])
    gv = gradient(dkv_ref[inner:])
    keep_ref[0] = jnp.where(first, gq, gv)
    give_ref[0] = jnp.where(first, gv, gq).astype(BF)
    gk = gradient(dkv_ref[:inner])
    go = go_ref[...] + got_ref[...].astype(F32)
    keep_ref[1] = jnp.where(first, gk, go)
    give_ref[1] = jnp.where(first, go, gk).astype(BF)


def fold_x_kernel(x_ref, mine_ref, got_ref, keep_ref, give_ref):
    total = mine_ref[...] + got_ref[...].astype(F32)
    first = x_ref[0] == 0
    keep_ref[...] = jnp.where(first, total[0], total[1])
    give_ref[...] = jnp.where(first, total[1], total[0]).astype(BF)


def share_kernel(bit_ref, mine_ref, got_ref, own_ref, give_ref, sum_ref):
    sum_ref[...] = mine_ref[...] + got_ref[...].astype(F32)
    keep, give = halves(bit_ref, own_ref.shape[0])
    own_ref[...] = sum_ref[keep, :]
    give_ref[...] = sum_ref[give, :].astype(BF)


def lines(small, first, width):
    half = small.shape[0] // 2
    pieces = []
    for at in range(-(-width // (2 * LANES))):
        line = first + at
        pieces += [small[line : line + 1], small[half + line : half + line + 1]]
    return jnp.concatenate(pieces, axis=1)[:, :width]


def share_sum_kernel(mine_ref, got_ref, small_ref, small_got_ref, out_ref):
    rows, width = mine_ref.shape
    out_ref[:rows] = (mine_ref[...] + got_ref[...].astype(F32)).astype(BF)
    small = small_ref[...] + small_got_ref[...]
    rel = small[1:2]
    rel = jnp.concatenate([rel, small[EXTRA + 1 : EXTRA + 2]], axis=1)
    rel = jnp.concatenate([rel, jnp.zeros((1, width - rel.shape[1]), F32)], axis=1)
    three = jnp.concatenate(
        [lines(small, 2, width), lines(small, 8, width), rel, jnp.zeros((5, width), F32)], axis=0
    )
    out_ref[rows:] = jnp.concatenate(split(three), axis=0)


def share_join_kernel(z_ref, *refs):
    shares, (out_ref, hold_ref) = refs[:-2], refs[-2:]
    n = len(shares)
    rows = shares[0].shape[0] - EXTRA
    for k, ref in enumerate(shares):
        at = lax.rem(z_ref[0] + n - k, n)
        line, rest, size = 0, at, n
        while size > 1:
            size //= 2
            line = line + lax.rem(rest, 2) * size
            rest = rest // 2
        out_ref[pl.ds(pl.multiple_of(line * rows, rows), rows), :] = ref[:rows]
        hold_ref[at] = merge(ref[rows : rows + 8], ref[rows + 8 :])
    total = hold_ref[0]
    for k in range(1, n):
        total = total + hold_ref[k]
    out_ref[n * rows :] = jnp.concatenate(split(total), axis=0)


def join_x_kernel(x_ref, own_ref, got_ref, out_ref, small_ref):
    inner = out_ref.shape[1]
    first = x_ref[0] == 0
    own = own_ref[:inner]
    got = got_ref[:inner]
    out_ref[0] = jnp.where(first, own, got)
    out_ref[1] = jnp.where(first, got, own)
    small_ref[...] = merge(own_ref[inner : inner + 8], own_ref[inner + 8 :]) + merge(
        got_ref[inner : inner + 8], got_ref[inner + 8 :]
    )


def join_core_kernel(c_ref, own_ref, got_ref, *outs):
    first = c_ref[0] == 0
    own = own_ref[...]
    got = got_ref[...]
    pair = (jnp.where(first, own, got), jnp.where(first, got, own))
    for at, out in enumerate(outs):
        out[...] = pair[at // 2][at % 2].astype(F32)


def place_kernel(c_ref, own_ref, got_ref, out_ref):
    out_ref[c_ref[0]] = own_ref[...]
    out_ref[1 - c_ref[0]] = got_ref[: own_ref.shape[0]]


def widen_kernel(src, *outs):
    for at, out in enumerate(outs):
        for lanes, (lines, places) in packing(*out.shape):
            piece = src[0, at, lines].astype(F32)
            lane = 0
            for first, size in places:
                wide = lanes.stop - lanes.start
                out[first : first + size, lanes] = piece[:, lane : lane + wide]
                lane += wide


def widen(v, rows, width):
    n, pieces, lines, _ = v.shape
    outs = pl.pallas_call(
        widen_kernel,
        out_shape=[sds((n * rows, width), F32)] * pieces,
        grid=(n,),
        in_specs=[pl.BlockSpec((1, pieces, lines, LANES), lambda i: (i, 0, 0, 0))],
        out_specs=[pl.BlockSpec((rows, width), lambda i: (i, 0))] * pieces,
        compiler_params=pltpu.CompilerParams(vmem_limit_bytes=32 << 20),
        cost_estimate=cost(500),
        name="widen",
    )(in_hbm(Order.follow(v)))
    return Order.done(outs)


def per_device(*args):
    Order.last = None
    return run(*args)


def run(
    inputs,
    lengths,
    delete_mask,
    buckets,
    gain_attn,
    w_query,
    w_key,
    w_value,
    w_out,
    rel_bias,
    gain_ffn,
    gate_weight,
    up_weight,
    down_weight,
    cotangent,
):
    seqs, row_count, width = inputs.shape
    dp_axis = lax.axis_size("dp")
    heads_axis = lax.axis_size("head")
    hid_axis = lax.axis_size("hid")
    assert seqs == 2 and heads_axis == 2 and hid_axis == 4
    z_at = lax.axis_index("dp")
    h_at = lax.axis_index("head")
    hid_at = lax.axis_index("hid")
    c_at = hid_at % 2
    x_at = hid_at // 2
    length = row_count * heads_axis * hid_axis
    block = 2 * row_count
    inner = w_query.shape[1]
    heads = inner // DH
    hidden = gate_weight.shape[1]
    bucket_count, total_heads = rel_bias.shape
    c_scalar = c_at.astype(jnp.int32).reshape(1)
    x_scalar = x_at.astype(jnp.int32).reshape(1)
    z_scalar = z_at.astype(jnp.int32).reshape(1)

    def core_swap(v, name):
        return move(v, "hid", [(i, i ^ 1) for i in range(hid_axis)], name)

    def x_swap(v, name):
        return move(v, "hid", [(i, i ^ 2) for i in range(hid_axis)], name)

    def y_swap(v, name):
        return move(v, "head", [(0, 1), (1, 0)], name)

    def grid_swap(v, relayed, name):
        pairs = []
        for h in range(heads_axis):
            for i in range(hid_axis):
                along_x = not relayed or i % 2 == 1
                along_y = not relayed or i % 2 == 0
                to = ((1 - h) if along_y else h) * hid_axis + ((i ^ 2) if along_x else i)
                pairs.append((h * hid_axis + i, to))
        return move(v, ("head", "hid"), pairs, name)

    def relay(from_x, from_y, name):
        picked = call(
            pick_kernel, sds(from_x.shape, BF), (from_x, from_y), "pick", scalars=(c_scalar,),
        )
        return grid_swap(picked, True, name)

    def stack(a, b):
        return jnp.concatenate([a, b], axis=0)

    def place(own, got):
        shape = sds((2, *own.shape), own.dtype)
        return call(place_kernel, shape, (own, got), "place", scalars=(c_scalar,), us=100)

    def after(v, *earlier):
        return lax.optimization_barrier((v, *earlier))[0]

    x_in = jnp.swapaxes(inputs, 1, 2)
    dy_in = jnp.swapaxes(cotangent, 1, 2)
    wq, wk, wv = w_query.T, w_key.T, w_value.T
    gate_w, up_w = gate_weight.T, up_weight.T
    gain_one = gain_attn.reshape(1, width)
    gain_two = gain_ffn.reshape(1, width)

    x_got = core_swap(x_in, "x_core")
    x_rows, normed_one, inv_one = call(
        prep_kernel,
        (sds((width, block), BF), sds((width, block), BF), sds((1, block), F32)),
        (in_hbm(x_in), x_got, gain_one),
        "prep",
        vmem=20,
        scalars=(c_scalar,),
    )
    normed_far_raw = y_swap(normed_one, "n1_y")

    dy_own = call(
        pair_kernel,
        sds((width, block), BF),
        (in_hbm(dy_in), in_hbm(core_swap(dy_in, "dy_core"))),
        "pair",
        vmem=16,
        scalars=(c_scalar,),
    )

    gate_other = core_swap(after(gate_w, x_got), "gate_core")
    up_other = core_swap(after(up_w, x_got), "up_core")
    down_other = core_swap(after(down_weight, x_got), "down_core")
    ffn_weights = (gate_w, gate_other, up_w, up_other, down_weight, down_other)
    def project(n):
        return call(
            qkv_kernel,
            (sds((inner, block), BF), sds((2 * inner, block), BF)),
            (n, wq, wk, wv),
            "qkv",
        )

    q_own, kv_own = project(normed_one)
    base = jnp.stack(
        [(h * 2 + x) * block for x in (x_at, 1 - x_at) for h in (h_at, 1 - h_at)]
    ).astype(jnp.int32)
    starts = (length - block - (base[:, None] - base[None, :2])).reshape(-1).astype(jnp.int32)
    bucket_rev = jnp.concatenate([jnp.full((1,), -1, jnp.int32), buckets[::-1]])
    hot = bucket_rev[None, :] == jnp.arange(bucket_count, dtype=jnp.int32)[:, None]
    local_bias = lax.dynamic_slice_in_dim(rel_bias, h_at * heads, heads, 1)
    table = jnp.sum(jnp.where(hot[None], local_bias.T[:, :, None], 0.0), axis=1)
    table = jnp.concatenate([table, jnp.zeros((8 - heads, 2 * length), F32)], axis=0)
    seq_mask = lax.dynamic_index_in_dim(delete_mask, c_at, 0, keepdims=False)
    seq_len = lax.dynamic_index_in_dim(lengths, c_at, 0, keepdims=False)
    seq_mask = jnp.where(jnp.arange(length, dtype=jnp.int32) < seq_len, seq_mask, NEG)
    seq_mask = seq_mask.reshape(2, 2, block)
    seq_mask = jnp.where(h_at == 0, seq_mask, seq_mask[::-1])
    seq_mask = jnp.where(x_at == 0, seq_mask, seq_mask[:, ::-1])
    seq_mask = jnp.swapaxes(seq_mask, 0, 1).reshape(1, length)
    seq_mask = after(seq_mask, gate_other, up_other)
    bias = make_bias(starts, table, seq_mask, heads, block, 4, 2)

    kv_own_x = x_swap(kv_own, "kv_own_x")
    normed_far_raw = after(normed_far_raw, bias, kv_own)
    normed_far = after(normed_far_raw, down_other, kv_own_x)
    w_half = after(w_out, kv_own).reshape(2, inner // 2, width)
    w_half = lax.dynamic_index_in_dim(w_half, c_at, 0, keepdims=False)
    w_half = y_swap(after(w_half, normed_far_raw), "wout_y")
    dy_y = y_swap(after(dy_own, w_half), "dy_y")
    w_half_got = core_swap(w_half, "wout_core")
    q_far, kv_far = project(normed_far)
    kv_far_x = x_swap(kv_far, "kv_far_x")
    dy_x = x_swap(after(dy_own, kv_far_x), "dy_x")
    queries = jnp.concatenate([q_own, q_far], axis=1)
    kvs = (kv_own, kv_far, kv_own_x, kv_far_x)

    probs, mixed = attn_fwd(queries, kvs, bias, heads, block)
    mixed_far = y_swap(mixed[:, block:], "mixed_y")
    mixed_far = after(mixed_far, dy_x, dy_y)
    mixed_own = mixed[:, :block]
    residual, normed_two, inv_two = call(
        mid_kernel,
        (hbm((width, block), F32), sds((width, block), BF), sds((1, block), F32)),
        (x_rows, mixed_own, mixed_far, w_out, w_half, w_half_got, gain_two),
        "mid",
        vmem=20,
        scalars=(c_scalar,),
    )

    n_x = x_swap(normed_two, "n2_x")
    n_y = y_swap(normed_two, "n2_y")
    dy_d = relay(dy_x, dy_y, "dy_d")
    def d_act_of(dy):
        shape = sds((2, hidden, block), F32)
        return call(d_act_kernel, shape, (dy, down_weight, down_other), "d_act")

    da_own = d_act_of(dy_own)
    act_o, dg_o, du_o, dn_o = ffn_chunk(normed_two, da_own, ffn_weights, BF)
    da_x = d_act_of(dy_x)
    da_y = d_act_of(dy_y)
    n_d = relay(n_x, n_y, "n2_d")
    act_x, dg_x, du_x, dn_x = ffn_chunk(n_x, da_x, ffn_weights, BF)
    got_x = x_swap(dn_x, "dn_x")
    act_y, dg_y, du_y, dn_y = ffn_chunk(n_y, da_y, ffn_weights, BF)
    got_y = y_swap(dn_y, "dn_y")
    act_d, dg_d, du_d, dn_d = ffn_chunk(n_d, d_act_of(dy_d), ffn_weights, BF)
    got_d = grid_swap(dn_d, False, "dn_d")

    n_all = (normed_two, n_x, n_y, n_d)
    dy_all = (dy_own, dy_x, dy_y, dy_d)
    pieces = (
        ((act_o, act_x, act_y, act_d), dy_all),
        ((dg_o, dg_x, dg_y, dg_d), n_all),
        ((du_o, du_x, du_y, du_d), n_all),
    )
    given_d = core_swap(wgrad_give(pieces[:1]), "wgrad_core")
    out_o = ffn_out(act_o, down_weight, down_other, BF)
    mids, rows = pieces[1]
    gated = (((after(mids[0], got_x, got_y), *mids[1:]), rows), pieces[2])
    given_gu = core_swap(wgrad_give(gated), "wgrad_core")
    part_x = ffn_out(act_x, down_weight, down_other, BF)
    part_y = ffn_out(act_y, down_weight, down_other, BF)
    part_d = ffn_out(act_d, down_weight, down_other, BF)
    shares = dp_axis if dp_axis <= 8 else 1
    ffn_grads = wgrad_sum(pieces, (given_d, given_gu), shares)
    if shares > 1:
        ffn_grads = lax.psum_scatter(ffn_grads, "dp", scatter_dimension=0, tiled=True)
    else:
        ffn_grads = lax.psum(ffn_grads, "dp")


    d_residual, d_branch, gain_ffn_part, d_mixed_own, d_mixed_give = call(
        mid_back_kernel,
        (
            hbm((width, block), F32),
            sds((width, block), BF),
            sds((1, width), F32),
            sds((inner, block), BF),
            sds((inner, block), BF),
        ),
        (*map(in_hbm, (dn_o, got_x, got_y, got_d, dy_own, residual)), inv_two, gain_two, w_out, w_half, w_half_got),
        "mid_back",
        vmem=24,
        scalars=(c_scalar,),
    )
    d_mixed = jnp.concatenate([d_mixed_own, y_swap(d_mixed_give, "dmixed_y")], axis=1)

    dq, dkv_own, dkv_give, col, table_grad = attn_bwd(
        starts, probs, queries, d_mixed, kvs, heads, block
    )
    dkv_got = x_swap(dkv_give, "dkv_x")
    out_x = in_hbm(x_swap(after(part_x, got_d), "out_x"))
    out_y = in_hbm(y_swap(after(part_y, got_d), "out_y"))
    d_branch = after(d_branch, dq)
    grad_out_own, grad_out_give = call(
        out_grad_kernel,
        (hbm((inner, width), F32), hbm((inner, width), BF)),
        (mixed_own, mixed_far, d_branch),
        "out_grad",
        vmem=20,
    )
    grad_out_got = y_swap(grad_out_give, "gout_y")
    dkv_got = after(dkv_got, out_x, out_y)
    table_grad = sum(jnp.roll(table_grad[:, i], -i, axis=1) for i in range(8))
    grad_rel = jnp.sum(jnp.where(hot[None], table_grad[:, None, :], 0.0), axis=2).T
    grad_rel = lax.dynamic_update_slice_in_dim(
        jnp.zeros((bucket_count, total_heads), F32), grad_rel, h_at * heads, 1
    )
    d_kv, back_own, back_give, small = call(
        kv_sum_kernel,
        (
            sds((2 * inner, 2 * block), BF),
            hbm((width, block), F32),
            hbm((width + 2 * EXTRA, block), BF),
            sds((EXTRA, block), F32),
        ),
        (
            *map(in_hbm, (dkv_own, dkv_got)), col,
            dq, *map(in_hbm, (normed_one, normed_far)), wq, wk, wv,
            gain_one, gain_ffn_part, grad_rel.reshape(1, -1),
        ),
        "kv_sum",
        vmem=24,
    )
    back_got = y_swap(back_give, "back_y")

    pair_f32, pair_bf = sds((2, inner, width), F32), sds((2, inner, width), BF)
    one_f32, one_bf = sds((inner, width), F32), sds((inner, width), BF)
    keep, give = call(
        fold_core_kernel,
        (hbm(pair_f32.shape, F32), hbm(pair_bf.shape, BF)),
        (dq, d_kv, *map(in_hbm, (normed_one, normed_far, grad_out_own, grad_out_got))),
        "fold_core",
        scalars=(c_scalar,),
        vmem=28,
    )
    keep, give = call(
        fold_x_kernel,
        (one_f32, one_bf),
        (in_hbm(keep), in_hbm(core_swap(give, "fold_core"))),
        "fold_x",
        vmem=20,
        scalars=(x_scalar,),
    )
    got = x_swap(give, "fold_x")
    steps = [1 << k for k in range(dp_axis.bit_length() - 1)]
    short = shares > 1 and 1 << len(steps) == dp_axis
    if short:
        keep, got = z_share(after(keep, back_got), got, steps[0], dp_axis, z_at)
    if shares > 1:
        ffn_grads = lax.all_gather(after(ffn_grads, keep), "dp", axis=0, tiled=True)
    rows_keep, rows_give, small, _ = call(
        last_kernel,
        (
            sds((width, row_count), F32),
            sds((width + 2 * EXTRA, row_count), F32),
            sds((2 * EXTRA, row_count), F32),
            sds((width + EXTRA, block), F32),
        ),
        (in_hbm(back_own), in_hbm(back_got), small, in_hbm(x_rows), inv_one, gain_one, in_hbm(d_residual)),
        "last",
        vmem=24,
        scalars=(c_scalar,),
    )
    rows_got = core_swap(rows_give, "grad_core")
    small_got = rows_got[width:]
    if short:
        for step in steps[1:]:
            keep, got = z_share(keep, got, step, dp_axis, z_at)
        folded = z_join(keep, got, small, small_got, dp_axis, z_scalar)
    else:
        folded = z_psum(keep, got, small, small_got)

    part_d = after(part_d, rows_keep)
    out_d = grid_swap(part_d, False, "out_d")
    out_keep, out_give, _ = call(
        out_rows_kernel,
        (
            sds((width, row_count), BF),
            sds((width, row_count), BF),
            sds((width, block), BF),
        ),
        tuple(map(in_hbm, (residual, out_o, out_x, out_y, out_d))),
        "out_rows",
        vmem=24,
        scalars=(c_scalar,),
    )

    joined = x_swap(folded, "join_x")
    grad_inputs = place(rows_keep, rows_got)
    output = place(out_keep, core_swap(out_give, "out_core"))
    folded, sums = call(
        join_x_kernel,
        (pair_bf, sds((8, width), F32)),
        (folded, joined),
        "join_x",
        scalars=(x_scalar,),
    )
    joined = core_swap(folded, "join_core")
    grad_w_query, grad_w_key, grad_w_value, grad_w_out = call(
        join_core_kernel,
        (one_f32,) * 4,
        (folded, joined),
        "join_core",
        scalars=(c_scalar,),
    )
    mask_keep, mask_got = small[:1], small_got[:1]
    grad_mask = jnp.where(c_at == 0, stack(mask_keep, mask_got), stack(mask_got, mask_keep))
    grad_down, grad_gate, grad_up = widen(ffn_grads, hidden // shares, width)
    return (
        jnp.swapaxes(output, 1, 2),
        jnp.swapaxes(grad_inputs, 1, 2),
        grad_mask,
        sums[0],
        grad_w_query.T,
        grad_w_key.T,
        grad_w_value.T,
        grad_w_out,
        sums[2, : bucket_count * total_heads].reshape(bucket_count, total_heads),
        sums[1],
        grad_gate.T,
        grad_up.T,
        grad_down,
    )


def z_swap(v, step, n, name):
    return move(v, "dp", [(i, i ^ step) for i in range(n)], name)


def z_share(mine, got, step, n, z_at):
    bit = ((z_at // step) % 2).astype(jnp.int32).reshape(1)
    rows, width = mine.shape
    half = (rows // 2, width)
    mine, give, _ = call(
        share_kernel,
        (sds(half, F32), sds(half, BF), sds((rows, width), F32)),
        (mine, got),
        "share",
        scalars=(bit,),
    )
    return mine, z_swap(give, step, n, "share_z")


def z_join(mine, got, small, small_got, n, z_scalar):
    rows, width = mine.shape
    total = call(
        share_sum_kernel,
        sds((rows + EXTRA, width), BF),
        (mine, got, small, small_got),
        "share_sum",
    )
    gots = [
        move(total, "dp", [(i, (i + k) % n) for i in range(n)], "join_z") for k in range(1, n)
    ]
    joined, _ = call(
        share_join_kernel,
        (sds((n * rows + EXTRA, width), BF), sds((n, 8, width), F32)),
        (total, *gots),
        "share_join",
        scalars=(z_scalar,),
    )
    return joined


def z_psum(mine, got, small, small_got):
    width = mine.shape[1]
    total = lax.psum((mine + got.astype(F32)).astype(BF), "dp")
    small = lax.psum(small + small_got, "dp")
    half = small.shape[0] // 2

    def row(first):
        both = jnp.concatenate([small[first:half], small[half + first :]], axis=1)
        return both.reshape(1, -1)[:, :width]

    three = jnp.concatenate([row(2), row(8), row(1), jnp.zeros((5, width), F32)], axis=0)
    return jnp.concatenate([total, *split(three)], axis=0)


def solution(mesh):
    rows = P("dp", ("head", "hid"), None)
    return jax.shard_map(
        per_device,
        mesh=mesh,
        in_specs=(
            rows,
            P("dp"),
            P("dp", None),
            P(),
            P(),
            P(None, "head"),
            P(None, "head"),
            P(None, "head"),
            P("head", None),
            P(),
            P(),
            P(None, ("head", "hid")),
            P(None, ("head", "hid")),
            P(("head", "hid"), None),
            rows,
        ),
        out_specs=(
            rows,
            rows,
            P("dp", ("head", "hid")),
            P(),
            P(None, "head"),
            P(None, "head"),
            P(None, "head"),
            P("head", None),
            P(),
            P(),
            P(None, ("head", "hid")),
            P(None, ("head", "hid")),
            P(("head", "hid"), None),
        ),
        check_vma=False,
    )
```
